32 devices in a mesh: items: 4 (over x, core), rows: 8 (over z, y).
Axes of the slice: x: 2, y: 2, z: 4, core: 2. Of those that a mesh axis runs over, the one named last changes fastest.
Arguments:
- tokens: bfloat16 [16384, 768], P(('items', 'rows')), may hold values from -6 to 6
- query_proj: bfloat16 [768, 768], P(('items', 'rows')), may hold values from -0.21875 to 0.21875
- key_proj: bfloat16 [768, 768], P(('items', 'rows')), may hold values from -0.21875 to 0.21875
- value_proj: bfloat16 [768, 768], P(('items', 'rows')), may hold values from -0.21875 to 0.21875
- query_bias: bfloat16 [768], P(('items', 'rows')), may hold values from -1.5 to 1.5
- value_bias: bfloat16 [768], P(('items', 'rows')), may hold values from -0.25 to 0.25
- output_proj: bfloat16 [768, 768], P(('items', 'rows')), may hold values from -0.875 to 0.875
- output_bias: bfloat16 [768], P(('items', 'rows')), may hold values from -1 to 1
- attn_gain: bfloat16 [768], P(('items', 'rows')), may hold values from 0.099609375 to 1.8984375
- attn_shift: bfloat16 [768], P(('items', 'rows')), may hold values from -1 to 1
- hidden_proj: bfloat16 [768, 3072], P(('items', 'rows')), may hold values from -0.21875 to 0.21875
- hidden_bias: bfloat16 [3072], P(('items', 'rows')), may hold values from -1 to 1
- return_proj: bfloat16 [3072, 768], P(('items', 'rows')), may hold values from -0.109375 to 0.109375
- return_bias: bfloat16 [768], P(('items', 'rows')), may hold values from -1 to 1
- final_gain: bfloat16 [768], P(('items', 'rows')), may hold values from 0.099609375 to 1.8984375
- final_shift: bfloat16 [768], P(('items', 'rows')), may hold values from -2.5 to 2.5
- item_lengths: int32 [4, 8], P('items'), may hold values from 1 to 1024, 4096 in all within a row
- out_grad: bfloat16 [16384, 768], P(('items', 'rows')), may hold values from -6 to 6
Outputs:
- layer_out: bfloat16 [16384, 768], P(('items', 'rows'))
- tokens_grad: float32 [16384, 768], P(('items', 'rows'))
- grad_query_proj: float32 [768, 768], P(('items', 'rows'))
- grad_key_proj: float32 [768, 768], P(('items', 'rows'))
- grad_value_proj: float32 [768, 768], P(('items', 'rows'))
- grad_query_bias: float32 [768], P(('items', 'rows'))
- grad_value_bias: float32 [768], P(('items', 'rows'))
- grad_output_proj: float32 [768, 768], P(('items', 'rows'))
- grad_output_bias: float32 [768], P(('items', 'rows'))
- grad_attn_gain: float32 [768], P(('items', 'rows'))
- grad_attn_shift: float32 [768], P(('items', 'rows'))
- grad_hidden_proj: float32 [768, 3072], P(('items', 'rows'))
- grad_hidden_bias: float32 [3072], P(('items', 'rows'))
- grad_return_proj: float32 [3072, 768], P(('items', 'rows'))
- grad_return_bias: float32 [768], P(('items', 'rows'))
- grad_final_gain: float32 [768], P(('items', 'rows'))
- grad_final_shift: float32 [768], P(('items', 'rows'))
The draws below stay inside these ranges and needn't reach their ends.
Inputs may be any that keep to these rules, and one draw needn't show every extreme that they name: `item_lengths`: each row lists the lengths of its group's 8 items in stream order and sums to 4096; in each row one item has exactly 1024 tokens.
All inputs are finite; a program needn't handle non-finite values.
Results may differ from the reference program's by a relative error of at most 0.014.
Values may be sent and summed in bfloat16 or wider, within the bound.
A program may use at most 192 MiB of HBM per device.

```python
import math
import jax
import jax.numpy as jnp
import numpy as np
from jax import lax

D = 768
H = 12
HEAD = 64
FF = 3072
TOK_DEV = 512
MAXLEN = 1024
GROUP_TOK = 4096
ITEMS_G = 8
TOKENS = 16384
N_ITEMS = 4


def level_of(rng, extent, cuts, least, top_value):
    def one(position, parts):
        heights = jax.random.uniform(jax.random.fold_in(jax.random.fold_in(rng, 6), position), (parts,), jnp.float32, least / len(cuts), top_value / len(cuts))
        return jnp.repeat(jnp.exp(heights), extent[position] // parts).reshape((-1,) + (1,) * (len(extent) - position - 1))

    loudness = one(*cuts[0])
    for cut in cuts[1:]:
        loudness = loudness * one(*cut)
    return loudness


def profile(count, total, bound, slope):
    weights = [(1 << 20) // math.isqrt(rank ** slope) + 1 for rank in range(2, count + 1)]
    rest, holding = total - bound - (count - 1), [1] * (count - 1)
    while rest > 0:
        movable = [i for i in range(count - 1) if holding[i] < bound]
        whole, budget = sum([weights[i] for i in movable]), rest
        for i in movable:
            more = min(bound - holding[i], max(1, budget * weights[i] // whole), rest)
            holding[i] = holding[i] + more
            rest = rest - more
    return np.array([bound] + holding)


def ragged(stream_key, number_of, total, bound, slope):
    if number_of == 2:
        one = jax.random.randint(stream_key, (), max(1, total - bound), min(bound, total - 1) + 1)
        return jnp.stack([one, total - one])
    tallies = jnp.asarray(profile(number_of, total, bound, slope), jnp.int32)
    twos = (number_of - 1) // 2
    giver, sink = tallies[1:1 + 2 * twos:2], tallies[2:2 + 2 * twos:2]
    slack = jnp.minimum(giver - 1, bound - sink)
    passed = jax.random.randint(jax.random.fold_in(stream_key, 1), (twos,), 0, 1 << 20) % (slack + 1)
    tallies = tallies.at[1:1 + 2 * twos:2].set(giver - passed).at[2:2 + 2 * twos:2].set(sink + passed)
    return tallies[jax.random.permutation(jax.random.fold_in(stream_key, 2), number_of)]


def noise(rng, shape, deviation, most, split=(), kind=jnp.bfloat16):
    factor_of = level_of(rng, shape, split, -0.22, 0.18) if split else 1.0
    entries = jax.random.normal(rng, shape, jnp.float32) * deviation * factor_of
    return jnp.minimum(jnp.maximum(entries, -most), most).astype(kind)


def setup_inputs(seed: int = 0) -> dict:
    streams_of = jax.random.split(jax.random.key(seed), 19)
    tokens = noise(streams_of[0], (TOKENS, D), 1.0, 6.0, ((0, 32),))
    query_proj = noise(streams_of[1], (D, D), D ** -0.5, 0.21875, ((0, 32),))
    key_proj = noise(streams_of[2], (D, D), D ** -0.5, 0.21875, ((0, 32),))
    value_proj = noise(streams_of[3], (D, D), D ** -0.5, 0.21875, ((0, 32),))
    query_bias = noise(streams_of[4], (D,), 0.3, 1.5, ((0, 32),))
    value_bias = noise(streams_of[5], (D,), 0.05, 0.25, ((0, 32),))
    output_proj = noise(streams_of[6], (D, D), (D // 16) ** -0.5, 0.875, ((0, 32),))
    output_bias = noise(streams_of[7], (D,), 0.2, 1.0, ((0, 32),))
    attn_gain = jnp.clip(1.0 + 0.18 * jax.random.normal(streams_of[8], (D,), jnp.float32), 0.099609375, 1.8984375).astype(jnp.bfloat16)
    attn_shift = noise(streams_of[9], (D,), 0.2, 1.0, ((0, 32),))
    hidden_proj = noise(streams_of[10], (D, FF), D ** -0.5, 0.21875, ((0, 32),))
    hidden_bias = noise(streams_of[11], (FF,), 0.2, 1.0, ((0, 32),))
    return_proj = noise(streams_of[12], (FF, D), FF ** -0.5, 0.109375, ((0, 32),))
    return_bias = noise(streams_of[13], (D,), 0.2, 1.0, ((0, 32),))
    final_gain = jnp.clip(1.0 + 0.18 * jax.random.normal(streams_of[14], (D,), jnp.float32), 0.099609375, 1.8984375).astype(jnp.bfloat16)
    final_shift = noise(streams_of[15], (D,), 0.5, 2.5, ((0, 32),))
    item_lengths = jax.vmap(lambda own: ragged(own, ITEMS_G, GROUP_TOK, MAXLEN, 2))(jax.random.split(streams_of[16], N_ITEMS)).reshape((N_ITEMS, ITEMS_G)).astype(jnp.int32)
    out_grad = noise(streams_of[17], (TOKENS, D), 1.0, 6.0, ((0, 32),))
    return dict(tokens=tokens, query_proj=query_proj, key_proj=key_proj, value_proj=value_proj, query_bias=query_bias, value_bias=value_bias, output_proj=output_proj, output_bias=output_bias, attn_gain=attn_gain, attn_shift=attn_shift, hidden_proj=hidden_proj, hidden_bias=hidden_bias, return_proj=return_proj, return_bias=return_bias, final_gain=final_gain, final_shift=final_shift, item_lengths=item_lengths, out_grad=out_grad)


@jax.custom_vjp
def low(v):
    return lax.optimization_barrier(v.astype(jnp.bfloat16)).astype(jnp.float32)

@jax.custom_vjp
def low_back(v):
    return v

def low_keep(v):
    return (low(v), None)

def low_pass(kept, grad):
    return (grad,)

def back_keep(v):
    return (v, None)

def back_low(kept, grad):
    return (low(grad),)
low.defvjp(low_keep, low_pass)
low_back.defvjp(back_keep, back_low)
highest = lax.Precision.HIGHEST
eps_norm = 1e-06
masked_score = -1e+30

def product(matrix, factor):
    return jnp.dot(matrix, factor, precision=highest, preferred_element_type=jnp.float32)

def layer_norm(hidden, norm_gain, norm_shift):
    row_mean = lax.optimization_barrier(jnp.mean(hidden, axis=1, keepdims=True))
    centred = hidden - row_mean
    row_var = lax.optimization_barrier(jnp.mean(centred * centred, axis=1, keepdims=True))
    return centred * lax.rsqrt(row_var + eps_norm) * norm_gain + norm_shift

def segment_ids(row_lengths, first_row, num_rows):
    item_ends = jnp.cumsum(row_lengths, dtype=jnp.int32)
    places = first_row + jnp.arange(num_rows, dtype=jnp.int32)
    return lax.optimization_barrier(jnp.sum((places[:, None] >= item_ends[None, :]).astype(jnp.int32), axis=1, dtype=jnp.int32))

def attention(query_rows, key_rows, value_rows, labels):
    blocks = GROUP_TOK // TOK_DEV
    score_scale = HEAD ** (-0.5)
    query_all = query_rows.reshape(N_ITEMS, GROUP_TOK, H, HEAD)
    pad_width = ((0, 0), (MAXLEN, MAXLEN), (0, 0), (0, 0))
    keys_all = jnp.pad(key_rows.reshape(N_ITEMS, GROUP_TOK, H, HEAD), pad_width)
    values_all = jnp.pad(value_rows.reshape(N_ITEMS, GROUP_TOK, H, HEAD), pad_width)
    labels_all = jnp.pad(labels.reshape(N_ITEMS, GROUP_TOK), ((0, 0), (MAXLEN, MAXLEN)), constant_values=-1)

    def one_block(block_index):
        group_index = (block_index // blocks).astype(jnp.int32)
        first_row = (block_index % blocks * TOK_DEV).astype(jnp.int32)
        anchor = jnp.zeros((), jnp.int32)
        block_query = lax.dynamic_slice(query_all, (group_index, first_row, anchor, anchor), (1, TOK_DEV, H, HEAD))[0]
        block_keys = lax.dynamic_slice(keys_all, (group_index, first_row, anchor, anchor), (1, TOK_DEV + 2 * MAXLEN, H, HEAD))[0]
        block_values = lax.dynamic_slice(values_all, (group_index, first_row, anchor, anchor), (1, TOK_DEV + 2 * MAXLEN, H, HEAD))[0]
        query_labels = lax.dynamic_slice(labels_all, (group_index, first_row + MAXLEN), (1, TOK_DEV))[0]
        key_labels = lax.dynamic_slice(labels_all, (group_index, first_row), (1, TOK_DEV + 2 * MAXLEN))[0]
        scores = jnp.einsum('qhd,khd->hqk', block_query, block_keys, precision=highest) * score_scale
        scores = low_back(scores)
        allowed = query_labels[:, None] == key_labels[None, :]
        scores = jnp.where(allowed[None], scores, masked_score)
        row_max = lax.optimization_barrier(jnp.max(scores, axis=2, keepdims=True))
        lifted = jnp.exp(scores - row_max)
        weights = lifted / lax.optimization_barrier(jnp.sum(lifted, axis=2, keepdims=True))
        outputs = jnp.einsum('hqk,khd->qhd', low(weights), block_values, precision=highest)
        return outputs.reshape(TOK_DEV, H * HEAD)
    results = lax.map(jax.checkpoint(one_block), jnp.arange(N_ITEMS * blocks, dtype=jnp.int32))
    return results.reshape(N_ITEMS * GROUP_TOK, H * HEAD)

def forward(tokens, query_proj, key_proj, value_proj, query_bias, value_bias, output_proj, output_bias, attn_gain, attn_shift, hidden_proj, hidden_bias, return_proj, return_bias, final_gain, final_shift, labels):
    query_rows = low_back(low(product(tokens, query_proj) + query_bias))
    key_rows = low_back(low(product(tokens, key_proj)))
    value_rows = low_back(low(product(tokens, value_proj) + value_bias))
    attended = low_back(low(attention(query_rows, key_rows, value_rows, labels)))
    branch = low_back(product(attended, output_proj) + output_bias)
    normed = layer_norm(tokens + branch, attn_gain, attn_shift)
    hidden_pre = low_back(product(low(normed), hidden_proj) + hidden_bias)
    active = low(jax.nn.gelu(hidden_pre, approximate=False))
    ffn_out = low_back(product(active, return_proj) + return_bias)
    return layer_norm(normed + ffn_out, final_gain, final_shift)

def reference(tokens, query_proj, key_proj, value_proj, query_bias, value_bias, output_proj, output_bias, attn_gain, attn_shift, hidden_proj, hidden_bias, return_proj, return_bias, final_gain, final_shift, item_lengths, out_grad):
    labels = jax.vmap(lambda lengths_row: segment_ids(lengths_row, jnp.zeros((), jnp.int32), GROUP_TOK))(item_lengths).reshape(-1)
    floats = tuple((array.astype(jnp.float32) for array in (tokens, query_proj, key_proj, value_proj, query_bias, value_bias, output_proj, output_bias, attn_gain, attn_shift, hidden_proj, hidden_bias, return_proj, return_bias, final_gain, final_shift)))

    def wrapped(*values):
        return forward(*values, labels)
    result, pullback = jax.vjp(wrapped, *floats)
    gradients = pullback(out_grad.astype(jnp.float32))
    return (result.astype(jnp.bfloat16), gradients[0], gradients[1], gradients[2], gradients[3], gradients[4], gradients[5], gradients[6], gradients[7], gradients[8], gradients[9], gradients[10], gradients[11], gradients[12], gradients[13], gradients[14], gradients[15])
```

```python
import functools
import jax
import jax.numpy as jnp
from jax import lax
from jax.experimental import pallas as pl
from jax.experimental.pallas import tpu as pltpu

from jax.sharding import PartitionSpec as P

MESH = pl.DeviceIdType.MESH
REACH = 2


def split_rows(rows):
    inner = 1
    while (2 * inner) ** 2 <= rows:
        inner *= 2
    return rows // inner, inner


def place(nz, ny):
    item, row = lax.axis_index("items"), lax.axis_index("rows")
    return item // 2, item % 2, row // ny, row % ny


def near(z, step, nz):
    way = 1 - 2 * (z // ((nz + 1) // 2))
    return lax.rem(z + way * step + nz * 2, nz)


def gather_kernel(na, nz, ny, count, *refs):
    tokens = refs[0]
    mine = refs[1 : 1 + count]
    window = refs[1 + count]
    full = refs[2 + count : 2 + 2 * count]
    (halo_send, halo_recv, local_sem, s1, r1, s2, r2, s3, r3, s4, r4) = refs[2 + 2 * count :]
    a, c, z, y = place(nz, ny)
    rows = nz * ny
    row = z * ny + y
    item = a * 2 + c

    def slot(a_, z_, y_):
        return (a_ * 2 + c) * rows + z_ * ny + y_

    barrier = pltpu.get_barrier_semaphore()

    def greet(i_, r_):
        pl.semaphore_signal(barrier, inc=1, device_id=(i_, r_), device_id_type=MESH)

    for d in range(1, nz):
        greet(item, near(z, d, nz) * ny + y)
    for d in range(1, ny):
        greet(item, z * ny + lax.rem(y + d, ny))
    for d in range(1, na):
        greet(lax.rem(a + d, na) * 2 + c, row)
    greet(a * 2 + 1 - c, row)
    for d in range(-REACH, REACH + 1):
        if d != 0:
            greet(item, lax.rem(row + d + rows, rows))
    pl.semaphore_wait(barrier, nz + ny + na - 2 + 2 * REACH)

    def remote(src, dst, send, recv, i_, r_):
        return pltpu.make_async_remote_copy(
            src_ref=src, dst_ref=dst, send_sem=send, recv_sem=recv, device_id=(i_, r_), device_id_type=MESH
        )

    locals_ = []
    for n in range(count):
        locals_.append(pltpu.make_async_copy(mine[n], full[n].at[slot(a, z, y)], local_sem.at[n]))
        locals_[-1].start()
    locals_.append(pltpu.make_async_copy(tokens, window.at[REACH], local_sem.at[count]))
    locals_[-1].start()

    for d in range(1, nz):
        zz = near(z, d, nz)
        for n in range(count):
            remote(mine[n], full[n].at[slot(a, z, y)], s1.at[d, n], r1.at[z, n], item, zz * ny + y).start()

    def wait1(zz, n):
        part = full[n].at[slot(a, zz, y)]
        remote(part, part, s1.at[0, n], r1.at[zz, n], item, row).wait_recv()

    def halo(d, start):
        k = d + REACH

        @pl.when((row + d >= 0) & (row + d < rows))
        def _():
            copy = remote(tokens, window.at[REACH - d], halo_send.at[k], halo_recv.at[REACH - d], item, row + d)
            if start:
                copy.start()
            else:
                copy.wait_send()
                part = window.at[k]
                remote(part, part, halo_send.at[k], halo_recv.at[k], item, row).wait_recv()

        @pl.when((row + d < 0) | (row + d >= rows))
        def _():
            copy = pltpu.make_async_copy(tokens, window.at[k], halo_recv.at[k])
            if start:
                copy.start()
            else:
                copy.wait()

    @pl.when(c == 0)
    def _():
        def second(step):
            zz = near(z, step, nz)
            for n in range(count):
                if step:
                    wait1(zz, n)
                for d in range(1, ny):
                    src = full[n].at[slot(a, zz, y)] if step else mine[n]
                    remote(src, full[n].at[slot(a, zz, y)], s2.at[step, d, n], r2.at[zz, y, n], item, z * ny + lax.rem(y + d, ny)).start()

        def third(step):
            zz = near(z, step, nz)
            for n in range(count):
                for d in range(1, ny):
                    yy = lax.rem(y + d, ny)
                    part = full[n].at[slot(a, zz, yy)]
                    remote(part, part, s2.at[step, 0, n], r2.at[zz, yy, n], item, row).wait_recv()
                if step == 0:
                    locals_[n].wait()
                block = full[n].at[pl.ds(slot(a, zz, 0), ny)]
                for d in range(1, na):
                    remote(block, block, s3.at[step, d, 0, n], r3.at[zz, a, 0, n], lax.rem(a + d, na) * 2 + c, row).start()

        def fourth(step):
            zz = near(z, step, nz)
            for e in range(na):
                aa = lax.rem(a + e, na)
                for n in range(count):
                    block = full[n].at[pl.ds(slot(aa, zz, 0), ny)]
                    if e:
                        remote(block, block, s3.at[step, 0, 0, n], r3.at[zz, aa, 0, n], item, row).wait_recv()
                    remote(block, block, s4.at[e, step, n], r4.at[aa, zz, n], a * 2 + 1 - c, row).start()

        for t in range(nz + 2):
            if t < nz:
                second(t)
            if t == 0:
                for d in (1, -1, 2, -2):
                    halo(d, True)
            if 0 <= t - 1 < nz:
                third(t - 1)
            if 0 <= t - 2 < nz:
                fourth(t - 2)
        for n in range(count):
            for step in range(nz):
                for d in range(1, ny):
                    part = full[n].at[slot(a, z, y)]
                    remote(part, part, s2.at[step, d, n], r2.at[z, y, n], item, row).wait_send()
                for d in range(1, na):
                    part = full[n].at[pl.ds(slot(a, z, 0), ny)]
                    remote(part, part, s3.at[step, d, 0, n], r3.at[z, a, 0, n], item, row).wait_send()

    @pl.when(c == 1)
    def _():
        def second(step):
            zz = near(z, step, nz)
            for n in range(count):
                if step:
                    wait1(zz, n)
                for d in range(1, na):
                    src = full[n].at[slot(a, zz, y)] if step else mine[n]
                    remote(src, full[n].at[slot(a, zz, y)], s2.at[step, d, n], r2.at[zz, a, n], lax.rem(a + d, na) * 2 + c, row).start()

        def third(step):
            zz = near(z, step, nz)
            for e in range(na):
                aa = lax.rem(a + e, na)
                for n in range(count):
                    part = full[n].at[slot(aa, zz, y)]
                    if e:
                        remote(part, part, s2.at[step, 0, n], r2.at[zz, aa, n], item, row).wait_recv()
                    if e == 0 and step == 0:
                        locals_[n].wait()
                    for d in range(1, ny):
                        remote(part, part, s3.at[step, e, d, n], r3.at[zz, aa, y, n], item, z * ny + lax.rem(y + d, ny)).start()

        def fourth(step):
            zz = near(z, step, nz)
            for e in range(na):
                aa = lax.rem(a + e, na)
                for n in range(count):
                    for d in range(1, ny):
                        yy = lax.rem(y + d, ny)
                        part = full[n].at[slot(aa, zz, yy)]
                        remote(part, part, s3.at[step, e, 0, n], r3.at[zz, aa, yy, n], item, row).wait_recv()
                    block = full[n].at[pl.ds(slot(aa, zz, 0), ny)]
                    remote(block, block, s4.at[e, step, n], r4.at[aa, zz, n], a * 2 + 1 - c, row).start()

        for t in range(nz + 2):
            if t < nz:
                second(t)
            if t == 0:
                for d in (1, -1, 2, -2):
                    halo(d, True)
            if 0 <= t - 1 < nz:
                third(t - 1)
            if 0 <= t - 2 < nz:
                fourth(t - 2)
        for n in range(count):
            for step in range(nz):
                part = full[n].at[slot(a, z, y)]
                for d in range(1, na):
                    remote(part, part, s2.at[step, d, n], r2.at[z, a, n], item, row).wait_send()
                for e in range(na):
                    for d in range(1, ny):
                        remote(part, part, s3.at[step, e, d, n], r3.at[z, a, y, n], item, row).wait_send()

    other = 1 - 2 * c
    for n in range(count):
        for d in range(1, nz):
            remote(mine[n], full[n].at[slot(a, z, y)], s1.at[d, n], r1.at[z, n], item, row).wait_send()
        for e in range(na):
            for step in range(nz):
                mineb = full[n].at[pl.ds(slot(a, z, 0), ny)]
                remote(mineb, mineb, s4.at[e, step, n], r4.at[0, 0, n], item, row).wait_send()
                theirs = full[n].at[pl.ds((e * 2 + 1 - c) * rows + step * ny, ny)]
                remote(theirs, theirs, s4.at[e, step, n], r4.at[e, step, n], item, row).wait_recv()
    for d in (1, -1, 2, -2):
        halo(d, False)
    locals_[count].wait()


def gather_all(mesh_shape, tokens, shards):
    na = mesh_shape["items"] // 2
    nz, ny = split_rows(mesh_shape["rows"])
    ndev = mesh_shape["items"] * mesh_shape["rows"]
    count = len(shards)
    nm = max(na, ny)
    dma = pltpu.SemaphoreType.DMA
    out_shape = [jax.ShapeDtypeStruct((2 * REACH + 1,) + tokens.shape, tokens.dtype)] + [
        jax.ShapeDtypeStruct((ndev,) + s.shape, s.dtype) for s in shards
    ]
    return pl.pallas_call(
        functools.partial(gather_kernel, na, nz, ny, count),
        out_shape=out_shape,
        in_specs=[pl.BlockSpec(memory_space=pltpu.VMEM)] * (1 + count),
        out_specs=[pl.BlockSpec(memory_space=pl.ANY)] * (1 + count),
        scratch_shapes=[
            dma((2 * REACH + 1,)), dma((2 * REACH + 1,)), dma((count + 1,)),
            dma((nz, count)), dma((nz, count)),
            dma((nz, nm, count)), dma((nz, nm, count)),
            dma((nz, na, ny, count)), dma((nz, na, ny, count)),
            dma((na, nz, count)), dma((na, nz, count)),
        ],
        compiler_params=pltpu.CompilerParams(collective_id=1, has_side_effects=True),
        name="gather_weights",
    )(tokens, *shards)


def scatter_kernel(na, nz, ny, plan, *refs):
    inputs = max(p[0] for p in plan) + 1
    given = refs[:inputs]
    outs = refs[inputs : 2 * inputs]
    scratch = refs[2 * inputs :]
    groups = (len(scratch) - 9) // 5
    bufs = [scratch[5 * g : 5 * g + 5] for g in range(groups)]
    load_sem, s0, r0, s1, r1, s2, r2, s3, r3 = scratch[5 * groups :]
    a, c, z, y = place(nz, ny)
    rows = nz * ny
    row = z * ny + y
    item = a * 2 + c

    barrier = pltpu.get_barrier_semaphore()

    def greet(i_, r_):
        pl.semaphore_signal(barrier, inc=1, device_id=(i_, r_), device_id_type=MESH)

    def at_z(d):
        return lax.rem(z + d, nz) * ny + y

    def at_y(d):
        return z * ny + lax.rem(y + d, ny)

    def at_a(d):
        return lax.rem(a + d, na) * 2 + c

    for d in range(1, nz):
        greet(item, at_z(d))
    for d in range(1, ny):
        greet(item, at_y(d))
    for d in range(1, na):
        greet(at_a(d), row)
    greet(a * 2 + 1 - c, row)
    pl.semaphore_wait(barrier, nz + ny + na - 2)

    def remote(src, dst, send, recv, i_, r_):
        return pltpu.make_async_remote_copy(
            src_ref=src, dst_ref=dst, send_sem=send, recv_sem=recv, device_id=(i_, r_), device_id_type=MESH
        )

    order, seen = [], {}
    for p in plan:
        order.append(seen.get(p[3], 0))
        seen[p[3]] = order[-1] + 1

    def buf(k, which):
        return bufs[plan[k][3]][which].at[order[k]]

    def source(k, item_, zz):
        ref, (number, first, column, group) = given[plan[k][0]], plan[k]
        height, width = bufs[group][0].shape[-2:]
        return ref.at[pl.ds(item_ * rows + zz * ny, ny), pl.ds(first, height), pl.ds(column, width)]

    def load(k, aa, zz):
        return pltpu.make_async_copy(source(k, aa * 2 + c, zz), buf(k, 0).at[aa, zz], load_sem.at[k, aa, zz])

    def core(k, aa, zz):
        return remote(
            source(k, aa * 2 + 1 - c, zz), buf(k, 1).at[aa, zz], s0.at[k, aa, zz], r0.at[k, aa, zz], a * 2 + 1 - c, row
        )

    def first0(k, d, zz):
        aa = lax.rem(a + d, na)
        return remote(
            buf(k, 0).at[aa, zz], buf(k, 2).at[pl.ds((d - 1) * rows + zz * ny, ny)],
            s1.at[k, d, zz], r1.at[k, d, zz], at_a(d), row,
        )

    def first1(k, d, aa):
        return remote(
            buf(k, 0).at[aa, :, lax.rem(y + d, ny)], buf(k, 2).at[pl.ds((d - 1) * na * nz + aa * nz, nz)],
            s1.at[k, d, aa], r1.at[k, d, aa], item, at_y(d),
        )

    def second0(k, d):
        return remote(
            buf(k, 0).at[a, :, lax.rem(y + d, ny)], buf(k, 3).at[pl.ds((d - 1) * nz, nz)],
            s2.at[k, d], r2.at[k, d], item, at_y(d),
        )

    def second1(k, d):
        return remote(
            buf(k, 0).at[lax.rem(a + d, na), :, y], buf(k, 3).at[pl.ds((d - 1) * nz, nz)],
            s2.at[k, d], r2.at[k, d], at_a(d), row,
        )

    def third(k, d):
        return remote(
            buf(k, 0).at[a, lax.rem(z + d, nz), y], buf(k, 4).at[d - 1], s3.at[k, d], r3.at[k, d], item, at_z(d)
        )

    def summed(refs_):
        total = refs_[0][...].astype(jnp.float32)
        for ref in refs_[1:]:
            total = total + ref[...].astype(jnp.float32)
        return total

    def add_into(dst, parts):
        dst[...] = summed([dst] + parts).astype(dst.dtype)

    chunks = range(len(plan))
    for k in chunks:
        for e in range(na):
            for zz in range(nz):
                core(k, lax.rem(a + 1 + e, na), zz).start()
                load(k, lax.rem(a + 1 + e, na), zz).start()

    def stage1(k):
        for e in range(na):
            aa = lax.rem(a + 1 + e, na)
            for zz in range(nz):
                load(k, aa, zz).wait()
                core(k, aa, zz).wait_recv()

                @pl.loop(0, ny)
                def _(yy):
                    add_into(buf(k, 0).at[aa, zz, yy], [buf(k, 1).at[aa, zz, yy]])

                if e < na - 1:

                    @pl.when(c == 0)
                    def _():
                        first0(k, e + 1, zz).start()

        @pl.when(c == 1)
        def _():
            for d in range(1, ny):
                for aa in range(na):
                    first1(k, d, aa).start()

    def stage2(k):
        @pl.when(c == 0)
        def _():
            for zz in range(nz):
                for d in range(1, na):
                    first0(k, d, zz).wait_recv()

                @pl.loop(0, ny)
                def _(yy):
                    add_into(
                        buf(k, 0).at[a, zz, yy], [buf(k, 2).at[(d - 1) * rows + zz * ny + yy] for d in range(1, na)]
                    )

            for d in range(1, ny):
                second0(k, d).start()

        @pl.when(c == 1)
        def _():
            for e in range(na):
                for d in range(1, ny):
                    for aa in range(na):
                        if e == 0:
                            first1(k, d, aa).wait_recv()
                aa = lax.rem(a + 1 + e, na)

                @pl.loop(0, nz)
                def _(zz):
                    add_into(
                        buf(k, 0).at[aa, zz, y],
                        [buf(k, 2).at[(d - 1) * na * nz + aa * nz + zz] for d in range(1, ny)],
                    )

            for d in range(1, na):
                second1(k, d).start()

    def stage3(k):
        width = na if na > ny else ny
        for d in range(1, width):
            if d < ny and d < na:
                second0(k, d).wait_recv()
            elif d < ny:

                @pl.when(c == 0)
                def _():
                    second0(k, d).wait_recv()

            else:

                @pl.when(c == 1)
                def _():
                    second1(k, d).wait_recv()

        def add_second(peers):
            @pl.loop(0, nz)
            def _(zz):
                add_into(buf(k, 0).at[a, zz, y], [buf(k, 3).at[(d - 1) * nz + zz] for d in range(1, peers)])

        if na == ny:
            add_second(na)
        else:

            @pl.when(c == 0)
            def _():
                add_second(ny)

            @pl.when(c == 1)
            def _():
                add_second(na)

        for d in range(1, nz):
            third(k, d).start()

    def stage4(k):
        for d in range(1, nz):
            third(k, d).wait_recv()
        number, first, column, group = plan[k]
        height, width = bufs[group][0].shape[-2:]
        outs[number][first : first + height, column : column + width] = summed(
            [buf(k, 0).at[a, z, y]] + [buf(k, 4).at[d - 1] for d in range(1, nz)]
        )

    stages = (stage1, stage2, stage3, stage4)
    for t in range(len(plan) + 3):
        for n, stage in enumerate(stages):
            if 0 <= t - n < len(plan):
                stage(t - n)

    for k in chunks:
        for aa in range(na):
            for zz in range(nz):
                core(k, aa, zz).wait_send()
        for d in range(1, nz):
            third(k, d).wait_send()

        @pl.when(c == 0)
        def _():
            for d in range(1, na):
                for zz in range(nz):
                    first0(k, d, zz).wait_send()
            for d in range(1, ny):
                second0(k, d).wait_send()

        @pl.when(c == 1)
        def _():
            for d in range(1, ny):
                for aa in range(na):
                    first1(k, d, aa).wait_send()
            for d in range(1, na):
                second1(k, d).wait_send()


def scatter_all(mesh_shape, grads, pieces, collective_id=2):
    na = mesh_shape["items"] // 2
    nz, ny = split_rows(mesh_shape["rows"])
    plan, kinds, number = [], [], []
    for n, (g, (height, width)) in enumerate(zip(grads, pieces)):
        kind = (height, width, g.dtype)
        if kind not in kinds:
            kinds.append(kind)
            number.append(0)
        group = kinds.index(kind)
        for first in range(0, g.shape[1], height):
            for column in range(0, g.shape[2], width):
                plan.append((n, first, column, group))
                number[group] += 1
    scratch = []
    for (height, width, dtype), many in zip(kinds, number):
        one = (height, width)
        first = max((na - 1) * nz * ny, (ny - 1) * na * nz)
        second = (max(na, ny) - 1) * nz
        scratch += [
            pltpu.VMEM((many, na, nz, ny) + one, dtype),
            pltpu.VMEM((many, na, nz, ny) + one, dtype),
            pltpu.VMEM((many, first) + one, dtype),
            pltpu.VMEM((many, second) + one, dtype),
            pltpu.VMEM((many, nz - 1) + one, dtype),
        ]
    k = len(plan)
    dma = pltpu.SemaphoreType.DMA
    nm = max(na, ny)
    scratch += [dma((k, na, nz))] * 3 + [dma((k, nm, max(nz, na)))] * 2 + [dma((k, nm))] * 2 + [dma((k, nz))] * 2
    return pl.pallas_call(
        functools.partial(scatter_kernel, na, nz, ny, tuple(plan)),
        out_shape=[jax.ShapeDtypeStruct(g.shape[1:], jnp.float32) for g in grads],
        in_specs=[pl.BlockSpec(memory_space=pl.ANY)] * len(grads),
        out_specs=[pl.BlockSpec(memory_space=pltpu.VMEM)] * len(grads),
        scratch_shapes=scratch,
        compiler_params=pltpu.CompilerParams(
            collective_id=collective_id, has_side_effects=True, vmem_limit_bytes=60 << 20
        ),
        name="scatter_grads",
    )(*grads)


H = 12
HEAD = 64
PAIR = 2 * HEAD
MASKED = -1e30


def dot_last(x, y):
    return lax.dot_general(x, y, (((1,), (1,)), ((), ())), preferred_element_type=jnp.float32)


def dot_plain(x, y):
    return jnp.dot(x, y, preferred_element_type=jnp.float32)


def one_side(block, side, scale=1.0):
    lane = lax.broadcasted_iota(jnp.int32, (1, PAIR), 1)
    keep = (lane // HEAD == side).astype(jnp.float32) * scale
    return (block.astype(jnp.float32) * keep).astype(jnp.bfloat16)


def allowed_pairs(first, last, base, shape):
    place = lax.broadcasted_iota(jnp.int32, shape, 0)
    return (place >= first - base) & (place < last - base)


def skewed(count, *stages):
    held = [None] * count
    for t in range(count + len(stages) - 1):
        for k, stage in enumerate(stages):
            n = t - k
            if 0 <= n < count:
                held[n] = stage(n) if k == 0 else stage(n, held[n])
    return tuple(held)


def attend_kernel(tile, step, bounds, query, keys, values, first, last, low, full, logsum):
    pairs = query.shape[1] // PAIR
    for i in range(query.shape[0] // tile):
        rows = slice(i * tile, (i + 1) * tile)
        cols = [slice(p * PAIR, (p + 1) * PAIR) for p in range(pairs)]
        heads = [(c, s, one_side(query[rows, c], s, HEAD**-0.5)) for c in cols for s in range(2)]
        start_at, end_at = first[:, rows], last[:, rows]

        def body(j, carry):
            block = pl.ds(pl.multiple_of(j * step, step), step)
            allowed = allowed_pairs(start_at, end_at, j * step, (step, tile))
            turned = [values[block, c].T for c in cols]

            def score(n):
                c, s, q = heads[n]
                return jnp.where(allowed, dot_last(keys[block, c], q), MASKED)

            def soften(n, scores):
                top, total, acc = carry[n]
                peak = jnp.maximum(top, jnp.max(scores, axis=0, keepdims=True))
                lifted = jnp.exp(scores - peak)
                fade = jnp.exp(top - peak)
                return peak, total * fade + jnp.sum(lifted, axis=0, keepdims=True), fade, lifted.astype(jnp.bfloat16)

            def gather(n, soft):
                peak, total, fade, lifted = soft
                s = heads[n][1]
                return peak, total, carry[n][2] * fade + dot_plain(turned[n // 2][s * HEAD : (s + 1) * HEAD], lifted)

            return skewed(len(heads), score, soften, gather)

        start = tuple(
            (
                jnp.full((1, tile), MASKED, jnp.float32),
                jnp.zeros((1, tile), jnp.float32),
                jnp.zeros((HEAD, tile), jnp.float32),
            )
            for _ in heads
        )
        done = lax.fori_loop(bounds[0, i], bounds[1, i], body, start)
        for p, c in enumerate(cols):
            (top0, total0, acc0), (top1, total1, acc1) = done[2 * p : 2 * p + 2]
            result = jnp.concatenate([acc0 / total0, acc1 / total1], axis=0).T
            low[rows, c] = result.astype(jnp.bfloat16)
            full[rows, c] = result
            logsum[2 * p, :, rows] = top0 + jnp.log(total0)
            logsum[2 * p + 1, :, rows] = top1 + jnp.log(total1)


def columns(rows, group):
    return pl.BlockSpec((rows, group * HEAD), lambda p, b: (0, p))


def lines(length, group):
    return pl.BlockSpec((group, 1, length), lambda p, b: (p, 0, 0))


def whole(*shape):
    return pl.BlockSpec(shape, lambda p, b: (0,) * len(shape))


def cost(matmuls):
    return pl.CostEstimate(flops=matmuls * 2 * H * HEAD * 512 * 1536, bytes_accessed=12 << 20, transcendentals=0)


VMEM = pltpu.CompilerParams(vmem_limit_bytes=56 << 20)


def attend(bounds, query, keys, values, first, last, tile, step, group):
    tokens, width = query.shape
    wide = keys.shape[0]
    return pl.pallas_call(
        functools.partial(attend_kernel, tile, step),
        grid_spec=pltpu.PrefetchScalarGridSpec(
            num_scalar_prefetch=1,
            grid=(H // group,),
            in_specs=[columns(tokens, group), columns(wide, group), columns(wide, group)] + [whole(1, tokens)] * 2,
            out_specs=[columns(tokens, group), columns(tokens, group), lines(tokens, group)],
        ),
        out_shape=[
            jax.ShapeDtypeStruct((tokens, width), jnp.bfloat16),
            jax.ShapeDtypeStruct((tokens, width), jnp.float32),
            jax.ShapeDtypeStruct((H, 1, tokens), jnp.float32),
        ],
        compiler_params=VMEM,
        cost_estimate=cost(2),
        name="attend",
    )(bounds, query, keys, values, first, last)


def query_grad_kernel(tile, step, bounds, query, grad, keys, values, logsum, centre, first, last, out):
    pairs = query.shape[1] // PAIR
    for i in range(query.shape[0] // tile):
        rows = slice(i * tile, (i + 1) * tile)
        cols = [slice(p * PAIR, (p + 1) * PAIR) for p in range(pairs)]
        heads = [
            (
                c, s, one_side(query[rows, c], s, HEAD**-0.5), one_side(grad[rows, c], s),
                logsum[2 * p + s, :, rows], centre[2 * p + s, :, rows],
            )
            for p, c in enumerate(cols)
            for s in range(2)
        ]
        start_at, end_at = first[:, rows], last[:, rows]

        def body(j, carry):
            block = pl.ds(pl.multiple_of(j * step, step), step)
            allowed = allowed_pairs(start_at, end_at, j * step, (step, tile))
            turned = [keys[block, c].T for c in cols]

            def score(n):
                c, s, q, g, top, mid = heads[n]
                return dot_last(keys[block, c], q), dot_last(values[block, c], g)

            def soften(n, both):
                top, mid = heads[n][4:]
                weights = jnp.exp(jnp.where(allowed, both[0] - top, MASKED))
                return (weights * (both[1] - mid)).astype(jnp.bfloat16)

            def gather(n, d_scores):
                s = heads[n][1]
                return carry[n] + dot_plain(turned[n // 2][s * HEAD : (s + 1) * HEAD], d_scores)

            return skewed(len(heads), score, soften, gather)

        start = tuple(jnp.zeros((HEAD, tile), jnp.float32) for _ in heads)
        done = lax.fori_loop(bounds[0, i], bounds[1, i], body, start)
        for p, c in enumerate(cols):
            both = jnp.concatenate(done[2 * p : 2 * p + 2], axis=0) * HEAD**-0.5
            out[rows, c] = both.T.astype(jnp.bfloat16)


def query_grad(bounds, query, grad, keys, values, logsum, centre, first, last, tile, step, group):
    tokens, width = query.shape
    wide = keys.shape[0]
    return pl.pallas_call(
        functools.partial(query_grad_kernel, tile, step),
        grid_spec=pltpu.PrefetchScalarGridSpec(
            num_scalar_prefetch=1,
            grid=(H // group,),
            in_specs=[columns(tokens, group)] * 2
            + [columns(wide, group)] * 2
            + [lines(tokens, group)] * 2
            + [whole(1, tokens)] * 2,
            out_specs=columns(tokens, group),
        ),
        out_shape=jax.ShapeDtypeStruct((tokens, width), jnp.bfloat16),
        compiler_params=VMEM,
        cost_estimate=cost(3),
        name="query_grad",
    )(bounds, query, grad, keys, values, logsum, centre, first, last)


def key_grad_kernel(tile, step, start_row, bounds, keys, values, query, grad, logsum, centre, first, last, d_keys, d_values):
    pairs = keys.shape[1] // PAIR
    lane = lax.broadcasted_iota(jnp.int32, (1, PAIR), 1)
    for i in range(keys.shape[0] // tile):
        rows = slice(i * tile, (i + 1) * tile)
        cols = [slice(p * PAIR, (p + 1) * PAIR) for p in range(pairs)]
        heads = [
            (c, 2 * p + s, one_side(keys[rows, c], s, HEAD**-0.5), one_side(values[rows, c], s))
            for p, c in enumerate(cols)
            for s in range(2)
        ]

        def body(j, carry):
            block = pl.ds(pl.multiple_of(j * step, step), step)
            allowed = allowed_pairs(first[:, block], last[:, block], start_row + i * tile, (tile, step))

            def score(m):
                c, n, k, v = heads[m]
                return dot_last(k, query[block, c]), dot_last(v, grad[block, c])

            def soften(m, both):
                n = heads[m][1]
                weights = jnp.exp(jnp.where(allowed, both[0] - logsum[n, :, block], MASKED))
                return (weights * (both[1] - centre[n, :, block])).astype(jnp.bfloat16), weights.astype(jnp.bfloat16)

            def gather(m, soft):
                c = heads[m][0]
                return (
                    carry[m][0] + dot_plain(soft[0], query[block, c]),
                    carry[m][1] + dot_plain(soft[1], grad[block, c]),
                )

            return skewed(len(heads), score, soften, gather)

        zero = jnp.zeros((tile, PAIR), jnp.float32)
        done = lax.fori_loop(bounds[0, i], bounds[1, i], body, tuple((zero, zero) for _ in heads))
        for p, c in enumerate(cols):
            (k0, v0), (k1, v1) = done[2 * p : 2 * p + 2]
            d_keys[rows, c] = (jnp.where(lane < HEAD, k0, k1) * HEAD**-0.5).astype(jnp.bfloat16)
            d_values[rows, c] = jnp.where(lane < HEAD, v0, v1).astype(jnp.bfloat16)


def key_grad(bounds, keys, values, query, grad, logsum, centre, first, last, tile, step, group):
    tokens, width = keys.shape
    wide = query.shape[0]
    return pl.pallas_call(
        functools.partial(key_grad_kernel, tile, step, REACH * tokens),
        grid_spec=pltpu.PrefetchScalarGridSpec(
            num_scalar_prefetch=1,
            grid=(H // group,),
            in_specs=[columns(tokens, group)] * 2
            + [columns(wide, group)] * 2
            + [lines(wide, group)] * 2
            + [whole(1, wide)] * 2,
            out_specs=[columns(tokens, group), columns(tokens, group)],
        ),
        out_shape=[jax.ShapeDtypeStruct((tokens, width), jnp.bfloat16)] * 2,
        compiler_params=VMEM,
        cost_estimate=cost(4),
        name="key_grad",
    )(bounds, keys, values, query, grad, logsum, centre, first, last)


eps_norm = 1e-06
AXES = ("items", "rows")


NAMES = (
    "query_proj", "key_proj", "value_proj", "query_bias", "value_bias", "output_proj", "output_bias", "attn_gain",
    "attn_shift", "hidden_proj", "hidden_bias", "return_proj", "return_bias", "final_gain", "final_shift",
)


def dot_rows(matrix, factor):
    return lax.dot_general(matrix, factor, (((0,), (0,)), ((), ())), preferred_element_type=jnp.float32)


def layer_norm(hidden, norm_gain, norm_shift):
    row_mean = jnp.mean(hidden, axis=1, keepdims=True)
    centred = hidden - row_mean
    row_var = jnp.mean(centred * centred, axis=1, keepdims=True)
    return centred * lax.rsqrt(row_var + eps_norm) * norm_gain + norm_shift


def shifted(value, by):
    peers = lax.axis_size("rows")
    pairs = [(i, i + by) for i in range(peers) if 0 <= i + by < peers]
    return lax.ppermute(value, "rows", pairs)


def halo(value):
    return [value if d == 0 else shifted(value, -d) for d in range(-REACH, REACH + 1)]


def item_tables(lengths, position, rows_dev, tile, step):
    ends = jnp.cumsum(lengths, dtype=jnp.int32)
    wide = (2 * REACH + 1) * rows_dev
    base = position - REACH * rows_dev

    def item_of(places):
        low = jnp.max(jnp.where(ends[None, :] <= places[:, None], ends[None, :], 0), axis=1)
        high = jnp.min(jnp.where(ends[None, :] > places[:, None], ends[None, :], ends[-1]), axis=1)
        return low - base, high - base

    places = base + jnp.arange(wide, dtype=jnp.int32)
    first, last = item_of(places)
    inside = (places >= 0) & (places < ends[-1])
    first, last = jnp.where(inside, first, wide), jnp.where(inside, last, -1)
    starts = position + jnp.arange(0, rows_dev, tile, dtype=jnp.int32)
    bounds = jnp.stack([item_of(starts)[0] // step, (item_of(starts + tile - 1)[1] + step - 1) // step])
    return first[None, :], last[None, :], jnp.clip(bounds, 0, wide // step).astype(jnp.int32)


TILE, STEP, GROUP = 256, 256, 12


def per_device(mesh_shape, tokens, *given):
    names = NAMES
    part = dict(zip(names, given[:15]))
    item_lengths, out_grad = given[15:]
    matrices = ["query_proj", "key_proj", "value_proj", "output_proj", "hidden_proj", "return_proj"]
    vectors = [n for n in names if n not in matrices]
    ndev = mesh_shape["items"] * mesh_shape["rows"]
    rows_dev, width = tokens.shape
    aligned = all(part[n].shape[0] % 8 == 0 for n in matrices)
    sizes = [part[n].shape[0] for n in vectors]
    used = sum(sizes)
    padded = -(-used // 1024) * 1024
    packed = jnp.pad(jnp.concatenate([part[n] for n in vectors]), (0, padded - used)).reshape(8, padded // 8)
    if aligned:
        got = gather_all(mesh_shape, tokens, [part[n] for n in matrices] + [packed])
        window = got[0].reshape(-1, width)
        wholes = [g.reshape((-1,) + g.shape[2:]) for g in got[1:-1]]
        flat = got[-1]
    else:
        window = jnp.concatenate(halo(tokens))
        wholes = [lax.all_gather(part[n], AXES, axis=0, tiled=True) for n in matrices]
        flat = lax.all_gather(packed, AXES, axis=0, tiled=False)
    flat = flat.reshape(ndev, padded)
    W = dict(zip(matrices, wholes))
    at = 0
    for n, size in zip(vectors, sizes):
        W[n] = flat[:, at : at + size].reshape(-1).astype(jnp.float32)
        at += size

    position = lax.axis_index("rows") * rows_dev
    first, last, bounds = item_tables(item_lengths[0], position, rows_dev, TILE, STEP)
    own = slice(REACH * rows_dev, (REACH + 1) * rows_dev)
    own_items = first[:, own], last[:, own]

    query_wide = (dot_plain(window, W["query_proj"]) + W["query_bias"]).astype(jnp.bfloat16)
    keys_wide = dot_plain(window, W["key_proj"]).astype(jnp.bfloat16)
    values_wide = (dot_plain(window, W["value_proj"]) + W["value_bias"]).astype(jnp.bfloat16)
    query, keys, values = query_wide[own], keys_wide[own], values_wide[own]
    attended, attended_full, logsum = attend(
        bounds, query, keys_wide, values_wide, *own_items, TILE, STEP, GROUP
    )

    mixed = tokens.astype(jnp.float32) + (dot_plain(attended, W["output_proj"]) + W["output_bias"])
    normed, attn_back = jax.vjp(layer_norm, mixed, W["attn_gain"], W["attn_shift"])
    normed_low = normed.astype(jnp.bfloat16)
    hidden_pre = dot_plain(normed_low, W["hidden_proj"]) + W["hidden_bias"]
    cdf = 0.5 * (1.0 + lax.erf(hidden_pre * (0.5**0.5)))
    active = (hidden_pre * cdf).astype(jnp.bfloat16)
    slope = cdf + hidden_pre * jnp.exp(-0.5 * hidden_pre * hidden_pre) * 0.3989422804014327
    second = normed + (dot_plain(active, W["return_proj"]) + W["return_bias"])
    result, final_back = jax.vjp(layer_norm, second, W["final_gain"], W["final_shift"])

    grads = {}
    d_second, grads["final_gain"], grads["final_shift"] = final_back(out_grad.astype(jnp.float32))
    d_ffn = d_second.astype(jnp.bfloat16)
    grads["return_bias"] = jnp.sum(d_ffn.astype(jnp.float32), axis=0)
    d_hidden = (dot_last(d_ffn, W["return_proj"]) * slope).astype(jnp.bfloat16)
    grads["hidden_bias"] = jnp.sum(d_hidden.astype(jnp.float32), axis=0)
    d_normed = dot_last(d_hidden, W["hidden_proj"]) + d_second
    d_mixed, grads["attn_gain"], grads["attn_shift"] = attn_back(d_normed)
    d_branch = d_mixed.astype(jnp.bfloat16)
    grads["output_bias"] = jnp.sum(d_branch.astype(jnp.float32), axis=0)
    d_attended = dot_last(d_branch, W["output_proj"]).astype(jnp.bfloat16)

    lanes = jnp.arange(width, dtype=jnp.int32)[None, :] // HEAD == jnp.arange(16, dtype=jnp.int32)[:, None]
    centre = lax.dot_general(
        lanes.astype(jnp.float32), d_attended.astype(jnp.float32) * attended_full, (((1,), (1,)), ((), ())),
        precision=lax.Precision.HIGHEST,
    )[:H, None]
    stats = jnp.concatenate([logsum, centre])
    grad_wide = jnp.concatenate(halo(d_attended))
    stats_wide = jnp.concatenate(halo(stats), axis=2)
    grads["return_proj"] = dot_rows(active, d_ffn)
    grads["hidden_proj"] = dot_rows(normed_low, d_hidden)
    grads["output_proj"] = dot_rows(attended, d_branch)
    d_query = query_grad(
        bounds, query, d_attended, keys_wide, values_wide, logsum, centre, *own_items, TILE, STEP, GROUP
    )
    d_keys, d_values = key_grad(
        bounds, keys, values, query_wide, grad_wide, stats_wide[:H], stats_wide[H:], first, last, TILE, STEP, GROUP
    )
    grads["query_proj"] = dot_rows(tokens, d_query)
    grads["key_proj"] = dot_rows(tokens, d_keys)
    grads["value_proj"] = dot_rows(tokens, d_values)
    grads["query_bias"] = jnp.sum(d_query.astype(jnp.float32), axis=0)
    grads["value_bias"] = jnp.sum(d_values.astype(jnp.float32), axis=0)
    tokens_grad = (
        d_mixed
        + dot_last(d_query, W["query_proj"])
        + dot_last(d_keys, W["key_proj"])
        + dot_last(d_values, W["value_proj"])
    )

    rows_of = jnp.concatenate([grads[n].reshape(ndev, size) for n, size in zip(vectors, sizes)], axis=1)
    rows_of = jnp.pad(rows_of, ((0, 0), (0, padded - used))).reshape(ndev, 8, padded // 8)
    low = [grads[n].astype(jnp.bfloat16).reshape((ndev, -1) + grads[n].shape[1:]) for n in matrices]
    if aligned:
        height = min(g.shape[1] for g in low)
        sums = scatter_all(mesh_shape, low + [rows_of], [(height, width)] * len(low) + [rows_of.shape[1:]])
    else:
        sums = [lax.psum_scatter(g, AXES, scatter_dimension=0, tiled=True)[0] for g in low + [rows_of]]
    total = {n: s.astype(jnp.float32) for n, s in zip(matrices, sums)}
    line = sums[-1].reshape(padded)
    at = 0
    for n, size in zip(vectors, sizes):
        total[n] = line[at : at + size]
        at += size
    return (result.astype(jnp.bfloat16), tokens_grad) + tuple(total[n] for n in names)


def solution(mesh):
    both = P(AXES)
    return jax.shard_map(
        functools.partial(per_device, dict(mesh.shape)),
        mesh=mesh,
        in_specs=(both,) * 16 + (P("items"), both),
        out_specs=(both,) * 17,
        check_vma=False,
    )
```

```python
import functools
import jax
import jax.numpy as jnp
from jax import lax
from jax.experimental import pallas as pl
from jax.experimental.pallas import tpu as pltpu

from jax.sharding import PartitionSpec as P

MESH = pl.DeviceIdType.MESH
REACH = 2


def split_rows(rows):
    inner = 1
    while (2 * inner) ** 2 <= rows:
        inner *= 2
    return rows // inner, inner


def place(nz, ny):
    item, row = lax.axis_index("items"), lax.axis_index("rows")
    return item // 2, item % 2, row // ny, row % ny


def near(z, step, nz):
    way = 1 - 2 * (z // ((nz + 1) // 2))
    return lax.rem(z + way * step + nz * 2, nz)


def spread_row(tiles, n, size):
    devices = tiles.shape[0]
    column = lax.broadcasted_iota(jnp.int32, (1, devices * size), 1).astype(jnp.float32)
    owner = jnp.floor((column + 0.5) / size)
    lane = lax.broadcasted_iota(jnp.int32, (tiles.shape[2], 1), 0).astype(jnp.float32)
    pick = (column - owner * size == lane).astype(jnp.float32).astype(jnp.bfloat16)
    spread = jnp.dot(tiles[:, n, :].astype(jnp.bfloat16), pick, preferred_element_type=jnp.float32)
    device = lax.broadcasted_iota(jnp.int32, (devices, 1), 0).astype(jnp.float32)
    return jnp.sum(jnp.where(owner == device, spread, 0.0), axis=0, keepdims=True)


def gather_kernel(na, nz, ny, sizes, *refs):
    weights = 6
    count = weights + 1
    tokens = refs[0]
    mine = list(refs[1 : 1 + weights])
    lines = refs[1 + weights : 1 + weights + len(sizes)]
    refs = refs[1 + weights + len(sizes) :]
    full = list(refs[:weights])
    rows_out = refs[weights : weights + len(sizes)]
    wide = refs[weights + len(sizes) : weights + len(sizes) + 3]
    (
        packed, tiles, window, matrix, made, out_sem, load_sem, halo_send, halo_recv, local_sem,
        s1, r1, s2, r2, s3, r3, s4, r4,
    ) = refs[weights + len(sizes) + 3 :]
    mine.append(packed)
    full.append(tiles)
    packed[...] = jnp.zeros_like(packed)
    for n, line in enumerate(lines):
        packed[n : n + 1, : line.shape[1]] = line[...].astype(jnp.float32)

    a, c, z, y = place(nz, ny)
    rows = nz * ny
    row = z * ny + y
    item = a * 2 + c

    def slot(a_, z_, y_):
        return (a_ * 2 + c) * rows + z_ * ny + y_

    barrier = pltpu.get_barrier_semaphore()

    def greet(i_, r_):
        pl.semaphore_signal(barrier, inc=1, device_id=(i_, r_), device_id_type=MESH)

    for d in range(1, nz):
        greet(item, near(z, d, nz) * ny + y)
    for d in range(1, ny):
        greet(item, z * ny + lax.rem(y + d, ny))
    for d in range(1, na):
        greet(lax.rem(a + d, na) * 2 + c, row)
    greet(a * 2 + 1 - c, row)
    for d in range(-REACH, REACH + 1):
        if d != 0:
            greet(item, lax.rem(row + d + rows, rows))
    pl.semaphore_wait(barrier, nz + ny + na - 2 + 2 * REACH)

    def remote(src, dst, send, recv, i_, r_):
        return pltpu.make_async_remote_copy(
            src_ref=src, dst_ref=dst, send_sem=send, recv_sem=recv, device_id=(i_, r_), device_id_type=MESH
        )

    def arrived(part, recv):
        remote(part, part, s1.at[0, 0], recv, item, row).wait_recv()

    soon, later = (0, 1, 2, weights), (3, 4, 5)
    for group in (soon, later):
        for d in range(1, nz):
            for n in group:
                remote(
                    mine[n], full[n].at[slot(a, z, y)], s1.at[d, n], r1.at[z, n], item, near(z, d, nz) * ny + y
                ).start()
    locals_ = [pltpu.make_async_copy(mine[n], full[n].at[slot(a, z, y)], local_sem.at[n]) for n in range(count)]
    locals_.append(pltpu.make_async_copy(tokens, window.at[REACH], local_sem.at[count]))
    for copy in locals_:
        copy.start()

    def halo(d, start):
        k = d + REACH

        @pl.when((row + d >= 0) & (row + d < rows))
        def _():
            if start:
                remote(
                    tokens, window.at[REACH - d], halo_send.at[k], halo_recv.at[REACH - d], item, row + d
                ).start()
            else:
                part = window.at[k]
                arrived(part, halo_recv.at[k])

        @pl.when((row + d < 0) | (row + d >= rows))
        def _():
            copy = pltpu.make_async_copy(tokens, window.at[k], halo_recv.at[k])
            if start:
                copy.start()
            else:
                copy.wait()

    def second(step, group):
        zz = near(z, step, nz)
        for n in group:
            part = full[n].at[slot(a, zz, y)]
            if step:
                arrived(part, r1.at[zz, n])
            for d in range(1, ny):
                remote(
                    part if step else mine[n], part, s2.at[step, d, n], r2.at[zz, y, n], item, z * ny + lax.rem(y + d, ny)
                ).start()

    def third(step, group):
        zz = near(z, step, nz)
        for n in group:
            for d in range(1, ny):
                yy = lax.rem(y + d, ny)
                arrived(full[n].at[slot(a, zz, yy)], r2.at[zz, yy, n])
            if step == 0:
                locals_[n].wait()
            block = full[n].at[pl.ds(slot(a, zz, 0), ny)]
            for d in range(1, na):
                remote(
                    block, block, s3.at[step, d, n], r3.at[zz, a, n], lax.rem(a + d, na) * 2 + c, row
                ).start()

    def fourth(step, group):
        zz = near(z, step, nz)
        for e in range(na):
            aa = lax.rem(a + e, na)
            for n in group:
                block = full[n].at[pl.ds(slot(aa, zz, 0), ny)]
                if e:
                    arrived(block, r3.at[zz, aa, n])
                remote(block, block, s4.at[e, step, n], r4.at[aa, zz, n], a * 2 + 1 - c, row).start()

    def settle(group):
        for n in group:
            for e in range(na):
                for step in range(nz):
                    theirs = full[n].at[pl.ds((e * 2 + 1 - c) * rows + step * ny, ny)]
                    arrived(theirs, r4.at[e, step, n])

    loads = [
        pltpu.make_async_copy(full[n], matrix.at[n], load_sem.at[n]) for n in range(3)
    ]
    stores = []

    def project(block, n):
        factor = matrix[n].reshape(tokens.shape[1], tokens.shape[1])
        total = jnp.dot(window[block], factor, preferred_element_type=jnp.float32)
        if n != 1:
            total = total + rows_out[n // 2][...]
        made[block, n] = total.astype(jnp.bfloat16)
        store = pltpu.make_async_copy(
            made.at[block, n], wide[n].at[pl.ds(block * tokens.shape[0], tokens.shape[0])], out_sem.at[block, n]
        )
        store.start()
        stores.append(store)

    second(0, soon)
    second(0, later)
    for t in range(1, nz):
        second(t, soon)
        third(t - 1, soon)
    third(nz - 1, soon)
    third(0, later)
    for t in range(1, nz):
        second(t, later)
        third(t, later)
        fourth(t - 1, soon)
    for d in HALO_ORDER:
        halo(d, True)
    fourth(nz - 1, soon)
    fourth(0, later)
    settle(soon)
    for load in loads:
        load.start()
    for n, size in enumerate(sizes):
        rows_out[n][...] = spread_row(tiles, n, size)
    fourth(1, later)
    locals_[count].wait()
    for n in range(3):
        loads[n].wait()
        project(REACH, n)
    for t in range(2, nz - 1):
        fourth(t, later)
    for k, d in enumerate(HALO_ORDER):
        halo(d, False)
        for n in range(3):
            project(REACH + d, n)
        if k == 1:
            fourth(nz - 1, later)
    settle(later)

    for n in range(count):
        for step in range(nz):
            part = full[n].at[slot(a, z, y)]
            if step:
                remote(mine[n], part, s1.at[step, n], r1.at[z, n], item, row).wait_send()
            for d in range(1, ny):
                remote(part, part, s2.at[step, d, n], r2.at[z, y, n], item, row).wait_send()
            block = full[n].at[pl.ds(slot(a, z, 0), ny)]
            for d in range(1, na):
                remote(block, block, s3.at[step, d, n], r3.at[z, a, n], item, row).wait_send()
            for e in range(na):
                remote(block, block, s4.at[e, step, n], r4.at[0, 0, n], item, row).wait_send()
    for d in HALO_ORDER:

        @pl.when((row + d >= 0) & (row + d < rows))
        def _():
            remote(
                tokens, window.at[REACH - d], halo_send.at[d + REACH], halo_recv.at[REACH - d], item, row
            ).wait_send()

    for store in stores:
        store.wait()


HALO_ORDER = (1, -1, 2, -2)


def gather_all(mesh_shape, tokens, shards, vectors):
    na = mesh_shape["items"] // 2
    nz, ny = split_rows(mesh_shape["rows"])
    ndev = mesh_shape["items"] * mesh_shape["rows"]
    count = len(shards) + 1
    rows_dev, width = tokens.shape
    blocks = 2 * REACH + 1
    dma = pltpu.SemaphoreType.DMA
    packed = (-(-len(vectors) // 8) * 8, 128)
    sizes = tuple(v.shape[0] for v in vectors)
    wide = jax.ShapeDtypeStruct((blocks * rows_dev, width), tokens.dtype)
    hbm, vmem = pl.BlockSpec(memory_space=pl.ANY), pl.BlockSpec(memory_space=pltpu.VMEM)
    return pl.pallas_call(
        functools.partial(gather_kernel, na, nz, ny, sizes),
        out_shape=[jax.ShapeDtypeStruct((ndev,) + s.shape, s.dtype) for s in shards]
        + [jax.ShapeDtypeStruct((1, ndev * size), jnp.float32) for size in sizes]
        + [wide] * 3,
        in_specs=[vmem] * (count + len(vectors)),
        out_specs=[hbm] * len(shards) + [vmem] * len(sizes) + [hbm] * 3,
        scratch_shapes=[
            pltpu.VMEM(packed, jnp.float32),
            pltpu.VMEM((ndev,) + packed, jnp.float32),
            pltpu.VMEM((blocks,) + tokens.shape, tokens.dtype),
            pltpu.VMEM((3, ndev) + shards[0].shape, tokens.dtype),
            pltpu.VMEM((blocks, 3) + tokens.shape, tokens.dtype),
            dma((blocks, 3)), dma((3,)),
            dma((blocks,)), dma((blocks,)), dma((count + 1,)),
            dma((nz, count)), dma((nz, count)),
            dma((nz, ny, count)), dma((nz, ny, count)),
            dma((nz, na, count)), dma((nz, na, count)),
            dma((na, nz, count)), dma((na, nz, count)),
        ],
        compiler_params=pltpu.CompilerParams(collective_id=1, has_side_effects=True, vmem_limit_bytes=56 << 20),
        name="gather_weights",
    )(tokens, *shards, *[v[None] for v in vectors])


def scatter_kernel(na, nz, ny, plan, *refs):
    inputs = max(p[0] for p in plan) + 1
    given = refs[:inputs]
    outs = refs[inputs : 2 * inputs]
    scratch = refs[2 * inputs :]
    groups = (len(scratch) - 9) // 5
    bufs = [scratch[5 * g : 5 * g + 5] for g in range(groups)]
    load_sem, s0, r0, s1, r1, s2, r2, s3, r3 = scratch[5 * groups :]
    a, c, z, y = place(nz, ny)
    rows = nz * ny
    row = z * ny + y
    item = a * 2 + c

    barrier = pltpu.get_barrier_semaphore()

    def greet(i_, r_):
        pl.semaphore_signal(barrier, inc=1, device_id=(i_, r_), device_id_type=MESH)

    def at_z(d):
        return lax.rem(z + d, nz) * ny + y

    def at_y(d):
        return z * ny + lax.rem(y + d, ny)

    def at_a(d):
        return lax.rem(a + d, na) * 2 + c

    for d in range(1, nz):
        greet(item, at_z(d))
    for d in range(1, ny):
        greet(item, at_y(d))
    for d in range(1, na):
        greet(at_a(d), row)
    greet(a * 2 + 1 - c, row)
    pl.semaphore_wait(barrier, nz + ny + na - 2)

    def remote(src, dst, send, recv, i_, r_):
        return pltpu.make_async_remote_copy(
            src_ref=src, dst_ref=dst, send_sem=send, recv_sem=recv, device_id=(i_, r_), device_id_type=MESH
        )

    order, seen = [], {}
    for p in plan:
        order.append(seen.get(p[3], 0))
        seen[p[3]] = order[-1] + 1

    def buf(k, which):
        return bufs[plan[k][3]][which].at[order[k]]

    def source(k, item_, zz):
        ref, (number, first, column, group) = given[plan[k][0]], plan[k]
        height, width = bufs[group][0].shape[-2:]
        return ref.at[pl.ds(item_ * rows + zz * ny, ny), pl.ds(first, height), pl.ds(column, width)]

    def load(k, aa, zz):
        return pltpu.make_async_copy(source(k, aa * 2 + c, zz), buf(k, 0).at[aa, zz], load_sem.at[k, aa, zz])

    def core(k, aa, zz):
        return remote(
            source(k, aa * 2 + 1 - c, zz), buf(k, 1).at[aa, zz], s0.at[k, aa, zz], r0.at[k, aa, zz], a * 2 + 1 - c, row
        )

    def first0(k, d, zz):
        aa = lax.rem(a + d, na)
        return remote(
            buf(k, 0).at[aa, zz], buf(k, 2).at[pl.ds((d - 1) * rows + zz * ny, ny)],
            s1.at[k, d, zz], r1.at[k, d, zz], at_a(d), row,
        )

    def first1(k, d, aa):
        return remote(
            buf(k, 0).at[aa, :, lax.rem(y + d, ny)], buf(k, 2).at[pl.ds((d - 1) * na * nz + aa * nz, nz)],
            s1.at[k, d, aa], r1.at[k, d, aa], item, at_y(d),
        )

    def second0(k, d):
        return remote(
            buf(k, 0).at[a, :, lax.rem(y + d, ny)], buf(k, 3).at[pl.ds((d - 1) * nz, nz)],
            s2.at[k, d], r2.at[k, d], item, at_y(d),
        )

    def second1(k, d):
        return remote(
            buf(k, 0).at[lax.rem(a + d, na), :, y], buf(k, 3).at[pl.ds((d - 1) * nz, nz)],
            s2.at[k, d], r2.at[k, d], at_a(d), row,
        )

    def third(k, d):
        return remote(
            buf(k, 0).at[a, lax.rem(z + d, nz), y], buf(k, 4).at[d - 1], s3.at[k, d], r3.at[k, d], item, at_z(d)
        )

    def summed(refs_):
        total = refs_[0][...].astype(jnp.float32)
        for ref in refs_[1:]:
            total = total + ref[...].astype(jnp.float32)
        return total

    def add_into(dst, parts):
        dst[...] = summed([dst] + parts).astype(dst.dtype)

    chunks = range(len(plan))
    for k in chunks:
        for e in range(na):
            for zz in range(nz):
                core(k, lax.rem(a + 1 + e, na), zz).start()
                load(k, lax.rem(a + 1 + e, na), zz).start()

    def stage1(k):
        for e in range(na):
            aa = lax.rem(a + 1 + e, na)
            for zz in range(nz):
                load(k, aa, zz).wait()
                core(k, aa, zz).wait_recv()

                @pl.loop(0, ny)
                def _(yy):
                    add_into(buf(k, 0).at[aa, zz, yy], [buf(k, 1).at[aa, zz, yy]])

                if e < na - 1:

                    @pl.when(c == 0)
                    def _():
                        first0(k, e + 1, zz).start()

        @pl.when(c == 1)
        def _():
            for d in range(1, ny):
                for aa in range(na):
                    first1(k, d, aa).start()

    def stage2(k):
        @pl.when(c == 0)
        def _():
            for zz in range(nz):
                for d in range(1, na):
                    first0(k, d, zz).wait_recv()

                @pl.loop(0, ny)
                def _(yy):
                    add_into(
                        buf(k, 0).at[a, zz, yy], [buf(k, 2).at[(d - 1) * rows + zz * ny + yy] for d in range(1, na)]
                    )

            for d in range(1, ny):
                second0(k, d).start()

        @pl.when(c == 1)
        def _():
            for e in range(na):
                for d in range(1, ny):
                    for aa in range(na):
                        if e == 0:
                            first1(k, d, aa).wait_recv()
                aa = lax.rem(a + 1 + e, na)

                @pl.loop(0, nz)
                def _(zz):
                    add_into(
                        buf(k, 0).at[aa, zz, y],
                        [buf(k, 2).at[(d - 1) * na * nz + aa * nz + zz] for d in range(1, ny)],
                    )

            for d in range(1, na):
                second1(k, d).start()

    def stage3(k):
        width = na if na > ny else ny
        for d in range(1, width):
            if d < ny and d < na:
                second0(k, d).wait_recv()
            elif d < ny:

                @pl.when(c == 0)
                def _():
                    second0(k, d).wait_recv()

            else:

                @pl.when(c == 1)
                def _():
                    second1(k, d).wait_recv()

        def add_second(peers):
            @pl.loop(0, nz)
            def _(zz):
                add_into(buf(k, 0).at[a, zz, y], [buf(k, 3).at[(d - 1) * nz + zz] for d in range(1, peers)])

        if na == ny:
            add_second(na)
        else:

            @pl.when(c == 0)
            def _():
                add_second(ny)

            @pl.when(c == 1)
            def _():
                add_second(na)

        for d in range(1, nz):
            third(k, d).start()

    def stage4(k):
        for d in range(1, nz):
            third(k, d).wait_recv()
        number, first, column, group = plan[k]
        height, width = bufs[group][0].shape[-2:]
        outs[number][first : first + height, column : column + width] = summed(
            [buf(k, 0).at[a, z, y]] + [buf(k, 4).at[d - 1] for d in range(1, nz)]
        )

    stages = (stage1, stage2, stage3, stage4)
    for t in range(len(plan) + 3):
        for n, stage in enumerate(stages):
            if 0 <= t - n < len(plan):
                stage(t - n)

    for k in chunks:
        for aa in range(na):
            for zz in range(nz):
                core(k, aa, zz).wait_send()
        for d in range(1, nz):
            third(k, d).wait_send()

        @pl.when(c == 0)
        def _():
            for d in range(1, na):
                for zz in range(nz):
                    first0(k, d, zz).wait_send()
            for d in range(1, ny):
                second0(k, d).wait_send()

        @pl.when(c == 1)
        def _():
            for d in range(1, ny):
                for aa in range(na):
                    first1(k, d, aa).wait_send()
            for d in range(1, na):
                second1(k, d).wait_send()


def scatter_all(mesh_shape, grads, pieces, collective_id=2):
    na = mesh_shape["items"] // 2
    nz, ny = split_rows(mesh_shape["rows"])
    plan, kinds, number = [], [], []
    for n, (g, (height, width)) in enumerate(zip(grads, pieces)):
        kind = (height, width, g.dtype)
        if kind not in kinds:
            kinds.append(kind)
            number.append(0)
        group = kinds.index(kind)
        for first in range(0, g.shape[1], height):
            for column in range(0, g.shape[2], width):
                plan.append((n, first, column, group))
                number[group] += 1
    scratch = []
    for (height, width, dtype), many in zip(kinds, number):
        one = (height, width)
        first = max((na - 1) * nz * ny, (ny - 1) * na * nz)
        second = (max(na, ny) - 1) * nz
        scratch += [
            pltpu.VMEM((many, na, nz, ny) + one, dtype),
            pltpu.VMEM((many, na, nz, ny) + one, dtype),
            pltpu.VMEM((many, first) + one, dtype),
            pltpu.VMEM((many, second) + one, dtype),
            pltpu.VMEM((many, nz - 1) + one, dtype),
        ]
    k = len(plan)
    dma = pltpu.SemaphoreType.DMA
    nm = max(na, ny)
    scratch += [dma((k, na, nz))] * 3 + [dma((k, nm, max(nz, na)))] * 2 + [dma((k, nm))] * 2 + [dma((k, nz))] * 2
    return pl.pallas_call(
        functools.partial(scatter_kernel, na, nz, ny, tuple(plan)),
        out_shape=[jax.ShapeDtypeStruct(g.shape[1:], jnp.float32) for g in grads],
        in_specs=[pl.BlockSpec(memory_space=pl.ANY)] * len(grads),
        out_specs=[pl.BlockSpec(memory_space=pltpu.VMEM)] * len(grads),
        scratch_shapes=scratch,
        compiler_params=pltpu.CompilerParams(
            collective_id=collective_id, has_side_effects=True, vmem_limit_bytes=60 << 20
        ),
        name="scatter_grads",
    )(*grads)


H = 12
HEAD = 64
PAIR = 2 * HEAD
MASKED = -1e30


def dot_last(x, y):
    return lax.dot_general(x, y, (((1,), (1,)), ((), ())), preferred_element_type=jnp.float32)


def dot_plain(x, y):
    return jnp.dot(x, y, preferred_element_type=jnp.float32)


def one_side(block, side, scale=1.0):
    lane = lax.broadcasted_iota(jnp.int32, (1, PAIR), 1)
    keep = (lane // HEAD == side).astype(jnp.float32) * scale
    return (block.astype(jnp.float32) * keep).astype(jnp.bfloat16)


def allowed_pairs(first, last, base, shape):
    place = lax.broadcasted_iota(jnp.int32, shape, 0)
    return (place >= first - base) & (place < last - base)


def skewed(count, *stages):
    held = [None] * count
    for t in range(count + len(stages) - 1):
        for k, stage in enumerate(stages):
            n = t - k
            if 0 <= n < count:
                held[n] = stage(n) if k == 0 else stage(n, held[n])
    return tuple(held)


def attend_kernel(tile, step, bounds, query, keys, values, first, last, low, full, logsum):
    pairs = query.shape[1] // PAIR
    for i in range(query.shape[0] // tile):
        rows = slice(i * tile, (i + 1) * tile)
        cols = [slice(p * PAIR, (p + 1) * PAIR) for p in range(pairs)]
        heads = [(c, s, one_side(query[rows, c], s, HEAD**-0.5)) for c in cols for s in range(2)]
        start_at, end_at = first[:, rows], last[:, rows]

        def body(j, carry):
            block = pl.ds(pl.multiple_of(j * step, step), step)
            allowed = allowed_pairs(start_at, end_at, j * step, (step, tile))
            turned = [values[block, c].T for c in cols]

            def score(n):
                c, s, q = heads[n]
                return jnp.where(allowed, dot_last(keys[block, c], q), MASKED)

            def soften(n, scores):
                top, total, acc = carry[n]
                peak = jnp.maximum(top, jnp.max(scores, axis=0, keepdims=True))
                lifted = jnp.exp(scores - peak)
                fade = jnp.exp(top - peak)
                return peak, total * fade + jnp.sum(lifted, axis=0, keepdims=True), fade, lifted.astype(jnp.bfloat16)

            def gather(n, soft):
                peak, total, fade, lifted = soft
                s = heads[n][1]
                return peak, total, carry[n][2] * fade + dot_plain(turned[n // 2][s * HEAD : (s + 1) * HEAD], lifted)

            return skewed(len(heads), score, soften, gather)

        start = tuple(
            (
                jnp.full((1, tile), MASKED, jnp.float32),
                jnp.zeros((1, tile), jnp.float32),
                jnp.zeros((HEAD, tile), jnp.float32),
            )
            for _ in heads
        )
        done = lax.fori_loop(bounds[0, i], bounds[1, i], body, start)
        for p, c in enumerate(cols):
            (top0, total0, acc0), (top1, total1, acc1) = done[2 * p : 2 * p + 2]
            result = jnp.concatenate([acc0 / total0, acc1 / total1], axis=0).T
            low[rows, c] = result.astype(jnp.bfloat16)
            full[rows, c] = result
            logsum[2 * p, :, rows] = top0 + jnp.log(total0)
            logsum[2 * p + 1, :, rows] = top1 + jnp.log(total1)


def columns(rows, group, block=0):
    return pl.BlockSpec((rows, group * HEAD), lambda p, b: (block, p))


def lines(length, group):
    return pl.BlockSpec((group, 1, length), lambda p, b: (p, 0, 0))


def whole(*shape):
    return pl.BlockSpec(shape, lambda p, b: (0,) * len(shape))


def cost(matmuls):
    return pl.CostEstimate(flops=matmuls * 2 * H * HEAD * 512 * 1536, bytes_accessed=12 << 20, transcendentals=0)


VMEM = pltpu.CompilerParams(vmem_limit_bytes=56 << 20)


def attend(bounds, query, keys, values, first, last, tile, step, group):
    wide, width = keys.shape
    tokens = first.shape[1]
    return pl.pallas_call(
        functools.partial(attend_kernel, tile, step),
        grid_spec=pltpu.PrefetchScalarGridSpec(
            num_scalar_prefetch=1,
            grid=(H // group,),
            in_specs=[columns(tokens, group, REACH), columns(wide, group), columns(wide, group)] + [whole(1, tokens)] * 2,
            out_specs=[columns(tokens, group), columns(tokens, group), lines(tokens, group)],
        ),
        out_shape=[
            jax.ShapeDtypeStruct((tokens, width), jnp.bfloat16),
            jax.ShapeDtypeStruct((tokens, width), jnp.float32),
            jax.ShapeDtypeStruct((H, 1, tokens), jnp.float32),
        ],
        compiler_params=VMEM,
        cost_estimate=cost(2),
        name="attend",
    )(bounds, query, keys, values, first, last)


def query_grad_kernel(tile, step, bounds, query, grad, keys, values, logsum, centre, first, last, out):
    pairs = query.shape[1] // PAIR
    for i in range(query.shape[0] // tile):
        rows = slice(i * tile, (i + 1) * tile)
        cols = [slice(p * PAIR, (p + 1) * PAIR) for p in range(pairs)]
        heads = [
            (
                c, s, one_side(query[rows, c], s, HEAD**-0.5), one_side(grad[rows, c], s),
                logsum[2 * p + s, :, rows], centre[2 * p + s, :, rows],
            )
            for p, c in enumerate(cols)
            for s in range(2)
        ]
        start_at, end_at = first[:, rows], last[:, rows]

        def body(j, carry):
            block = pl.ds(pl.multiple_of(j * step, step), step)
            allowed = allowed_pairs(start_at, end_at, j * step, (step, tile))
            turned = [keys[block, c].T for c in cols]

            def score(n):
                c, s, q, g, top, mid = heads[n]
                return dot_last(keys[block, c], q), dot_last(values[block, c], g)

            def soften(n, both):
                top, mid = heads[n][4:]
                weights = jnp.exp(jnp.where(allowed, both[0] - top, MASKED))
                return (weights * (both[1] - mid)).astype(jnp.bfloat16)

            def gather(n, d_scores):
                s = heads[n][1]
                return carry[n] + dot_plain(turned[n // 2][s * HEAD : (s + 1) * HEAD], d_scores)

            return skewed(len(heads), score, soften, gather)

        start = tuple(jnp.zeros((HEAD, tile), jnp.float32) for _ in heads)
        done = lax.fori_loop(bounds[0, i], bounds[1, i], body, start)
        for p, c in enumerate(cols):
            both = jnp.concatenate(done[2 * p : 2 * p + 2], axis=0) * HEAD**-0.5
            out[rows, c] = both.T.astype(jnp.bfloat16)


def query_grad(bounds, query, grad, keys, values, logsum, centre, first, last, tile, step, group):
    tokens, width = grad.shape
    wide = keys.shape[0]
    return pl.pallas_call(
        functools.partial(query_grad_kernel, tile, step),
        grid_spec=pltpu.PrefetchScalarGridSpec(
            num_scalar_prefetch=1,
            grid=(H // group,),
            in_specs=[columns(tokens, group, REACH), columns(tokens, group)]
            + [columns(wide, group)] * 2
            + [lines(tokens, group)] * 2
            + [whole(1, tokens)] * 2,
            out_specs=columns(tokens, group),
        ),
        out_shape=jax.ShapeDtypeStruct((tokens, width), jnp.bfloat16),
        compiler_params=VMEM,
        cost_estimate=cost(3),
        name="query_grad",
    )(bounds, query, grad, keys, values, logsum, centre, first, last)


def key_grad_kernel(tile, step, bounds, keys, values, query, first, last, *refs):
    blocks = refs[: 2 * REACH + 1]
    d_keys, d_values, grad, arrived = refs[2 * REACH + 1 :]
    tokens, width = d_keys.shape
    copies = [pltpu.make_async_copy(b, grad.at[k], arrived.at[k]) for k, b in enumerate(blocks)]
    for copy in copies:
        copy.start()
    for copy in copies:
        copy.wait()
    cols = [slice(p * PAIR, (p + 1) * PAIR) for p in range(width // PAIR)]
    for i in range(tokens // tile):
        rows = slice(i * tile, (i + 1) * tile)
        heads = [
            (c, one_side(keys[rows, c], s, HEAD**-0.5), one_side(values[rows, c], s)) for c in cols for s in range(2)
        ]

        def body(j, carry):
            block = pl.ds(pl.multiple_of(j * step, step), step)
            of = j * step // tokens
            part = pl.ds(pl.multiple_of(j * step - of * tokens, step), step)
            allowed = allowed_pairs(first[:, block], last[:, block], REACH * tokens + i * tile, (tile, step))
            stats = grad[of, part, width:].astype(jnp.float32).T
            many = len(heads)
            stats = stats[: 2 * many] + stats[2 * many : 4 * many] + stats[4 * many : 6 * many]

            def score(n):
                c, k, v = heads[n]
                return dot_last(k, query[block, c]), dot_last(v, grad[of, part, c])

            def soften(n, both):
                weights = jnp.exp(jnp.where(allowed, both[0] - stats[n : n + 1], MASKED))
                d_scores = weights * (both[1] - stats[many + n : many + n + 1])
                return d_scores.astype(jnp.bfloat16), weights.astype(jnp.bfloat16)

            turned = [(query[block, c].T, grad[of, part, c].T) for c in cols]

            def gather(n, soft):
                side = slice(n % 2 * HEAD, (n % 2 + 1) * HEAD)
                q, g = turned[n // 2]
                return carry[n][0] + dot_last(q[side], soft[0]), carry[n][1] + dot_last(g[side], soft[1])

            return skewed(many, score, soften, gather)

        zero = jnp.zeros((HEAD, tile), jnp.float32)
        done = lax.fori_loop(bounds[0, i], bounds[1, i], body, tuple((zero, zero) for _ in heads))
        for p, c in enumerate(cols):
            (k0, v0), (k1, v1) = done[2 * p : 2 * p + 2]
            d_keys[rows, c] = (jnp.concatenate([k0, k1], axis=0) * HEAD**-0.5).T.astype(jnp.bfloat16)
            d_values[rows, c] = jnp.concatenate([v0, v1], axis=0).T.astype(jnp.bfloat16)


def key_grad(bounds, keys, values, query, grads, first, last, tile, step):
    wide, width = query.shape
    tokens = wide // (2 * REACH + 1)
    own = pl.BlockSpec((tokens, width), lambda p, b: (REACH, 0))
    return pl.pallas_call(
        functools.partial(key_grad_kernel, tile, step),
        grid_spec=pltpu.PrefetchScalarGridSpec(
            num_scalar_prefetch=1,
            grid=(1,),
            in_specs=[own, own, whole(wide, width)]
            + [whole(1, wide)] * 2
            + [pl.BlockSpec(memory_space=pl.ANY)] * (2 * REACH + 1),
            out_specs=[whole(tokens, width)] * 2,
            scratch_shapes=[
                pltpu.VMEM((2 * REACH + 1,) + grads[0].shape, jnp.bfloat16), pltpu.SemaphoreType.DMA((2 * REACH + 1,))
            ],
        ),
        out_shape=[jax.ShapeDtypeStruct((tokens, width), jnp.bfloat16)] * 2,
        compiler_params=VMEM,
        cost_estimate=cost(4),
        name="key_grad",
    )(bounds, keys, values, query, first, last, *grads)


eps_norm = 1e-06
AXES = ("items", "rows")


NAMES = (
    "query_proj", "key_proj", "value_proj", "query_bias", "value_bias", "output_proj", "output_bias", "attn_gain",
    "attn_shift", "hidden_proj", "hidden_bias", "return_proj", "return_bias", "final_gain", "final_shift",
)


def dot_rows(matrix, factor):
    return lax.dot_general(matrix, factor, (((0,), (0,)), ((), ())), preferred_element_type=jnp.float32)


def layer_norm(hidden, norm_gain, norm_shift):
    row_mean = jnp.mean(hidden, axis=1, keepdims=True)
    centred = hidden - row_mean
    row_var = jnp.mean(centred * centred, axis=1, keepdims=True)
    return centred * lax.rsqrt(row_var + eps_norm) * norm_gain + norm_shift


def shifted(value, by):
    peers = lax.axis_size("rows")
    pairs = [(i, i + by) for i in range(peers) if 0 <= i + by < peers]
    return lax.ppermute(value, "rows", pairs)


def halo(value):
    return [value if d == 0 else shifted(value, -d) for d in range(-REACH, REACH + 1)]


def in_thirds(value, width):
    high = lax.reduce_precision(value, 8, 7)
    middle = lax.reduce_precision(value - high, 8, 7)
    pieces = jnp.concatenate([high, middle, value - high - middle], axis=1)
    return jnp.pad(pieces, ((0, 0), (0, width - pieces.shape[1]))).astype(jnp.bfloat16)


def item_tables(lengths, position, rows_dev, tile, step):
    ends = jnp.cumsum(lengths, dtype=jnp.int32)
    wide = (2 * REACH + 1) * rows_dev
    base = position - REACH * rows_dev

    def item_of(places):
        low = jnp.max(jnp.where(ends[None, :] <= places[:, None], ends[None, :], 0), axis=1)
        high = jnp.min(jnp.where(ends[None, :] > places[:, None], ends[None, :], ends[-1]), axis=1)
        return low - base, high - base

    places = base + jnp.arange(wide, dtype=jnp.int32)
    first, last = item_of(places)
    inside = (places >= 0) & (places < ends[-1])
    first, last = jnp.where(inside, first, wide), jnp.where(inside, last, -1)
    starts = position + jnp.arange(0, rows_dev, tile, dtype=jnp.int32)
    bounds = jnp.stack([item_of(starts)[0] // step, (item_of(starts + tile - 1)[1] + step - 1) // step])
    return first[None, :], last[None, :], jnp.clip(bounds, 0, wide // step).astype(jnp.int32)


TILE, STEP, GROUP = 256, 256, 12


def per_device(mesh_shape, tokens, *given):
    names = NAMES
    part = dict(zip(names, given[:15]))
    item_lengths, out_grad = given[15:]
    matrices = ["query_proj", "key_proj", "value_proj", "output_proj", "hidden_proj", "return_proj"]
    vectors = [n for n in names if n not in matrices]
    ndev = mesh_shape["items"] * mesh_shape["rows"]
    rows_dev, width = tokens.shape
    aligned = all(part[n].shape[0] % 8 == 0 for n in matrices) and all(part[n].shape[0] <= 128 for n in vectors)
    sizes = [part[n].shape[0] for n in vectors]
    used = sum(sizes)
    padded = -(-used // 1024) * 1024
    W = {}
    if aligned:
        got = gather_all(mesh_shape, tokens, [part[n] for n in matrices], [part[n] for n in vectors])
        wholes = [g.reshape((-1,) + g.shape[2:]) for g in got[: len(matrices)]]
        W.update(zip(vectors, (g[0] for g in got[len(matrices) : -3])))
        query_wide, keys_wide, values_wide = got[-3:]
    else:
        wholes = [lax.all_gather(part[n], AXES, axis=0, tiled=True) for n in matrices]
        flat = lax.all_gather(jnp.concatenate([part[n] for n in vectors]), AXES, axis=0, tiled=False)
        at = 0
        for n, size in zip(vectors, sizes):
            W[n] = flat[:, at : at + size].reshape(-1).astype(jnp.float32)
            at += size
        window = jnp.concatenate(halo(tokens))
        query_wide = (dot_plain(window, wholes[0]) + W["query_bias"]).astype(jnp.bfloat16)
        keys_wide = dot_plain(window, wholes[1]).astype(jnp.bfloat16)
        values_wide = (dot_plain(window, wholes[2]) + W["value_bias"]).astype(jnp.bfloat16)
    W.update(zip(matrices, wholes))

    position = lax.axis_index("rows") * rows_dev
    first, last, bounds = item_tables(item_lengths[0], position, rows_dev, TILE, STEP)
    own = slice(REACH * rows_dev, (REACH + 1) * rows_dev)
    own_items = first[:, own], last[:, own]

    attended, attended_full, logsum = attend(
        bounds, query_wide, keys_wide, values_wide, *own_items, TILE, STEP, GROUP
    )

    mixed = tokens.astype(jnp.float32) + (dot_plain(attended, W["output_proj"]) + W["output_bias"])
    normed, attn_back = jax.vjp(layer_norm, mixed, W["attn_gain"], W["attn_shift"])
    normed_low = normed.astype(jnp.bfloat16)
    hidden_pre = dot_plain(normed_low, W["hidden_proj"]) + W["hidden_bias"]
    cdf = 0.5 * (1.0 + lax.erf(hidden_pre * (0.5**0.5)))
    active = (hidden_pre * cdf).astype(jnp.bfloat16)
    slope = cdf + hidden_pre * jnp.exp(-0.5 * hidden_pre * hidden_pre) * 0.3989422804014327
    second = normed + (dot_plain(active, W["return_proj"]) + W["return_bias"])
    result, final_back = jax.vjp(layer_norm, second, W["final_gain"], W["final_shift"])

    grads = {}
    d_second, grads["final_gain"], grads["final_shift"] = final_back(out_grad.astype(jnp.float32))
    d_ffn = d_second.astype(jnp.bfloat16)
    grads["return_bias"] = jnp.sum(d_ffn.astype(jnp.float32), axis=0)
    d_hidden = (dot_last(d_ffn, W["return_proj"]) * slope).astype(jnp.bfloat16)
    grads["hidden_bias"] = jnp.sum(d_hidden.astype(jnp.float32), axis=0)
    d_normed = dot_last(d_hidden, W["hidden_proj"]) + d_second
    d_mixed, grads["attn_gain"], grads["attn_shift"] = attn_back(d_normed)
    d_branch = d_mixed.astype(jnp.bfloat16)
    grads["output_bias"] = jnp.sum(d_branch.astype(jnp.float32), axis=0)
    d_attended = dot_last(d_branch, W["output_proj"]).astype(jnp.bfloat16)

    lanes = jnp.arange(width, dtype=jnp.int32)[None, :] // HEAD == jnp.arange(16, dtype=jnp.int32)[:, None]
    product = d_attended.astype(jnp.float32) * attended_full
    lanes = lanes.astype(jnp.float32)
    highest = lax.Precision.HIGHEST
    centre = lax.dot_general(lanes, product, (((1,), (1,)), ((), ())), precision=highest)[:H, None]
    stats = jnp.concatenate([logsum[:, 0], centre[:, 0]]).T
    grad_blocks = halo(jnp.concatenate([d_attended, in_thirds(stats, PAIR)], axis=1))
    grads["return_proj"] = dot_rows(active, d_ffn)
    grads["hidden_proj"] = dot_rows(normed_low, d_hidden)
    grads["output_proj"] = dot_rows(attended, d_branch)
    d_query = query_grad(
        bounds, query_wide, d_attended, keys_wide, values_wide, logsum, centre, *own_items, TILE, STEP, GROUP
    )
    d_keys, d_values = key_grad(bounds, keys_wide, values_wide, query_wide, grad_blocks, first, last, TILE, STEP)
    grads["query_proj"] = dot_rows(tokens, d_query)
    grads["key_proj"] = dot_rows(tokens, d_keys)
    grads["value_proj"] = dot_rows(tokens, d_values)
    grads["query_bias"] = jnp.sum(d_query.astype(jnp.float32), axis=0)
    grads["value_bias"] = jnp.sum(d_values.astype(jnp.float32), axis=0)
    tokens_grad = (
        d_mixed
        + dot_last(d_query, W["query_proj"])
        + dot_last(d_keys, W["key_proj"])
        + dot_last(d_values, W["value_proj"])
    )

    rows_of = jnp.concatenate([grads[n].reshape(ndev, size) for n, size in zip(vectors, sizes)], axis=1)
    rows_of = jnp.pad(rows_of, ((0, 0), (0, padded - used))).reshape(ndev, 8, padded // 8)
    low = [grads[n].astype(jnp.bfloat16).reshape((ndev, -1) + grads[n].shape[1:]) for n in matrices]
    if aligned:
        height = min(g.shape[1] for g in low)
        sums = scatter_all(mesh_shape, low + [rows_of], [(height, width)] * len(low) + [rows_of.shape[1:]])
    else:
        sums = [lax.psum_scatter(g, AXES, scatter_dimension=0, tiled=True)[0] for g in low + [rows_of]]
    total = {n: s.astype(jnp.float32) for n, s in zip(matrices, sums)}
    line = sums[-1].reshape(padded)
    at = 0
    for n, size in zip(vectors, sizes):
        total[n] = line[at : at + size]
        at += size
    return (result.astype(jnp.bfloat16), tokens_grad) + tuple(total[n] for n in names)


def solution(mesh):
    both = P(AXES)
    return jax.shard_map(
        functools.partial(per_device, dict(mesh.shape)),
        mesh=mesh,
        in_specs=(both,) * 16 + (P("items"), both),
        out_specs=(both,) * 17,
        check_vma=False,
    )
```

```python
import functools
import jax
import jax.numpy as jnp
from jax import lax
from jax.experimental import pallas as pl
from jax.experimental.pallas import tpu as pltpu

from jax.sharding import PartitionSpec as P

MESH = pl.DeviceIdType.MESH
REACH = 2


def split_rows(rows):
    inner = 1
    while (2 * inner) ** 2 <= rows:
        inner *= 2
    return rows // inner, inner


def place(nz, ny):
    item, row = lax.axis_index("items"), lax.axis_index("rows")
    return item // 2, item % 2, row // ny, row % ny


def near(z, step, nz):
    way = 1 - 2 * (z // ((nz + 1) // 2))
    return lax.rem(z + way * step + nz * 2, nz)


def spread_row(tiles, n, size):
    devices = tiles.shape[0]
    column = lax.broadcasted_iota(jnp.int32, (1, devices * size), 1).astype(jnp.float32)
    owner = jnp.floor((column + 0.5) / size)
    lane = lax.broadcasted_iota(jnp.int32, (tiles.shape[2], 1), 0).astype(jnp.float32)
    pick = (column - owner * size == lane).astype(jnp.float32).astype(jnp.bfloat16)
    spread = jnp.dot(tiles[:, n, :].astype(jnp.bfloat16), pick, preferred_element_type=jnp.float32)
    device = lax.broadcasted_iota(jnp.int32, (devices, 1), 0).astype(jnp.float32)
    return jnp.sum(jnp.where(owner == device, spread, 0.0), axis=0, keepdims=True)


def gather_kernel(na, nz, ny, sizes, *refs):
    weights = 6
    count = weights + 1
    tokens = refs[0]
    mine = list(refs[1 : 1 + weights])
    lines = refs[1 + weights : 1 + weights + len(sizes)]
    refs = refs[1 + weights + len(sizes) :]
    full = list(refs[:weights])
    rows_out = refs[weights : weights + len(sizes)]
    wide = refs[weights + len(sizes)]
    (
        packed, tiles, window, matrix, bias, made, out_sem, load_sem, halo_send, halo_recv, local_sem,
        s1, r1, s2, r2, s3, r3, s4, r4,
    ) = refs[weights + len(sizes) + 1 :]
    mine.append(packed)
    full.append(tiles)
    packed[...] = jnp.zeros_like(packed)
    for n, line in enumerate(lines):
        packed[n : n + 1, : line.shape[1]] = line[...].astype(jnp.float32)

    a, c, z, y = place(nz, ny)
    rows = nz * ny
    row = z * ny + y
    item = a * 2 + c

    def slot(a_, z_, y_):
        return (a_ * 2 + c) * rows + z_ * ny + y_

    barrier = pltpu.get_barrier_semaphore()

    def greet(i_, r_):
        pl.semaphore_signal(barrier, inc=1, device_id=(i_, r_), device_id_type=MESH)

    for d in range(1, nz):
        greet(item, near(z, d, nz) * ny + y)
    for d in range(1, ny):
        greet(item, z * ny + lax.rem(y + d, ny))
    for d in range(1, na):
        greet(lax.rem(a + d, na) * 2 + c, row)
    greet(a * 2 + 1 - c, row)
    for d in range(-REACH, REACH + 1):
        if d != 0:
            greet(item, lax.rem(row + d + rows, rows))
    pl.semaphore_wait(barrier, nz + ny + na - 2 + 2 * REACH)

    def remote(src, dst, send, recv, i_, r_):
        return pltpu.make_async_remote_copy(
            src_ref=src, dst_ref=dst, send_sem=send, recv_sem=recv, device_id=(i_, r_), device_id_type=MESH
        )

    def arrived(part, recv):
        remote(part, part, s1.at[0, 0], recv, item, row).wait_recv()

    soon, later = (0, 1, 2, weights), (3, 4, 5)
    for group in (soon, later):
        for d in range(1, nz):
            for n in group:
                remote(
                    mine[n], full[n].at[slot(a, z, y)], s1.at[d, n], r1.at[z, n], item, near(z, d, nz) * ny + y
                ).start()
    locals_ = [pltpu.make_async_copy(mine[n], full[n].at[slot(a, z, y)], local_sem.at[n]) for n in range(count)]
    locals_.append(pltpu.make_async_copy(tokens, window.at[REACH], local_sem.at[count]))
    for copy in locals_:
        copy.start()

    def halo(d, start):
        k = d + REACH

        @pl.when((row + d >= 0) & (row + d < rows))
        def _():
            if start:
                remote(
                    tokens, window.at[REACH - d], halo_send.at[k], halo_recv.at[REACH - d], item, row + d
                ).start()
            else:
                part = window.at[k]
                arrived(part, halo_recv.at[k])

        @pl.when((row + d < 0) | (row + d >= rows))
        def _():
            copy = pltpu.make_async_copy(tokens, window.at[k], halo_recv.at[k])
            if start:
                copy.start()
            else:
                copy.wait()

    def second(step, group):
        zz = near(z, step, nz)
        for n in group:
            part = full[n].at[slot(a, zz, y)]
            if step:
                arrived(part, r1.at[zz, n])
            for d in range(1, ny):
                remote(
                    part if step else mine[n], part, s2.at[step, d, n], r2.at[zz, y, n], item, z * ny + lax.rem(y + d, ny)
                ).start()

    def third(step, group):
        zz = near(z, step, nz)
        for n in group:
            for d in range(1, ny):
                yy = lax.rem(y + d, ny)
                arrived(full[n].at[slot(a, zz, yy)], r2.at[zz, yy, n])
            if step == 0:
                locals_[n].wait()
            block = full[n].at[pl.ds(slot(a, zz, 0), ny)]
            for d in range(1, na):
                remote(
                    block, block, s3.at[step, d, n], r3.at[zz, a, n], lax.rem(a + d, na) * 2 + c, row
                ).start()

    def fourth(step, group):
        zz = near(z, step, nz)
        for e in range(na):
            aa = lax.rem(a + e, na)
            for n in group:
                block = full[n].at[pl.ds(slot(aa, zz, 0), ny)]
                if e:
                    arrived(block, r3.at[zz, aa, n])
                remote(block, block, s4.at[e, step, n], r4.at[aa, zz, n], a * 2 + 1 - c, row).start()

    def settle(group):
        for n in group:
            for e in range(na):
                for step in range(nz):
                    theirs = full[n].at[pl.ds((e * 2 + 1 - c) * rows + step * ny, ny)]
                    arrived(theirs, r4.at[e, step, n])

    loads = [
        pltpu.make_async_copy(full[n], matrix.at[n], load_sem.at[n]) for n in range(3)
    ]
    def store(block, n):
        rows_dev = tokens.shape[0]
        return pltpu.make_async_copy(
            made.at[block, n], wide.at[n, pl.ds(block * rows_dev, rows_dev)], out_sem.at[block, n]
        )

    def project(block):
        @pl.loop(0, 3)
        def _(n):
            factor = matrix[n].reshape(tokens.shape[1], tokens.shape[1])
            total = jnp.dot(window[block], factor, preferred_element_type=jnp.float32)
            made[block, n] = (total + bias[n]).astype(jnp.bfloat16)
            store(block, n).start()

    second(0, soon)
    second(0, later)
    for t in range(1, nz):
        second(t, soon)
        third(t - 1, soon)
    third(nz - 1, soon)
    third(0, later)
    for t in range(1, nz):
        second(t, later)
        third(t, later)
        fourth(t - 1, soon)
    for d in HALO_ORDER:
        halo(d, True)
    fourth(nz - 1, soon)
    fourth(0, later)
    settle(soon)
    for load in loads:
        load.start()
    for n, size in enumerate(sizes):
        rows_out[n][...] = spread_row(tiles, n, size)
    bias[0] = rows_out[0][...]
    bias[1] = jnp.zeros_like(bias[1])
    bias[2] = rows_out[1][...]
    fourth(1, later)
    locals_[count].wait()
    for load in loads:
        load.wait()
    project(REACH)
    for t in range(2, nz - 1):
        fourth(t, later)
    for k, d in enumerate(HALO_ORDER):
        halo(d, False)
        project(REACH + d)
        if k == 1:
            fourth(nz - 1, later)
    settle(later)

    for n in range(count):
        for step in range(nz):
            part = full[n].at[slot(a, z, y)]
            if step:
                remote(mine[n], part, s1.at[step, n], r1.at[z, n], item, row).wait_send()
            for d in range(1, ny):
                remote(part, part, s2.at[step, d, n], r2.at[z, y, n], item, row).wait_send()
            block = full[n].at[pl.ds(slot(a, z, 0), ny)]
            for d in range(1, na):
                remote(block, block, s3.at[step, d, n], r3.at[z, a, n], item, row).wait_send()
            for e in range(na):
                remote(block, block, s4.at[e, step, n], r4.at[0, 0, n], item, row).wait_send()
    for d in HALO_ORDER:

        @pl.when((row + d >= 0) & (row + d < rows))
        def _():
            remote(
                tokens, window.at[REACH - d], halo_send.at[d + REACH], halo_recv.at[REACH - d], item, row
            ).wait_send()

    for block in range(2 * REACH + 1):
        for n in range(3):
            store(block, n).wait()


HALO_ORDER = (1, -1, 2, -2)


def gather_all(mesh_shape, tokens, shards, vectors):
    na = mesh_shape["items"] // 2
    nz, ny = split_rows(mesh_shape["rows"])
    ndev = mesh_shape["items"] * mesh_shape["rows"]
    count = len(shards) + 1
    rows_dev, width = tokens.shape
    blocks = 2 * REACH + 1
    dma = pltpu.SemaphoreType.DMA
    packed = (-(-len(vectors) // 8) * 8, 128)
    sizes = tuple(v.shape[0] for v in vectors)
    wide = jax.ShapeDtypeStruct((3, blocks * rows_dev, width), tokens.dtype)
    hbm, vmem = pl.BlockSpec(memory_space=pl.ANY), pl.BlockSpec(memory_space=pltpu.VMEM)
    return pl.pallas_call(
        functools.partial(gather_kernel, na, nz, ny, sizes),
        out_shape=[jax.ShapeDtypeStruct((ndev,) + s.shape, s.dtype) for s in shards]
        + [jax.ShapeDtypeStruct((1, ndev * size), jnp.float32) for size in sizes]
        + [wide],
        in_specs=[vmem] * (count + len(vectors)),
        out_specs=[hbm] * len(shards) + [vmem] * len(sizes) + [hbm],
        scratch_shapes=[
            pltpu.VMEM(packed, jnp.float32),
            pltpu.VMEM((ndev,) + packed, jnp.float32),
            pltpu.VMEM((blocks,) + tokens.shape, tokens.dtype),
            pltpu.VMEM((3, ndev) + shards[0].shape, tokens.dtype),
            pltpu.VMEM((3, 1, width), jnp.float32),
            pltpu.VMEM((blocks, 3) + tokens.shape, tokens.dtype),
            dma((blocks, 3)), dma((3,)),
            dma((blocks,)), dma((blocks,)), dma((count + 1,)),
            dma((nz, count)), dma((nz, count)),
            dma((nz, ny, count)), dma((nz, ny, count)),
            dma((nz, na, count)), dma((nz, na, count)),
            dma((na, nz, count)), dma((na, nz, count)),
        ],
        compiler_params=pltpu.CompilerParams(collective_id=1, has_side_effects=True, vmem_limit_bytes=56 << 20),
        name="gather_weights",
    )(tokens, *shards, *[v[None] for v in vectors])


def scatter_kernel(na, nz, ny, *refs):
    active, d_ffn, normed, d_hidden, attended, d_branch, tokens, d_query, d_keys, d_values, lines = refs[:11]
    sum_hidden, sum_return, sum_output, sum_query, sum_key, sum_value, sum_lines = refs[11:18]
    (
        act, hid, left, right, turned, product, parts, parts_lines, low, low_lines,
        given_sem, s0, r0, s1, r1, s2, r2, s3, r3,
    ) = refs[18:]
    a, c, z, y = place(nz, ny)
    rows = nz * ny
    row = z * ny + y
    item = a * 2 + c
    devices = 2 * na * rows
    width = left.shape[2]
    height = width // devices
    blocks = hid.shape[1] // width
    many = 2 * blocks + 5
    tile = many - 1

    loads = [
        pltpu.make_async_copy(src, dst, given_sem.at[n])
        for n, (src, dst) in enumerate(
            (
                (normed, left.at[0]), (d_hidden, hid), (active, act), (d_ffn, right.at[0]), (attended, left.at[1]),
                (d_branch, right.at[1]), (tokens, left.at[2]), (d_query, right.at[2]), (d_keys, right.at[3]),
                (d_values, right.at[4]),
            )
        )
    ]
    for load in loads:
        load.start()
    for side in range(2):
        for aa in range(na):
            parts_lines[side, aa] = lines[aa, side]

    barrier = pltpu.get_barrier_semaphore()

    def greet(i_, r_):
        pl.semaphore_signal(barrier, inc=1, device_id=(i_, r_), device_id_type=MESH)

    def at_z(d):
        return lax.rem(z + d, nz) * ny + y

    def at_y(d):
        return z * ny + lax.rem(y + d, ny)

    def at_a(d):
        return lax.rem(a + d, na) * 2 + c

    for d in range(1, nz):
        greet(item, at_z(d))
    for d in range(1, ny):
        greet(item, at_y(d))
    for d in range(1, na):
        greet(at_a(d), row)
    greet(a * 2 + 1 - c, row)
    pl.semaphore_wait(barrier, nz + ny + na - 2)

    def remote(src, dst, send, recv, i_, r_):
        return pltpu.make_async_remote_copy(
            src_ref=src, dst_ref=dst, send_sem=send, recv_sem=recv, device_id=(i_, r_), device_id_type=MESH
        )

    def is_tile(k):
        return isinstance(k, int) and k == tile

    def part(k, side):
        return parts_lines.at[side] if is_tile(k) else parts.at[k, side]

    def mine(k):
        return part(k, c)

    def landing(k, which):
        return low_lines[which] if is_tile(k) else low[which].at[k]

    def core(k, aa, zz):
        return remote(
            part(k, 1 - c).at[aa, zz], landing(k, 0).at[aa, zz], s0.at[k, aa, zz], r0.at[k, aa, zz], a * 2 + 1 - c, row
        )

    def send_core(k):
        for e in range(na):
            for zz in range(nz):
                core(k, lax.rem(a + 1 + e, na), zz).start()

    def first0(k, d, zz):
        aa = lax.rem(a + d, na)
        return remote(
            mine(k).at[aa, zz], landing(k, 1).at[pl.ds((d - 1) * rows + zz * ny, ny)],
            s1.at[k, d, zz], r1.at[k, d, zz], at_a(d), row,
        )

    def first1(k, d, aa):
        return remote(
            mine(k).at[aa, :, lax.rem(y + d, ny)], landing(k, 1).at[pl.ds((d - 1) * na * nz + aa * nz, nz)],
            s1.at[k, d, aa], r1.at[k, d, aa], item, at_y(d),
        )

    def second0(k, d):
        return remote(
            mine(k).at[a, :, lax.rem(y + d, ny)], landing(k, 2).at[pl.ds((d - 1) * nz, nz)],
            s2.at[k, d], r2.at[k, d], item, at_y(d),
        )

    def second1(k, d):
        return remote(
            mine(k).at[lax.rem(a + d, na), :, y], landing(k, 2).at[pl.ds((d - 1) * nz, nz)],
            s2.at[k, d], r2.at[k, d], at_a(d), row,
        )

    def third(k, d):
        return remote(
            mine(k).at[a, lax.rem(z + d, nz), y], landing(k, 3).at[d - 1], s3.at[k, d], r3.at[k, d], item, at_z(d)
        )

    def summed(refs_):
        total = refs_[0][...].astype(jnp.float32)
        for ref in refs_[1:]:
            total = total + ref[...].astype(jnp.float32)
        return total

    def add_into(dst, others):
        dst[...] = summed([dst] + others).astype(dst.dtype)

    def stage1(k):
        for e in range(na):
            aa = lax.rem(a + 1 + e, na)
            for zz in range(nz):
                core(k, aa, zz).wait_recv()

                @pl.loop(0, ny)
                def _(yy):
                    add_into(mine(k).at[aa, zz, yy], [landing(k, 0).at[aa, zz, yy]])

                if e < na - 1:

                    @pl.when(c == 0)
                    def _():
                        first0(k, e + 1, zz).start()

        @pl.when(c == 1)
        def _():
            for d in range(1, ny):
                for aa in range(na):
                    first1(k, d, aa).start()

    def stage2(k):
        @pl.when(c == 0)
        def _():
            for zz in range(nz):
                for d in range(1, na):
                    first0(k, d, zz).wait_recv()

                @pl.loop(0, ny)
                def _(yy):
                    add_into(
                        mine(k).at[a, zz, yy], [landing(k, 1).at[(d - 1) * rows + zz * ny + yy] for d in range(1, na)]
                    )

            for d in range(1, ny):
                second0(k, d).start()

        @pl.when(c == 1)
        def _():
            for d in range(1, ny):
                for aa in range(na):
                    first1(k, d, aa).wait_recv()
            for aa in range(na):

                @pl.loop(0, nz)
                def _(zz):
                    add_into(
                        mine(k).at[aa, zz, y],
                        [landing(k, 1).at[(d - 1) * na * nz + aa * nz + zz] for d in range(1, ny)],
                    )

            for d in range(1, na):
                second1(k, d).start()

    def stage3(k):
        def rest(peers, second):
            for d in range(1, peers):
                second(k, d).wait_recv()

            @pl.loop(0, nz)
            def _(zz):
                add_into(mine(k).at[a, zz, y], [landing(k, 2).at[(d - 1) * nz + zz] for d in range(1, peers)])

        @pl.when(c == 0)
        def _():
            rest(ny, second0)

        @pl.when(c == 1)
        def _():
            rest(na, second1)

        for d in range(1, nz):
            third(k, d).start()

    def stage4(k):
        for d in range(1, nz):
            third(k, d).wait_recv()
        total = summed([mine(k).at[a, z, y]] + [landing(k, 3).at[d - 1] for d in range(1, nz)])
        if k < blocks:
            sum_hidden[:, k * width : (k + 1) * width] = total
        elif k < 2 * blocks:
            sum_return[(k - blocks) * height : (k - blocks + 1) * height] = total
        else:
            (sum_output, sum_query, sum_key, sum_value, sum_lines)[k - 2 * blocks][...] = total

    def spread(k):
        @pl.loop(0, devices)
        def _(n):
            i_, r_ = n // rows, lax.rem(n, rows)
            parts[k, lax.rem(i_, 2), i_ // 2, r_ // ny, lax.rem(r_, ny)] = product[
                pl.ds(pl.multiple_of(n * height, 8), height)
            ].astype(parts.dtype)

    def times(factor):
        product[...] = jnp.dot(turned[...], factor, preferred_element_type=jnp.float32)

    def make_hidden(first, last):
        @pl.loop(first, last)
        def _(k):
            times(hid[:, pl.ds(pl.multiple_of(k * width, width), width)])
            spread(k)
            send_core(k)

    def make_return():
        @pl.loop(0, 2 * na)
        def _(i_):
            turned[...] = act[:, pl.ds(pl.multiple_of(i_ * width, width), width)].T
            times(right[0])

            @pl.loop(0, rows)
            def _(r_):
                for k in range(blocks):
                    parts[blocks + k, lax.rem(i_, 2), i_ // 2, r_ // ny, lax.rem(r_, ny)] = product[
                        pl.ds(pl.multiple_of((r_ * blocks + k) * height, 8), height)
                    ].astype(parts.dtype)

        for k in range(blocks):
            send_core(blocks + k)

    def make_rest():
        @pl.loop(0, 4)
        def _(n):
            turned[...] = left[jnp.minimum(n + 1, 2)].T
            times(right[n + 1])
            spread(2 * blocks + n)
            send_core(2 * blocks + n)

    send_core(tile)
    loads[0].wait()
    turned[...] = left[0].T
    loads[1].wait()
    make_hidden(0, 2)
    stages = (stage1, stage2, stage3, stage4)
    for t in range(many + 3):
        for n, stage in enumerate(stages):
            if 0 <= t - n < many:
                stage(t - n)
        if t == 0:
            make_hidden(2, blocks)
        if t == 1:
            loads[2].wait()
            loads[3].wait()
            make_return()
        if t == 2:
            for load in loads[4:]:
                load.wait()
            make_rest()

    for k in range(many):
        for aa in range(na):
            for zz in range(nz):
                core(k, aa, zz).wait_send()
        for d in range(1, nz):
            third(k, d).wait_send()

        @pl.when(c == 0)
        def _():
            for d in range(1, na):
                for zz in range(nz):
                    first0(k, d, zz).wait_send()
            for d in range(1, ny):
                second0(k, d).wait_send()

        @pl.when(c == 1)
        def _():
            for d in range(1, ny):
                for aa in range(na):
                    first1(k, d, aa).wait_send()
            for d in range(1, na):
                second1(k, d).wait_send()


def scatter_all(mesh_shape, factors, lines):
    na = mesh_shape["items"] // 2
    nz, ny = split_rows(mesh_shape["rows"])
    devices = 2 * na * nz * ny
    tokens, wide = factors[0].shape
    width = factors[1].shape[1]
    height = width // devices
    blocks = wide // width
    many = 2 * blocks + 5
    dma = pltpu.SemaphoreType.DMA
    nm = max(na, ny)
    low = jnp.bfloat16
    first = max((na - 1) * nz * ny, (ny - 1) * na * nz)
    second = (nm - 1) * nz
    lands = [(na, nz, ny), (first,), (second,), (nz - 1,)]
    one, tile = (height, width), lines.shape[1:]
    f32 = lambda *shape: jax.ShapeDtypeStruct(shape, jnp.float32)
    return pl.pallas_call(
        functools.partial(scatter_kernel, na, nz, ny),
        out_shape=[f32(height, wide), f32(height * blocks, width)] + [f32(*one)] * 4 + [f32(*tile)],
        in_specs=[pl.BlockSpec(memory_space=pl.ANY)] * 10 + [pl.BlockSpec(memory_space=pltpu.VMEM)],
        out_specs=[pl.BlockSpec(memory_space=pltpu.VMEM)] * 7,
        scratch_shapes=[
            pltpu.VMEM((tokens, wide), low),
            pltpu.VMEM((tokens, wide), low),
            pltpu.VMEM((3, tokens, width), low),
            pltpu.VMEM((5, tokens, width), low),
            pltpu.VMEM((width, tokens), low),
            pltpu.VMEM((width, width), jnp.float32),
            pltpu.VMEM((many - 1, 2, na, nz, ny) + one, low),
            pltpu.VMEM((2, na, nz, ny) + tile, jnp.float32),
            [pltpu.VMEM((many - 1,) + land + one, low) for land in lands],
            [pltpu.VMEM(land + tile, jnp.float32) for land in lands],
            dma((10,)),
        ]
        + [dma((many, na, nz))] * 2
        + [dma((many, nm, max(nz, na)))] * 2
        + [dma((many, nm))] * 2
        + [dma((many, nz))] * 2,
        compiler_params=pltpu.CompilerParams(collective_id=2, has_side_effects=True, vmem_limit_bytes=63 << 20),
        name="scatter_grads",
    )(*factors, lines.reshape((na, 2, nz, ny) + tile))


H = 12
HEAD = 64
PAIR = 2 * HEAD
MASKED = -1e30


def dot_last(x, y):
    return lax.dot_general(x, y, (((1,), (1,)), ((), ())), preferred_element_type=jnp.float32)


def dot_plain(x, y):
    return jnp.dot(x, y, preferred_element_type=jnp.float32)


def one_side(block, side, scale=1.0):
    lane = lax.broadcasted_iota(jnp.int32, (1, PAIR), 1)
    keep = (lane // HEAD == side).astype(jnp.float32) * scale
    return (block.astype(jnp.float32) * keep).astype(jnp.bfloat16)


FAR = 1 << 24


def item_at(lengths, place):
    first, last, end = jnp.zeros_like(place), jnp.full_like(place, FAR), 0
    for n in range(lengths.shape[1]):
        end = end + lengths[0, n]
        first = jnp.where(end <= place, end, first)
        last = jnp.where(end > place, jnp.minimum(last, end), last)
    return first, last, end


def span(lengths, start, tile, base, step, most):
    low = item_at(lengths, start)[0] - base
    high = item_at(lengths, start + tile - 1)[1] - base
    return jnp.maximum(low, 0) // step, jnp.minimum((high + step - 1) // step, most)


def items_of(lengths, start, count):
    place = start + lax.broadcasted_iota(jnp.int32, (1, count), 1)
    first, last, end = item_at(lengths, place)
    inside = (place >= 0) & (place < end)
    return jnp.where(inside, first, FAR), jnp.where(inside, last, -1)


def allowed_pairs(first, last, base, shape):
    place = lax.broadcasted_iota(jnp.int32, shape, 0)
    return (place >= first - base) & (place < last - base)


def skewed(count, *stages):
    held = [None] * count
    for t in range(count + len(stages) - 1):
        for k, stage in enumerate(stages):
            n = t - k
            if 0 <= n < count:
                held[n] = stage(n) if k == 0 else stage(n, held[n])
    return tuple(held)


def attend_kernel(tile, step, lengths, query, keys, values, low, full, logsum):
    wide, width = keys.shape
    tokens = wide // (2 * REACH + 1)
    base = (lax.axis_index("rows") - REACH) * tokens
    start = base + REACH * tokens + pl.program_id(0) * tile
    cols = [slice(p * PAIR, (p + 1) * PAIR) for p in range(width // PAIR)]
    heads = [(c, s, one_side(query[:, c], s, HEAD**-0.5)) for c in cols for s in range(2)]
    first, last = items_of(lengths, start, tile)

    def body(j, carry):
        block = pl.ds(pl.multiple_of(j * step, step), step)
        allowed = allowed_pairs(first, last, base + j * step, (step, tile))
        turned = [values[block, c].T for c in cols]

        def score(n):
            c, s, q = heads[n]
            return jnp.where(allowed, dot_last(keys[block, c], q), MASKED)

        def soften(n, scores):
            top, total, acc = carry[n]
            peak = jnp.maximum(top, jnp.max(scores, axis=0, keepdims=True))
            lifted = jnp.exp(scores - peak)
            fade = jnp.exp(top - peak)
            return peak, total * fade + jnp.sum(lifted, axis=0, keepdims=True), fade, lifted.astype(jnp.bfloat16)

        def gather(n, soft):
            peak, total, fade, lifted = soft
            s = heads[n][1]
            return peak, total, carry[n][2] * fade + dot_plain(turned[n // 2][s * HEAD : (s + 1) * HEAD], lifted)

        return skewed(len(heads), score, soften, gather)

    empty = tuple(
        (
            jnp.full((1, tile), MASKED, jnp.float32),
            jnp.zeros((1, tile), jnp.float32),
            jnp.zeros((HEAD, tile), jnp.float32),
        )
        for _ in heads
    )
    done = lax.fori_loop(*span(lengths, start, tile, base, step, wide // step), body, empty)
    for p, c in enumerate(cols):
        (top0, total0, acc0), (top1, total1, acc1) = done[2 * p : 2 * p + 2]
        result = jnp.concatenate([acc0 / total0, acc1 / total1], axis=0).T
        low[:, c] = result.astype(jnp.bfloat16)
        full[:, c] = result
        logsum[2 * p] = top0 + jnp.log(total0)
        logsum[2 * p + 1] = top1 + jnp.log(total1)


def own_tile(n, tile, tiles, width):
    return pl.BlockSpec((None, tile, width), lambda i, b: (n, REACH * tiles + i, 0))


def window_of(n, wide, width):
    return pl.BlockSpec((None, wide, width), lambda i, b: (n, 0, 0))


def tile_of(tile, width):
    return pl.BlockSpec((tile, width), lambda i, b: (i, 0))


def lines(tile):
    return pl.BlockSpec((H, 1, tile), lambda i, b: (0, 0, i))


def cost(matmuls):
    return pl.CostEstimate(flops=matmuls * 2 * H * HEAD * 512 * 1536, bytes_accessed=12 << 20, transcendentals=0)


VMEM = pltpu.CompilerParams(vmem_limit_bytes=56 << 20)


def attend(lengths, projected, tile, step):
    _, wide, width = projected.shape
    tokens = wide // (2 * REACH + 1)
    tiles = tokens // tile
    return pl.pallas_call(
        functools.partial(attend_kernel, tile, step),
        grid_spec=pltpu.PrefetchScalarGridSpec(
            num_scalar_prefetch=1,
            grid=(tiles,),
            in_specs=[own_tile(0, tile, tiles, width), window_of(1, wide, width), window_of(2, wide, width)],
            out_specs=[tile_of(tile, width), tile_of(tile, width), lines(tile)],
        ),
        out_shape=[
            jax.ShapeDtypeStruct((tokens, width), jnp.bfloat16),
            jax.ShapeDtypeStruct((tokens, width), jnp.float32),
            jax.ShapeDtypeStruct((H, 1, tokens), jnp.float32),
        ],
        compiler_params=VMEM,
        cost_estimate=cost(2),
        name="attend",
    )(lengths, projected, projected, projected)


def query_grad_kernel(tile, step, lengths, query, grad, keys, values, logsum, centre, out):
    wide, width = keys.shape
    tokens = wide // (2 * REACH + 1)
    base = (lax.axis_index("rows") - REACH) * tokens
    start = base + REACH * tokens + pl.program_id(0) * tile
    cols = [slice(p * PAIR, (p + 1) * PAIR) for p in range(width // PAIR)]
    heads = [
        (c, s, one_side(query[:, c], s, HEAD**-0.5), one_side(grad[:, c], s), logsum[2 * p + s], centre[2 * p + s])
        for p, c in enumerate(cols)
        for s in range(2)
    ]
    first, last = items_of(lengths, start, tile)

    def body(j, carry):
        block = pl.ds(pl.multiple_of(j * step, step), step)
        allowed = allowed_pairs(first, last, base + j * step, (step, tile))
        turned = [keys[block, c].T for c in cols]

        def score(n):
            c, s, q, g, top, mid = heads[n]
            return dot_last(keys[block, c], q), dot_last(values[block, c], g)

        def soften(n, both):
            top, mid = heads[n][4:]
            weights = jnp.exp(jnp.where(allowed, both[0] - top, MASKED))
            return (weights * (both[1] - mid)).astype(jnp.bfloat16)

        def gather(n, d_scores):
            s = heads[n][1]
            return carry[n] + dot_plain(turned[n // 2][s * HEAD : (s + 1) * HEAD], d_scores)

        return skewed(len(heads), score, soften, gather)

    empty = tuple(jnp.zeros((HEAD, tile), jnp.float32) for _ in heads)
    done = lax.fori_loop(*span(lengths, start, tile, base, step, wide // step), body, empty)
    for p, c in enumerate(cols):
        both = jnp.concatenate(done[2 * p : 2 * p + 2], axis=0) * HEAD**-0.5
        out[:, c] = both.T.astype(jnp.bfloat16)


def query_grad(lengths, projected, grad, logsum, centre, tile, step):
    _, wide, width = projected.shape
    tokens = grad.shape[0]
    tiles = tokens // tile
    return pl.pallas_call(
        functools.partial(query_grad_kernel, tile, step),
        grid_spec=pltpu.PrefetchScalarGridSpec(
            num_scalar_prefetch=1,
            grid=(tiles,),
            in_specs=[
                own_tile(0, tile, tiles, width), tile_of(tile, width),
                window_of(1, wide, width), window_of(2, wide, width), lines(tile), lines(tile),
            ],
            out_specs=tile_of(tile, width),
        ),
        out_shape=jax.ShapeDtypeStruct((tokens, width), jnp.bfloat16),
        compiler_params=VMEM,
        cost_estimate=cost(3),
        name="query_grad",
    )(lengths, projected, grad, projected, projected, logsum, centre)


def key_grad_kernel(tile, step, lengths, keys, values, query, *refs):
    blocks = refs[: 2 * REACH + 1]
    d_keys, d_values, grad, arrived = refs[2 * REACH + 1 :]
    wide, width = query.shape
    tokens = wide // (2 * REACH + 1)
    base = (lax.axis_index("rows") - REACH) * tokens
    start = base + REACH * tokens + pl.program_id(0) * tile

    @pl.when(pl.program_id(0) == 0)
    def _():
        copies = [pltpu.make_async_copy(b, grad.at[k], arrived.at[k]) for k, b in enumerate(blocks)]
        for copy in copies:
            copy.start()
        for copy in copies:
            copy.wait()

    cols = [slice(p * PAIR, (p + 1) * PAIR) for p in range(width // PAIR)]
    heads = [(c, one_side(keys[:, c], s, HEAD**-0.5), one_side(values[:, c], s)) for c in cols for s in range(2)]
    many = len(heads)

    def body(j, carry):
        block = pl.ds(pl.multiple_of(j * step, step), step)
        of = j * step // tokens
        part = pl.ds(pl.multiple_of(j * step - of * tokens, step), step)
        first, last = items_of(lengths, base + j * step, step)
        allowed = allowed_pairs(first, last, start, (tile, step))
        stats = grad[of, part, width:].astype(jnp.float32).T
        stats = stats[: 2 * many] + stats[2 * many : 4 * many] + stats[4 * many : 6 * many]

        def score(n):
            c, k, v = heads[n]
            return dot_last(k, query[block, c]), dot_last(v, grad[of, part, c])

        def soften(n, both):
            weights = jnp.exp(jnp.where(allowed, both[0] - stats[n : n + 1], MASKED))
            d_scores = weights * (both[1] - stats[many + n : many + n + 1])
            return d_scores.astype(jnp.bfloat16), weights.astype(jnp.bfloat16)

        turned = [(query[block, c].T, grad[of, part, c].T) for c in cols]

        def gather(n, soft):
            side = slice(n % 2 * HEAD, (n % 2 + 1) * HEAD)
            q, g = turned[n // 2]
            return carry[n][0] + dot_last(q[side], soft[0]), carry[n][1] + dot_last(g[side], soft[1])

        return skewed(many, score, soften, gather)

    zero = jnp.zeros((HEAD, tile), jnp.float32)
    limits = span(lengths, start, tile, base, step, wide // step)
    done = lax.fori_loop(*limits, body, tuple((zero, zero) for _ in heads))
    for p, c in enumerate(cols):
        (k0, v0), (k1, v1) = done[2 * p : 2 * p + 2]
        d_keys[:, c] = (jnp.concatenate([k0, k1], axis=0) * HEAD**-0.5).T.astype(jnp.bfloat16)
        d_values[:, c] = jnp.concatenate([v0, v1], axis=0).T.astype(jnp.bfloat16)


def key_grad(lengths, projected, grads, tile, step):
    _, wide, width = projected.shape
    tokens = wide // (2 * REACH + 1)
    tiles = tokens // tile
    return pl.pallas_call(
        functools.partial(key_grad_kernel, tile, step),
        grid_spec=pltpu.PrefetchScalarGridSpec(
            num_scalar_prefetch=1,
            grid=(tiles,),
            in_specs=[own_tile(1, tile, tiles, width), own_tile(2, tile, tiles, width), window_of(0, wide, width)]
            + [pl.BlockSpec(memory_space=pl.ANY)] * (2 * REACH + 1),
            out_specs=[tile_of(tile, width)] * 2,
            scratch_shapes=[
                pltpu.VMEM((2 * REACH + 1,) + grads[0].shape, jnp.bfloat16), pltpu.SemaphoreType.DMA((2 * REACH + 1,))
            ],
        ),
        out_shape=[jax.ShapeDtypeStruct((tokens, width), jnp.bfloat16)] * 2,
        compiler_params=VMEM,
        cost_estimate=cost(4),
        name="key_grad",
    )(lengths, projected, projected, projected, *grads)


eps_norm = 1e-06
AXES = ("items", "rows")


NAMES = (
    "query_proj", "key_proj", "value_proj", "query_bias", "value_bias", "output_proj", "output_bias", "attn_gain",
    "attn_shift", "hidden_proj", "hidden_bias", "return_proj", "return_bias", "final_gain", "final_shift",
)


def dot_rows(matrix, factor):
    return lax.dot_general(matrix, factor, (((0,), (0,)), ((), ())), preferred_element_type=jnp.float32)


def layer_norm(hidden, norm_gain, norm_shift):
    row_mean = jnp.mean(hidden, axis=1, keepdims=True)
    centred = hidden - row_mean
    row_var = jnp.mean(centred * centred, axis=1, keepdims=True)
    return centred * lax.rsqrt(row_var + eps_norm) * norm_gain + norm_shift


def shifted(value, by):
    peers = lax.axis_size("rows")
    pairs = [(i, i + by) for i in range(peers) if 0 <= i + by < peers]
    return lax.ppermute(value, "rows", pairs)


def halo(value):
    return [value if d == 0 else shifted(value, -d) for d in range(-REACH, REACH + 1)]


def in_thirds(value, width):
    high = lax.reduce_precision(value, 8, 7)
    middle = lax.reduce_precision(value - high, 8, 7)
    pieces = jnp.concatenate([high, middle, value - high - middle], axis=1)
    return jnp.pad(pieces, ((0, 0), (0, width - pieces.shape[1]))).astype(jnp.bfloat16)


TILE, STEP = 256, 256


def per_device(mesh_shape, tokens, *given):
    names = NAMES
    part = dict(zip(names, given[:15]))
    item_lengths, out_grad = given[15:]
    matrices = ["query_proj", "key_proj", "value_proj", "output_proj", "hidden_proj", "return_proj"]
    vectors = [n for n in names if n not in matrices]
    ndev = mesh_shape["items"] * mesh_shape["rows"]
    rows_dev, width = tokens.shape
    aligned = all(part[n].shape[0] % 8 == 0 for n in matrices) and all(part[n].shape[0] <= 128 for n in vectors)
    sizes = [part[n].shape[0] for n in vectors]
    used = sum(sizes)
    padded = -(-used // 1024) * 1024
    W = {}
    if aligned:
        got = gather_all(mesh_shape, tokens, [part[n] for n in matrices], [part[n] for n in vectors])
        wholes = [g.reshape((-1,) + g.shape[2:]) for g in got[: len(matrices)]]
        W.update(zip(vectors, got[len(matrices) : -1]))
        projected = got[-1]
    else:
        wholes = [lax.all_gather(part[n], AXES, axis=0, tiled=True) for n in matrices]
        flat = lax.all_gather(jnp.concatenate([part[n] for n in vectors]), AXES, axis=0, tiled=False)
        at = 0
        for n, size in zip(vectors, sizes):
            W[n] = flat[:, at : at + size].reshape(1, -1).astype(jnp.float32)
            at += size
        window = jnp.concatenate(halo(tokens))
        query_wide = (dot_plain(window, wholes[0]) + W["query_bias"]).astype(jnp.bfloat16)
        keys_wide = dot_plain(window, wholes[1]).astype(jnp.bfloat16)
        values_wide = (dot_plain(window, wholes[2]) + W["value_bias"]).astype(jnp.bfloat16)
        projected = jnp.stack([query_wide, keys_wide, values_wide])
    W.update(zip(matrices, wholes))

    attended, attended_full, logsum = attend(item_lengths, projected, TILE, STEP)

    mixed = tokens.astype(jnp.float32) + (dot_plain(attended, W["output_proj"]) + W["output_bias"])
    normed, attn_back = jax.vjp(layer_norm, mixed, W["attn_gain"], W["attn_shift"])
    normed_low = normed.astype(jnp.bfloat16)
    hidden_pre = dot_plain(normed_low, W["hidden_proj"]) + W["hidden_bias"]
    cdf = 0.5 * (1.0 + lax.erf(hidden_pre * (0.5**0.5)))
    active = (hidden_pre * cdf).astype(jnp.bfloat16)
    slope = cdf + hidden_pre * jnp.exp(-0.5 * hidden_pre * hidden_pre) * 0.3989422804014327
    second = normed + (dot_plain(active, W["return_proj"]) + W["return_bias"])
    result, final_back = jax.vjp(layer_norm, second, W["final_gain"], W["final_shift"])

    grads = {}
    d_second, grads["final_gain"], grads["final_shift"] = final_back(out_grad.astype(jnp.float32))
    d_ffn = d_second.astype(jnp.bfloat16)
    grads["return_bias"] = jnp.sum(d_ffn.astype(jnp.float32), axis=0)
    d_hidden = (dot_last(d_ffn, W["return_proj"]) * slope).astype(jnp.bfloat16)
    grads["hidden_bias"] = jnp.sum(d_hidden.astype(jnp.float32), axis=0)
    d_normed = dot_last(d_hidden, W["hidden_proj"]) + d_second
    d_mixed, grads["attn_gain"], grads["attn_shift"] = attn_back(d_normed)
    d_branch = d_mixed.astype(jnp.bfloat16)
    grads["output_bias"] = jnp.sum(d_branch.astype(jnp.float32), axis=0)
    d_attended = dot_last(d_branch, W["output_proj"]).astype(jnp.bfloat16)

    lanes = jnp.arange(width, dtype=jnp.int32)[None, :] // HEAD == jnp.arange(16, dtype=jnp.int32)[:, None]
    product = d_attended.astype(jnp.float32) * attended_full
    lanes = lanes.astype(jnp.float32)
    highest = lax.Precision.HIGHEST
    centre = lax.dot_general(lanes, product, (((1,), (1,)), ((), ())), precision=highest)[:H, None]
    stats = jnp.concatenate([logsum[:, 0], centre[:, 0]]).T
    grad_blocks = halo(jnp.concatenate([d_attended, in_thirds(stats, PAIR)], axis=1))
    d_query = query_grad(item_lengths, projected, d_attended, logsum, centre, TILE, STEP)
    d_keys, d_values = key_grad(item_lengths, projected, grad_blocks, TILE, STEP)
    grads["query_bias"] = jnp.sum(d_query.astype(jnp.float32), axis=0)
    grads["value_bias"] = jnp.sum(d_values.astype(jnp.float32), axis=0)
    tokens_grad = (
        d_mixed
        + dot_last(d_query, W["query_proj"])
        + dot_last(d_keys, W["key_proj"])
        + dot_last(d_values, W["value_proj"])
    )

    rows_of = jnp.concatenate([grads[n].reshape(ndev, size) for n, size in zip(vectors, sizes)], axis=1)
    rows_of = jnp.pad(rows_of, ((0, 0), (0, padded - used))).reshape(ndev, 8, padded // 8)
    factors = (
        active, d_ffn, normed_low, d_hidden, attended, d_branch, tokens, d_query, d_keys, d_values
    )
    order = ("hidden_proj", "return_proj", "output_proj", "query_proj", "key_proj", "value_proj")
    if aligned:
        sums = scatter_all(mesh_shape, factors, rows_of)
    else:
        pairs = ((2, 3), (0, 1), (4, 5), (6, 7), (6, 8), (6, 9))
        low = [dot_rows(factors[i], factors[j]).astype(jnp.bfloat16) for i, j in pairs]
        low = [g.reshape((ndev, -1) + g.shape[1:]) for g in low] + [rows_of]
        sums = [lax.psum_scatter(g, AXES, scatter_dimension=0, tiled=True)[0] for g in low]
    total = {n: s.astype(jnp.float32) for n, s in zip(order, sums)}
    line = sums[-1].reshape(padded)
    at = 0
    for n, size in zip(vectors, sizes):
        total[n] = line[at : at + size]
        at += size
    return (result.astype(jnp.bfloat16), tokens_grad) + tuple(total[n] for n in names)


def solution(mesh):
    both = P(AXES)
    return jax.shard_map(
        functools.partial(per_device, dict(mesh.shape)),
        mesh=mesh,
        in_specs=(both,) * 16 + (P("items"), both),
        out_specs=(both,) * 17,
        check_vma=False,
    )
```

```python
import functools
import jax
import jax.numpy as jnp
from jax import lax
from jax.experimental import pallas as pl
from jax.experimental.pallas import tpu as pltpu

from jax.sharding import PartitionSpec as P

MESH = pl.DeviceIdType.MESH
REACH = 2


def split_rows(rows):
    inner = 1
    while (2 * inner) ** 2 <= rows:
        inner *= 2
    return rows // inner, inner


def place(nz, ny):
    item, row = lax.axis_index("items"), lax.axis_index("rows")
    return item // 2, item % 2, row // ny, row % ny


def near(z, step, nz):
    way = 1 - 2 * (z // ((nz + 1) // 2))
    return lax.rem(z + way * step + nz * 2, nz)


def spread_row(tiles, n, size):
    devices = tiles.shape[0]
    column = lax.broadcasted_iota(jnp.int32, (1, devices * size), 1).astype(jnp.float32)
    owner = jnp.floor((column + 0.5) / size)
    lane = lax.broadcasted_iota(jnp.int32, (tiles.shape[2], 1), 0).astype(jnp.float32)
    pick = (column - owner * size == lane).astype(jnp.float32).astype(jnp.bfloat16)
    spread = jnp.dot(tiles[:, n, :].astype(jnp.bfloat16), pick, preferred_element_type=jnp.float32)
    device = lax.broadcasted_iota(jnp.int32, (devices, 1), 0).astype(jnp.float32)
    return jnp.sum(jnp.where(owner == device, spread, 0.0), axis=0, keepdims=True)


def gather_kernel(na, nz, ny, sizes, *refs):
    weights = 6
    count = weights + 1
    tokens = refs[0]
    mine = list(refs[1 : 1 + weights])
    lines = refs[1 + weights : 1 + weights + len(sizes)]
    refs = refs[1 + weights + len(sizes) :]
    full = list(refs[:weights])
    rows_out, last_out, wide = refs[weights : weights + 3]
    (
        packed, tiles, window, matrix, bias, made, out_sem, load_sem, halo_send, halo_recv, local_sem,
        s1, r1, s2, r2, s3, r3, s4, r4,
    ) = refs[weights + 3 :]
    mine.append(packed)
    full.append(tiles)
    packed[...] = jnp.zeros_like(packed)
    for n, line in enumerate(lines):
        packed[n : n + 1, : line.shape[1]] = line[...].astype(jnp.float32)

    a, c, z, y = place(nz, ny)
    rows = nz * ny
    row = z * ny + y
    item = a * 2 + c

    def slot(a_, z_, y_):
        return (a_ * 2 + c) * rows + z_ * ny + y_

    barrier = pltpu.get_barrier_semaphore()

    def greet(i_, r_):
        pl.semaphore_signal(barrier, inc=1, device_id=(i_, r_), device_id_type=MESH)

    for d in range(1, nz):
        greet(item, near(z, d, nz) * ny + y)
    for d in range(1, ny):
        greet(item, z * ny + lax.rem(y + d, ny))
    for d in range(1, na):
        greet(lax.rem(a + d, na) * 2 + c, row)
    greet(a * 2 + 1 - c, row)
    for d in range(-REACH, REACH + 1):
        if d != 0:
            greet(item, lax.rem(row + d + rows, rows))
    pl.semaphore_wait(barrier, nz + ny + na - 2 + 2 * REACH)

    def remote(src, dst, send, recv, i_, r_):
        return pltpu.make_async_remote_copy(
            src_ref=src, dst_ref=dst, send_sem=send, recv_sem=recv, device_id=(i_, r_), device_id_type=MESH
        )

    def arrived(part, recv):
        remote(part, part, s1.at[0, 0], recv, item, row).wait_recv()

    soon, later = (0, 1, 2, weights), (3, 4, 5)
    for group in (soon, later):
        for d in range(1, nz):
            for n in group:
                remote(
                    mine[n], full[n].at[slot(a, z, y)], s1.at[d, n], r1.at[z, n], item, near(z, d, nz) * ny + y
                ).start()
    locals_ = [pltpu.make_async_copy(mine[n], full[n].at[slot(a, z, y)], local_sem.at[n]) for n in range(count)]
    locals_.append(pltpu.make_async_copy(tokens, window.at[REACH], local_sem.at[count]))
    for copy in locals_:
        copy.start()

    def halo_at(k):
        beside = 1 - 2 * lax.rem(y, 2)
        two = (k * (3 - k)) // 2
        return (1 - two) * beside * (1 - 2 * (k // 3)) + two * 2 * (3 - 2 * k)

    def halo(d, start):
        k = d + REACH

        @pl.when((row + d >= 0) & (row + d < rows))
        def _():
            if start:
                remote(
                    tokens, window.at[REACH - d], halo_send.at[k], halo_recv.at[REACH - d], item, row + d
                ).start()
            else:
                part = window.at[k]
                arrived(part, halo_recv.at[k])

        @pl.when((row + d < 0) | (row + d >= rows))
        def _():
            copy = pltpu.make_async_copy(tokens, window.at[k], halo_recv.at[k])
            if start:
                copy.start()
            else:
                copy.wait()

    def second(step, group):
        zz = near(z, step, nz)
        for n in group:
            part = full[n].at[slot(a, zz, y)]
            if step:
                arrived(part, r1.at[zz, n])
            for d in range(1, ny):
                remote(
                    part if step else mine[n], part, s2.at[step, d, n], r2.at[zz, y, n], item, z * ny + lax.rem(y + d, ny)
                ).start()

    def third(step, group):
        zz = near(z, step, nz)
        for n in group:
            for d in range(1, ny):
                yy = lax.rem(y + d, ny)
                arrived(full[n].at[slot(a, zz, yy)], r2.at[zz, yy, n])
            if step == 0:
                locals_[n].wait()
            block = full[n].at[pl.ds(slot(a, zz, 0), ny)]
            for d in range(1, na):
                remote(
                    block, block, s3.at[step, d, n], r3.at[zz, a, n], lax.rem(a + d, na) * 2 + c, row
                ).start()

    def fourth(step, group):
        zz = near(z, step, nz)
        for e in range(na):
            aa = lax.rem(a + e, na)
            for n in group:
                block = full[n].at[pl.ds(slot(aa, zz, 0), ny)]
                if e:
                    arrived(block, r3.at[zz, aa, n])
                remote(block, block, s4.at[e, step, n], r4.at[aa, zz, n], a * 2 + 1 - c, row).start()

    def settle(group):
        for n in group:
            for e in range(na):
                for step in range(nz):
                    theirs = full[n].at[pl.ds((e * 2 + 1 - c) * rows + step * ny, ny)]
                    arrived(theirs, r4.at[e, step, n])

    loads = [
        pltpu.make_async_copy(full[n], matrix.at[n], load_sem.at[n]) for n in range(3)
    ]
    def store(block, n):
        rows_dev = tokens.shape[0]
        return pltpu.make_async_copy(
            made.at[block, n], wide.at[n, pl.ds(block * rows_dev, rows_dev)], out_sem.at[block, n]
        )

    def project(block):
        @pl.loop(0, 3)
        def _(n):
            factor = matrix[n].reshape(tokens.shape[1], tokens.shape[1])
            total = jnp.dot(window[block], factor, preferred_element_type=jnp.float32)
            made[block, n] = (total + bias[n]).astype(jnp.bfloat16)
            store(block, n).start()

    second(0, soon)
    second(0, later)
    for t in range(1, nz):
        second(t, soon)
        third(t - 1, soon)
    third(nz - 1, soon)
    third(0, later)
    halo(halo_at(0), True)
    for t in range(1, nz):
        second(t, later)
        if t == 1:
            halo(halo_at(1), True)
            halo(halo_at(2), True)
        if t == nz - 1:
            halo(halo_at(3), True)
        third(t - 1, later) if t > 1 else None
        fourth(t - 1, soon)
    fourth(nz - 1, soon)
    third(nz - 1, later)
    settle(soon)
    for load in loads:
        load.start()
    fourth(0, later)
    for n, size in enumerate(sizes[:-1]):
        rows_out[n : n + 1] = spread_row(tiles, n, size)
    last_out[...] = spread_row(tiles, len(sizes) - 1, sizes[-1])
    bias[0] = rows_out[0:1]
    bias[1] = jnp.zeros_like(bias[1])
    bias[2] = rows_out[1:2]
    locals_[count].wait()
    for load in loads:
        load.wait()
    project(REACH)
    for t in range(1, nz - 1):
        fourth(t, later)

    @pl.loop(0, 2)
    def _(k):
        halo(halo_at(k), False)
        project(REACH + halo_at(k))

    fourth(nz - 1, later)

    @pl.loop(2, 4)
    def _(k):
        halo(halo_at(k), False)
        project(REACH + halo_at(k))

    settle(later)

    for n in range(count):
        for step in range(nz):
            part = full[n].at[slot(a, z, y)]
            if step:
                remote(mine[n], part, s1.at[step, n], r1.at[z, n], item, row).wait_send()
            for d in range(1, ny):
                remote(part, part, s2.at[step, d, n], r2.at[z, y, n], item, row).wait_send()
            block = full[n].at[pl.ds(slot(a, z, 0), ny)]
            for d in range(1, na):
                remote(block, block, s3.at[step, d, n], r3.at[z, a, n], item, row).wait_send()
            for e in range(na):
                remote(block, block, s4.at[e, step, n], r4.at[0, 0, n], item, row).wait_send()
    for d in (1, -1, 2, -2):

        @pl.when((row + d >= 0) & (row + d < rows))
        def _():
            remote(
                tokens, window.at[REACH - d], halo_send.at[d + REACH], halo_recv.at[REACH - d], item, row
            ).wait_send()

    for block in range(2 * REACH + 1):
        for n in range(3):
            store(block, n).wait()


def gather_all(mesh_shape, tokens, shards, vectors):
    na = mesh_shape["items"] // 2
    nz, ny = split_rows(mesh_shape["rows"])
    ndev = mesh_shape["items"] * mesh_shape["rows"]
    count = len(shards) + 1
    rows_dev, width = tokens.shape
    blocks = 2 * REACH + 1
    dma = pltpu.SemaphoreType.DMA
    packed = (-(-len(vectors) // 8) * 8, 128)
    sizes = tuple(v.shape[0] for v in vectors)
    wide = jax.ShapeDtypeStruct((3, blocks * rows_dev, width), tokens.dtype)
    hbm, vmem = pl.BlockSpec(memory_space=pl.ANY), pl.BlockSpec(memory_space=pltpu.VMEM)
    return pl.pallas_call(
        functools.partial(gather_kernel, na, nz, ny, sizes),
        out_shape=[jax.ShapeDtypeStruct((ndev,) + s.shape, s.dtype) for s in shards]
        + [jax.ShapeDtypeStruct((len(sizes) - 1, width), jnp.float32)]
        + [jax.ShapeDtypeStruct((1, ndev * sizes[-1]), jnp.float32), wide],
        in_specs=[vmem] * (count + len(vectors)),
        out_specs=[hbm] * len(shards) + [vmem, vmem, hbm],
        scratch_shapes=[
            pltpu.VMEM(packed, jnp.float32),
            pltpu.VMEM((ndev,) + packed, jnp.float32),
            pltpu.VMEM((blocks,) + tokens.shape, tokens.dtype),
            pltpu.VMEM((3, ndev) + shards[0].shape, tokens.dtype),
            pltpu.VMEM((3, 1, width), jnp.float32),
            pltpu.VMEM((blocks, 3) + tokens.shape, tokens.dtype),
            dma((blocks, 3)), dma((3,)),
            dma((blocks,)), dma((blocks,)), dma((count + 1,)),
            dma((nz, count)), dma((nz, count)),
            dma((nz, ny, count)), dma((nz, ny, count)),
            dma((nz, na, count)), dma((nz, na, count)),
            dma((na, nz, count)), dma((na, nz, count)),
        ],
        compiler_params=pltpu.CompilerParams(collective_id=1, has_side_effects=True, vmem_limit_bytes=56 << 20),
        name="gather_weights",
    )(tokens, *shards, *[v[None] for v in vectors])


def scatter_kernel(na, nz, ny, *refs):
    active, d_ffn, normed, d_hidden, attended, d_branch, tokens, d_query, d_keys, d_values, lines = refs[:11]
    sums, sum_lines = refs[11:13]
    (
        act, hid, left, right, turned, product, parts, parts_lines, low, low_lines,
        given_sem, s0, r0, s1, r1, s2, r2, s3, r3,
    ) = refs[13:]
    a, c, z, y = place(nz, ny)
    rows = nz * ny
    row = z * ny + y
    item = a * 2 + c
    devices = 2 * na * rows
    width = left.shape[2]
    height = width // devices
    blocks = hid.shape[1] // width
    many = 2 * blocks + 5
    tile = many - 1

    loads = [
        pltpu.make_async_copy(src, dst, given_sem.at[n])
        for n, (src, dst) in enumerate(
            (
                (normed, left.at[0]), (d_hidden, hid), (active, act), (d_ffn, right.at[0]), (attended, left.at[1]),
                (d_branch, right.at[1]), (tokens, left.at[2]), (d_query, right.at[2]), (d_keys, right.at[3]),
                (d_values, right.at[4]),
            )
        )
    ]
    for load in loads:
        load.start()
    for side in range(2):
        for aa in range(na):
            parts_lines[side, aa] = lines[aa, side]

    barrier = pltpu.get_barrier_semaphore()

    def greet(i_, r_):
        pl.semaphore_signal(barrier, inc=1, device_id=(i_, r_), device_id_type=MESH)

    def at_z(d):
        return lax.rem(z + d, nz) * ny + y

    def at_y(d):
        return z * ny + lax.rem(y + d, ny)

    def at_a(d):
        return lax.rem(a + d, na) * 2 + c

    for d in range(1, nz):
        greet(item, at_z(d))
    for d in range(1, ny):
        greet(item, at_y(d))
    for d in range(1, na):
        greet(at_a(d), row)
    greet(a * 2 + 1 - c, row)
    pl.semaphore_wait(barrier, nz + ny + na - 2)

    def remote(src, dst, send, recv, i_, r_):
        return pltpu.make_async_remote_copy(
            src_ref=src, dst_ref=dst, send_sem=send, recv_sem=recv, device_id=(i_, r_), device_id_type=MESH
        )

    def is_tile(k):
        return isinstance(k, int) and k == tile

    def part(k, side):
        return parts_lines.at[side] if is_tile(k) else parts.at[k, side]

    def mine(k):
        return part(k, c)

    def landing(k, which):
        return low_lines[which] if is_tile(k) else low[which].at[k]

    def core(k, aa, zz):
        return remote(
            part(k, 1 - c).at[aa, zz], landing(k, 0).at[aa, zz], s0.at[k, aa, zz], r0.at[k, aa, zz], a * 2 + 1 - c, row
        )

    def send_core(k):
        for e in range(na):
            for zz in range(nz):
                core(k, lax.rem(a + 1 + e, na), zz).start()

    def first0(k, d, zz):
        aa = lax.rem(a + d, na)
        return remote(
            mine(k).at[aa, zz], landing(k, 1).at[pl.ds((d - 1) * rows + zz * ny, ny)],
            s1.at[k, d, zz], r1.at[k, d, zz], at_a(d), row,
        )

    def first1(k, d, aa):
        return remote(
            mine(k).at[aa, :, lax.rem(y + d, ny)], landing(k, 1).at[pl.ds((d - 1) * na * nz + aa * nz, nz)],
            s1.at[k, d, aa], r1.at[k, d, aa], item, at_y(d),
        )

    def second0(k, d):
        return remote(
            mine(k).at[a, :, lax.rem(y + d, ny)], landing(k, 2).at[pl.ds((d - 1) * nz, nz)],
            s2.at[k, d], r2.at[k, d], item, at_y(d),
        )

    def second1(k, d):
        return remote(
            mine(k).at[lax.rem(a + d, na), :, y], landing(k, 2).at[pl.ds((d - 1) * nz, nz)],
            s2.at[k, d], r2.at[k, d], at_a(d), row,
        )

    def third(k, d):
        return remote(
            mine(k).at[a, lax.rem(z + d, nz), y], landing(k, 3).at[d - 1], s3.at[k, d], r3.at[k, d], item, at_z(d)
        )

    def summed(refs_):
        total = refs_[0][...].astype(jnp.float32)
        for ref in refs_[1:]:
            total = total + ref[...].astype(jnp.float32)
        return total

    def add_into(dst, others):
        dst[...] = summed([dst] + others).astype(dst.dtype)

    def stage1(k):
        for e in range(na):
            aa = lax.rem(a + 1 + e, na)
            for zz in range(nz):
                core(k, aa, zz).wait_recv()

                @pl.loop(0, ny)
                def _(yy):
                    add_into(mine(k).at[aa, zz, yy], [landing(k, 0).at[aa, zz, yy]])

                if e < na - 1:

                    @pl.when(c == 0)
                    def _():
                        first0(k, e + 1, zz).start()

        @pl.when(c == 1)
        def _():
            for d in range(1, ny):
                for aa in range(na):
                    first1(k, d, aa).start()

    def stage2(k):
        @pl.when(c == 0)
        def _():
            for zz in range(nz):
                for d in range(1, na):
                    first0(k, d, zz).wait_recv()

                @pl.loop(0, ny)
                def _(yy):
                    add_into(
                        mine(k).at[a, zz, yy], [landing(k, 1).at[(d - 1) * rows + zz * ny + yy] for d in range(1, na)]
                    )

            for d in range(1, ny):
                second0(k, d).start()

        @pl.when(c == 1)
        def _():
            for d in range(1, ny):
                for aa in range(na):
                    first1(k, d, aa).wait_recv()
            for aa in range(na):

                @pl.loop(0, nz)
                def _(zz):
                    add_into(
                        mine(k).at[aa, zz, y],
                        [landing(k, 1).at[(d - 1) * na * nz + aa * nz + zz] for d in range(1, ny)],
                    )

            for d in range(1, na):
                second1(k, d).start()

    def stage3(k):
        def rest(peers, second):
            for d in range(1, peers):
                second(k, d).wait_recv()

            @pl.loop(0, nz)
            def _(zz):
                add_into(mine(k).at[a, zz, y], [landing(k, 2).at[(d - 1) * nz + zz] for d in range(1, peers)])

        @pl.when(c == 0)
        def _():
            rest(ny, second0)

        @pl.when(c == 1)
        def _():
            rest(na, second1)

        for d in range(1, nz):
            third(k, d).start()

    def stage4(k):
        for d in range(1, nz):
            third(k, d).wait_recv()
        total = summed([mine(k).at[a, z, y]] + [landing(k, 3).at[d - 1] for d in range(1, nz)])
        if is_tile(k):
            sum_lines[...] = total
        else:
            sums[k] = total

    def spread(k):
        @pl.loop(0, devices)
        def _(n):
            i_, r_ = n // rows, lax.rem(n, rows)
            parts[k, lax.rem(i_, 2), i_ // 2, r_ // ny, lax.rem(r_, ny)] = product[
                pl.ds(pl.multiple_of(n * height, 8), height)
            ].astype(parts.dtype)

    def times(factor):
        product[...] = jnp.dot(turned[...], factor, preferred_element_type=jnp.float32)

    def make_hidden(first, last):
        @pl.loop(first, last)
        def _(k):
            times(hid[:, pl.ds(pl.multiple_of(k * width, width), width)])
            spread(k)
            send_core(k)

    def make_return():
        @pl.loop(0, 2 * na)
        def _(i_):
            turned[...] = act[:, pl.ds(pl.multiple_of(i_ * width, width), width)].T
            times(right[0])

            @pl.loop(0, rows)
            def _(r_):
                for k in range(blocks):
                    parts[blocks + k, lax.rem(i_, 2), i_ // 2, r_ // ny, lax.rem(r_, ny)] = product[
                        pl.ds(pl.multiple_of((r_ * blocks + k) * height, 8), height)
                    ].astype(parts.dtype)

        for k in range(blocks):
            send_core(blocks + k)

    def make_rest():
        @pl.loop(0, 4)
        def _(n):
            turned[...] = left[jnp.minimum(n + 1, 2)].T
            times(right[n + 1])
            spread(2 * blocks + n)
            send_core(2 * blocks + n)

    send_core(tile)
    loads[0].wait()
    turned[...] = left[0].T
    loads[1].wait()
    make_hidden(0, 2)
    def beat(t):
        for n, stage in enumerate((stage1, stage2, stage3, stage4)):
            if not isinstance(t, int) or 0 <= t - n < many:
                stage(t - n)

    beat(0)
    make_hidden(2, blocks)
    beat(1)
    loads[2].wait()
    loads[3].wait()
    make_return()
    beat(2)
    for load in loads[4:]:
        load.wait()
    make_rest()
    pl.loop(3, tile)(beat)
    for t in range(tile, many + 3):
        beat(t)

    def finish(k):
        for aa in range(na):
            for zz in range(nz):
                core(k, aa, zz).wait_send()
        for d in range(1, nz):
            third(k, d).wait_send()

        @pl.when(c == 0)
        def _():
            for d in range(1, na):
                for zz in range(nz):
                    first0(k, d, zz).wait_send()
            for d in range(1, ny):
                second0(k, d).wait_send()

        @pl.when(c == 1)
        def _():
            for d in range(1, ny):
                for aa in range(na):
                    first1(k, d, aa).wait_send()
            for d in range(1, na):
                second1(k, d).wait_send()

    pl.loop(0, tile)(finish)
    finish(tile)


def scatter_all(mesh_shape, factors, lines):
    na = mesh_shape["items"] // 2
    nz, ny = split_rows(mesh_shape["rows"])
    devices = 2 * na * nz * ny
    tokens, wide = factors[0].shape
    width = factors[1].shape[1]
    height = width // devices
    blocks = wide // width
    many = 2 * blocks + 5
    dma = pltpu.SemaphoreType.DMA
    nm = max(na, ny)
    low = jnp.bfloat16
    first = max((na - 1) * nz * ny, (ny - 1) * na * nz)
    second = (nm - 1) * nz
    lands = [(na, nz, ny), (first,), (second,), (nz - 1,)]
    one, tile = (height, width), lines.shape[1:]
    f32 = lambda *shape: jax.ShapeDtypeStruct(shape, jnp.float32)
    return pl.pallas_call(
        functools.partial(scatter_kernel, na, nz, ny),
        out_shape=[f32(many - 1, *one), f32(*tile)],
        in_specs=[pl.BlockSpec(memory_space=pl.ANY)] * 10 + [pl.BlockSpec(memory_space=pltpu.VMEM)],
        out_specs=[pl.BlockSpec(memory_space=pltpu.VMEM)] * 2,
        scratch_shapes=[
            pltpu.VMEM((tokens, wide), low),
            pltpu.VMEM((tokens, wide), low),
            pltpu.VMEM((3, tokens, width), low),
            pltpu.VMEM((5, tokens, width), low),
            pltpu.VMEM((width, tokens), low),
            pltpu.VMEM((width, width), jnp.float32),
            pltpu.VMEM((many - 1, 2, na, nz, ny) + one, low),
            pltpu.VMEM((2, na, nz, ny) + tile, jnp.float32),
            [pltpu.VMEM((many - 1,) + land + one, low) for land in lands],
            [pltpu.VMEM(land + tile, jnp.float32) for land in lands],
            dma((10,)),
        ]
        + [dma((many, na, nz))] * 2
        + [dma((many, nm, max(nz, na)))] * 2
        + [dma((many, nm))] * 2
        + [dma((many, nz))] * 2,
        compiler_params=pltpu.CompilerParams(collective_id=2, has_side_effects=True, vmem_limit_bytes=63 << 20),
        name="scatter_grads",
    )(*factors, lines.reshape((na, 2, nz, ny) + tile))


H = 12
HEAD = 64
PAIR = 2 * HEAD
MASKED = -1e30


def dot_last(x, y):
    return lax.dot_general(x, y, (((1,), (1,)), ((), ())), preferred_element_type=jnp.float32)


def dot_plain(x, y):
    return jnp.dot(x, y, preferred_element_type=jnp.float32)


def one_side(block, side, scale=1.0):
    lane = lax.broadcasted_iota(jnp.int32, (1, PAIR), 1)
    keep = (lane // HEAD == side).astype(jnp.float32) * scale
    return (block.astype(jnp.float32) * keep).astype(jnp.bfloat16)


FAR = 1 << 24


def item_at(lengths, place):
    first, last, end = jnp.zeros_like(place), jnp.full_like(place, FAR), 0
    for n in range(lengths.shape[1]):
        end = end + lengths[0, n]
        first = jnp.where(end <= place, end, first)
        last = jnp.where(end > place, jnp.minimum(last, end), last)
    return first, last, end


def span(lengths, start, tile, base, step, most):
    low = item_at(lengths, start)[0] - base
    high = item_at(lengths, start + tile - 1)[1] - base
    return jnp.maximum(low, 0) // step, jnp.minimum((high + step - 1) // step, most)


def items_of(lengths, start, count):
    place = start + lax.broadcasted_iota(jnp.int32, (1, count), 1)
    first, last, end = item_at(lengths, place)
    inside = (place >= 0) & (place < end)
    return jnp.where(inside, first, FAR), jnp.where(inside, last, -1)


def allowed_pairs(first, last, base, shape):
    place = lax.broadcasted_iota(jnp.int32, shape, 0)
    return (place >= first - base) & (place < last - base)


def skewed(count, *stages):
    held = [None] * count
    for t in range(count + len(stages) - 1):
        for k, stage in enumerate(stages):
            n = t - k
            if 0 <= n < count:
                held[n] = stage(n) if k == 0 else stage(n, held[n])
    return tuple(held)


def attend_kernel(tile, step, lengths, query, keys, values, low, full, logsum):
    wide, width = keys.shape
    tokens = wide // (2 * REACH + 1)
    base = (lax.axis_index("rows") - REACH) * tokens
    start = base + REACH * tokens + pl.program_id(0) * tile
    cols = [slice(p * PAIR, (p + 1) * PAIR) for p in range(width // PAIR)]
    heads = [(c, s, one_side(query[:, c], s, HEAD**-0.5)) for c in cols for s in range(2)]
    first, last = items_of(lengths, start, tile)

    def body(j, carry):
        block = pl.ds(pl.multiple_of(j * step, step), step)
        allowed = allowed_pairs(first, last, base + j * step, (step, tile))
        turned = [values[block, c].T for c in cols]

        def score(n):
            c, s, q = heads[n]
            return jnp.where(allowed, dot_last(keys[block, c], q), MASKED)

        def soften(n, scores):
            top, total, acc = carry[n]
            peak = jnp.maximum(top, jnp.max(scores, axis=0, keepdims=True))
            lifted = jnp.exp(scores - peak)
            fade = jnp.exp(top - peak)
            return peak, total * fade + jnp.sum(lifted, axis=0, keepdims=True), fade, lifted.astype(jnp.bfloat16)

        def gather(n, soft):
            peak, total, fade, lifted = soft
            s = heads[n][1]
            return peak, total, carry[n][2] * fade + dot_plain(turned[n // 2][s * HEAD : (s + 1) * HEAD], lifted)

        return skewed(len(heads), score, soften, gather)

    empty = tuple(
        (
            jnp.full((1, tile), MASKED, jnp.float32),
            jnp.zeros((1, tile), jnp.float32),
            jnp.zeros((HEAD, tile), jnp.float32),
        )
        for _ in heads
    )
    done = lax.fori_loop(*span(lengths, start, tile, base, step, wide // step), body, empty)
    for p, c in enumerate(cols):
        (top0, total0, acc0), (top1, total1, acc1) = done[2 * p : 2 * p + 2]
        result = jnp.concatenate([acc0 / total0, acc1 / total1], axis=0).T
        low[:, c] = result.astype(jnp.bfloat16)
        full[:, c] = result
        logsum[2 * p] = top0 + jnp.log(total0)
        logsum[2 * p + 1] = top1 + jnp.log(total1)


def own_tile(n, tile, tiles, width):
    return pl.BlockSpec((None, tile, width), lambda i, b: (n, REACH * tiles + i, 0))


def window_of(n, wide, width):
    return pl.BlockSpec((None, wide, width), lambda i, b: (n, 0, 0))


def tile_of(tile, width):
    return pl.BlockSpec((tile, width), lambda i, b: (i, 0))


def lines(tile):
    return pl.BlockSpec((H, 1, tile), lambda i, b: (0, 0, i))


def cost(matmuls):
    return pl.CostEstimate(flops=matmuls * 2 * H * HEAD * 512 * 1536, bytes_accessed=12 << 20, transcendentals=0)


VMEM = pltpu.CompilerParams(vmem_limit_bytes=56 << 20)


def attend(lengths, projected, tile, step):
    _, wide, width = projected.shape
    tokens = wide // (2 * REACH + 1)
    tiles = tokens // tile
    return pl.pallas_call(
        functools.partial(attend_kernel, tile, step),
        grid_spec=pltpu.PrefetchScalarGridSpec(
            num_scalar_prefetch=1,
            grid=(tiles,),
            in_specs=[own_tile(0, tile, tiles, width), window_of(1, wide, width), window_of(2, wide, width)],
            out_specs=[tile_of(tile, width), tile_of(tile, width), lines(tile)],
        ),
        out_shape=[
            jax.ShapeDtypeStruct((tokens, width), jnp.bfloat16),
            jax.ShapeDtypeStruct((tokens, width), jnp.float32),
            jax.ShapeDtypeStruct((H, 1, tokens), jnp.float32),
        ],
        compiler_params=VMEM,
        cost_estimate=cost(2),
        name="attend",
    )(lengths, projected, projected, projected)


def query_grad_kernel(tile, step, lengths, query, grad, keys, values, logsum, centre, out):
    wide, width = keys.shape
    tokens = wide // (2 * REACH + 1)
    base = (lax.axis_index("rows") - REACH) * tokens
    start = base + REACH * tokens + pl.program_id(0) * tile
    cols = [slice(p * PAIR, (p + 1) * PAIR) for p in range(width // PAIR)]
    heads = [
        (c, s, one_side(query[:, c], s, HEAD**-0.5), one_side(grad[:, c], s), logsum[2 * p + s], centre[2 * p + s])
        for p, c in enumerate(cols)
        for s in range(2)
    ]
    first, last = items_of(lengths, start, tile)

    def body(j, carry):
        block = pl.ds(pl.multiple_of(j * step, step), step)
        allowed = allowed_pairs(first, last, base + j * step, (step, tile))
        turned = [keys[block, c].T for c in cols]

        def score(n):
            c, s, q, g, top, mid = heads[n]
            return dot_last(keys[block, c], q), dot_last(values[block, c], g)

        def soften(n, both):
            top, mid = heads[n][4:]
            weights = jnp.exp(jnp.where(allowed, both[0] - top, MASKED))
            return (weights * (both[1] - mid)).astype(jnp.bfloat16)

        def gather(n, d_scores):
            s = heads[n][1]
            return carry[n] + dot_plain(turned[n // 2][s * HEAD : (s + 1) * HEAD], d_scores)

        return skewed(len(heads), score, soften, gather)

    empty = tuple(jnp.zeros((HEAD, tile), jnp.float32) for _ in heads)
    done = lax.fori_loop(*span(lengths, start, tile, base, step, wide // step), body, empty)
    for p, c in enumerate(cols):
        both = jnp.concatenate(done[2 * p : 2 * p + 2], axis=0) * HEAD**-0.5
        out[:, c] = both.T.astype(jnp.bfloat16)


def query_grad(lengths, projected, grad, logsum, centre, tile, step):
    _, wide, width = projected.shape
    tokens = grad.shape[0]
    tiles = tokens // tile
    return pl.pallas_call(
        functools.partial(query_grad_kernel, tile, step),
        grid_spec=pltpu.PrefetchScalarGridSpec(
            num_scalar_prefetch=1,
            grid=(tiles,),
            in_specs=[
                own_tile(0, tile, tiles, width), tile_of(tile, width),
                window_of(1, wide, width), window_of(2, wide, width), lines(tile), lines(tile),
            ],
            out_specs=tile_of(tile, width),
        ),
        out_shape=jax.ShapeDtypeStruct((tokens, width), jnp.bfloat16),
        compiler_params=VMEM,
        cost_estimate=cost(3),
        name="query_grad",
    )(lengths, projected, grad, projected, projected, logsum, centre)


def key_grad_kernel(tile, step, lengths, keys, values, query, *refs):
    blocks = refs[: 2 * REACH + 1]
    d_keys, d_values, grad, arrived = refs[2 * REACH + 1 :]
    wide, width = query.shape
    tokens = wide // (2 * REACH + 1)
    base = (lax.axis_index("rows") - REACH) * tokens
    start = base + REACH * tokens + pl.program_id(0) * tile

    @pl.when(pl.program_id(0) == 0)
    def _():
        copies = [pltpu.make_async_copy(b, grad.at[k], arrived.at[k]) for k, b in enumerate(blocks)]
        for copy in copies:
            copy.start()
        for copy in copies:
            copy.wait()

    cols = [slice(p * PAIR, (p + 1) * PAIR) for p in range(width // PAIR)]
    heads = [(c, one_side(keys[:, c], s, HEAD**-0.5), one_side(values[:, c], s)) for c in cols for s in range(2)]
    many = len(heads)

    def body(j, carry):
        block = pl.ds(pl.multiple_of(j * step, step), step)
        of = j * step // tokens
        part = pl.ds(pl.multiple_of(j * step - of * tokens, step), step)
        first, last = items_of(lengths, base + j * step, step)
        allowed = allowed_pairs(first, last, start, (tile, step))
        stats = grad[of, part, width:].astype(jnp.float32).T
        stats = stats[: 2 * many] + stats[2 * many : 4 * many] + stats[4 * many : 6 * many]

        def score(n):
            c, k, v = heads[n]
            return dot_last(k, query[block, c]), dot_last(v, grad[of, part, c])

        def soften(n, both):
            weights = jnp.exp(jnp.where(allowed, both[0] - stats[n : n + 1], MASKED))
            d_scores = weights * (both[1] - stats[many + n : many + n + 1])
            return d_scores.astype(jnp.bfloat16), weights.astype(jnp.bfloat16)

        turned = [(query[block, c].T, grad[of, part, c].T) for c in cols]

        def gather(n, soft):
            side = slice(n % 2 * HEAD, (n % 2 + 1) * HEAD)
            q, g = turned[n // 2]
            return carry[n][0] + dot_last(q[side], soft[0]), carry[n][1] + dot_last(g[side], soft[1])

        return skewed(many, score, soften, gather)

    zero = jnp.zeros((HEAD, tile), jnp.float32)
    limits = span(lengths, start, tile, base, step, wide // step)
    done = lax.fori_loop(*limits, body, tuple((zero, zero) for _ in heads))
    for p, c in enumerate(cols):
        (k0, v0), (k1, v1) = done[2 * p : 2 * p + 2]
        d_keys[:, c] = (jnp.concatenate([k0, k1], axis=0) * HEAD**-0.5).T.astype(jnp.bfloat16)
        d_values[:, c] = jnp.concatenate([v0, v1], axis=0).T.astype(jnp.bfloat16)


def key_grad(lengths, projected, grads, tile, step):
    _, wide, width = projected.shape
    tokens = wide // (2 * REACH + 1)
    tiles = tokens // tile
    return pl.pallas_call(
        functools.partial(key_grad_kernel, tile, step),
        grid_spec=pltpu.PrefetchScalarGridSpec(
            num_scalar_prefetch=1,
            grid=(tiles,),
            in_specs=[own_tile(1, tile, tiles, width), own_tile(2, tile, tiles, width), window_of(0, wide, width)]
            + [pl.BlockSpec(memory_space=pl.ANY)] * (2 * REACH + 1),
            out_specs=[tile_of(tile, width)] * 2,
            scratch_shapes=[
                pltpu.VMEM((2 * REACH + 1,) + grads[0].shape, jnp.bfloat16), pltpu.SemaphoreType.DMA((2 * REACH + 1,))
            ],
        ),
        out_shape=[jax.ShapeDtypeStruct((tokens, width), jnp.bfloat16)] * 2,
        compiler_params=VMEM,
        cost_estimate=cost(4),
        name="key_grad",
    )(lengths, projected, projected, projected, *grads)


eps_norm = 1e-06
AXES = ("items", "rows")


NAMES = (
    "query_proj", "key_proj", "value_proj", "query_bias", "value_bias", "output_proj", "output_bias", "attn_gain",
    "attn_shift", "hidden_proj", "hidden_bias", "return_proj", "return_bias", "final_gain", "final_shift",
)


def dot_rows(matrix, factor):
    return lax.dot_general(matrix, factor, (((0,), (0,)), ((), ())), preferred_element_type=jnp.float32)


def layer_norm(hidden, norm_gain, norm_shift):
    row_mean = jnp.mean(hidden, axis=1, keepdims=True)
    centred = hidden - row_mean
    row_var = jnp.mean(centred * centred, axis=1, keepdims=True)
    return centred * lax.rsqrt(row_var + eps_norm) * norm_gain + norm_shift


def shifted(value, by):
    peers = lax.axis_size("rows")
    pairs = [(i, i + by) for i in range(peers) if 0 <= i + by < peers]
    return lax.ppermute(value, "rows", pairs)


def halo(value):
    return [value if d == 0 else shifted(value, -d) for d in range(-REACH, REACH + 1)]


def in_thirds(value, width):
    high = lax.reduce_precision(value, 8, 7)
    middle = lax.reduce_precision(value - high, 8, 7)
    pieces = jnp.concatenate([high, middle, value - high - middle], axis=1)
    return jnp.pad(pieces, ((0, 0), (0, width - pieces.shape[1]))).astype(jnp.bfloat16)


TILE, STEP = 256, 256


def per_device(mesh_shape, tokens, *given):
    names = NAMES
    part = dict(zip(names, given[:15]))
    item_lengths, out_grad = given[15:]
    matrices = ["query_proj", "key_proj", "value_proj", "output_proj", "hidden_proj", "return_proj"]
    vectors = [n for n in names if n not in matrices]
    outer = [n for n in vectors if n != "hidden_bias"]
    ndev = mesh_shape["items"] * mesh_shape["rows"]
    rows_dev, width = tokens.shape
    aligned = all(part[n].shape[0] % 8 == 0 for n in matrices) and all(part[n].shape[0] <= 128 for n in vectors)
    sizes = [part[n].shape[0] for n in vectors]
    used = sum(sizes)
    padded = -(-used // 1024) * 1024
    W = {}
    if aligned:
        got = gather_all(mesh_shape, tokens, [part[n] for n in matrices], [part[n] for n in outer + ["hidden_bias"]])
        wholes = [g.reshape((-1,) + g.shape[2:]) for g in got[: len(matrices)]]
        for k, n in enumerate(outer):
            W[n] = got[-3][k : k + 1]
        W["hidden_bias"] = got[-2]
        projected = got[-1]
    else:
        wholes = [lax.all_gather(part[n], AXES, axis=0, tiled=True) for n in matrices]
        flat = lax.all_gather(jnp.concatenate([part[n] for n in vectors]), AXES, axis=0, tiled=False)
        at = 0
        for n, size in zip(vectors, sizes):
            W[n] = flat[:, at : at + size].reshape(1, -1).astype(jnp.float32)
            at += size
        window = jnp.concatenate(halo(tokens))
        query_wide = (dot_plain(window, wholes[0]) + W["query_bias"]).astype(jnp.bfloat16)
        keys_wide = dot_plain(window, wholes[1]).astype(jnp.bfloat16)
        values_wide = (dot_plain(window, wholes[2]) + W["value_bias"]).astype(jnp.bfloat16)
        projected = jnp.stack([query_wide, keys_wide, values_wide])
    W.update(zip(matrices, wholes))

    attended, attended_full, logsum = attend(item_lengths, projected, TILE, STEP)

    mixed = tokens.astype(jnp.float32) + (dot_plain(attended, W["output_proj"]) + W["output_bias"])
    normed, attn_back = jax.vjp(layer_norm, mixed, W["attn_gain"], W["attn_shift"])
    normed_low = normed.astype(jnp.bfloat16)
    hidden_pre = dot_plain(normed_low, W["hidden_proj"]) + W["hidden_bias"]
    cdf = 0.5 * (1.0 + lax.erf(hidden_pre * (0.5**0.5)))
    active = (hidden_pre * cdf).astype(jnp.bfloat16)
    slope = cdf + hidden_pre * jnp.exp(-0.5 * hidden_pre * hidden_pre) * 0.3989422804014327
    second = normed + (dot_plain(active, W["return_proj"]) + W["return_bias"])
    result, final_back = jax.vjp(layer_norm, second, W["final_gain"], W["final_shift"])

    grads = {}
    d_second, grads["final_gain"], grads["final_shift"] = final_back(out_grad.astype(jnp.float32))
    d_ffn = d_second.astype(jnp.bfloat16)
    grads["return_bias"] = jnp.sum(d_ffn.astype(jnp.float32), axis=0)
    d_hidden = (dot_last(d_ffn, W["return_proj"]) * slope).astype(jnp.bfloat16)
    grads["hidden_bias"] = jnp.sum(d_hidden.astype(jnp.float32), axis=0)
    d_normed = dot_last(d_hidden, W["hidden_proj"]) + d_second
    d_mixed, grads["attn_gain"], grads["attn_shift"] = attn_back(d_normed)
    d_branch = d_mixed.astype(jnp.bfloat16)
    grads["output_bias"] = jnp.sum(d_branch.astype(jnp.float32), axis=0)
    d_attended = dot_last(d_branch, W["output_proj"]).astype(jnp.bfloat16)

    lanes = jnp.arange(width, dtype=jnp.int32)[None, :] // HEAD == jnp.arange(16, dtype=jnp.int32)[:, None]
    product = d_attended.astype(jnp.float32) * attended_full
    lanes = lanes.astype(jnp.float32)
    highest = lax.Precision.HIGHEST
    centre = lax.dot_general(lanes, product, (((1,), (1,)), ((), ())), precision=highest)[:H, None]
    stats = jnp.concatenate([logsum[:, 0], centre[:, 0]]).T
    grad_blocks = halo(jnp.concatenate([d_attended, in_thirds(stats, PAIR)], axis=1))
    d_query = query_grad(item_lengths, projected, d_attended, logsum, centre, TILE, STEP)
    d_keys, d_values = key_grad(item_lengths, projected, grad_blocks, TILE, STEP)
    grads["query_bias"] = jnp.sum(d_query.astype(jnp.float32), axis=0)
    grads["value_bias"] = jnp.sum(d_values.astype(jnp.float32), axis=0)
    tokens_grad = (
        d_mixed
        + dot_last(d_query, W["query_proj"])
        + dot_last(d_keys, W["key_proj"])
        + dot_last(d_values, W["value_proj"])
    )

    rows_of = jnp.concatenate([grads[n].reshape(ndev, size) for n, size in zip(vectors, sizes)], axis=1)
    rows_of = jnp.pad(rows_of, ((0, 0), (0, padded - used))).reshape(ndev, 8, padded // 8)
    factors = (
        active, d_ffn, normed_low, d_hidden, attended, d_branch, tokens, d_query, d_keys, d_values
    )
    order = ("hidden_proj", "return_proj", "output_proj", "query_proj", "key_proj", "value_proj")
    if aligned:
        chunks, tile = scatter_all(mesh_shape, factors, rows_of)
        blocks = d_hidden.shape[1] // width
        sums = [
            jnp.concatenate([chunks[k] for k in range(blocks)], axis=1),
            chunks[blocks : 2 * blocks].reshape(-1, width),
        ] + [chunks[2 * blocks + k] for k in range(4)] + [tile]
    else:
        pairs = ((2, 3), (0, 1), (4, 5), (6, 7), (6, 8), (6, 9))
        low = [dot_rows(factors[i], factors[j]).astype(jnp.bfloat16) for i, j in pairs]
        low = [g.reshape((ndev, -1) + g.shape[1:]) for g in low] + [rows_of]
        sums = [lax.psum_scatter(g, AXES, scatter_dimension=0, tiled=True)[0] for g in low]
    total = {n: s.astype(jnp.float32) for n, s in zip(order, sums)}
    line = sums[-1].reshape(padded)
    at = 0
    for n, size in zip(vectors, sizes):
        total[n] = line[at : at + size]
        at += size
    return (result.astype(jnp.bfloat16), tokens_grad) + tuple(total[n] for n in names)


def solution(mesh):
    both = P(AXES)
    return jax.shard_map(
        functools.partial(per_device, dict(mesh.shape)),
        mesh=mesh,
        in_specs=(both,) * 16 + (P("items"), both),
        out_specs=(both,) * 17,
        check_vma=False,
    )
```

```python
import functools
import jax
import jax.numpy as jnp
from jax import lax
from jax.experimental import pallas as pl
from jax.experimental.pallas import tpu as pltpu

from jax.sharding import PartitionSpec as P

MESH = pl.DeviceIdType.MESH
REACH = 2


def split_rows(rows):
    inner = 1
    while (2 * inner) ** 2 <= rows:
        inner *= 2
    return rows // inner, inner


def place(nz, ny):
    item, row = lax.axis_index("items"), lax.axis_index("rows")
    return item // 2, item % 2, row // ny, row % ny


def near(z, step, nz):
    way = 1 - 2 * (z // ((nz + 1) // 2))
    return lax.rem(z + way * step + nz * 2, nz)


def spread_row(tiles, n, size):
    devices = tiles.shape[0]
    column = lax.broadcasted_iota(jnp.int32, (1, devices * size), 1).astype(jnp.float32)
    owner = jnp.floor((column + 0.5) / size)
    lane = lax.broadcasted_iota(jnp.int32, (tiles.shape[2], 1), 0).astype(jnp.float32)
    pick = (column - owner * size == lane).astype(jnp.float32).astype(jnp.bfloat16)
    spread = jnp.dot(tiles[:, n, :].astype(jnp.bfloat16), pick, preferred_element_type=jnp.float32)
    device = lax.broadcasted_iota(jnp.int32, (devices, 1), 0).astype(jnp.float32)
    return jnp.sum(jnp.where(owner == device, spread, 0.0), axis=0, keepdims=True)


def gather_kernel(na, nz, ny, sizes, *refs):
    weights = 6
    count = weights + 1
    lengths, tokens = refs[:2]
    refs = refs[1:]
    mine = list(refs[1 : 1 + weights])
    lines = refs[1 + weights : 1 + weights + len(sizes)]
    refs = refs[1 + weights + len(sizes) :]
    full = list(refs[:weights])
    rows_out, last_out, wide, low, full_low, logsum = refs[weights : weights + 6]
    (
        packed, tiles, window, matrix, bias, made, sided, top, total, acc, bounds, out_sem, load_sem, halo_send, halo_recv, local_sem,
        s1, r1, s2, r2, s3, r3, s4, r4,
    ) = refs[weights + 6 :]
    mine.append(packed)
    full.append(tiles)
    packed[...] = jnp.zeros_like(packed)
    for n, line in enumerate(lines):
        packed[n : n + 1, : line.shape[1]] = line[...].astype(jnp.float32)

    a, c, z, y = place(nz, ny)
    rows = nz * ny
    row = z * ny + y
    item = a * 2 + c

    def slot(a_, z_, y_):
        return (a_ * 2 + c) * rows + z_ * ny + y_

    barrier = pltpu.get_barrier_semaphore()

    def greet(i_, r_):
        pl.semaphore_signal(barrier, inc=1, device_id=(i_, r_), device_id_type=MESH)

    for d in range(1, nz):
        greet(item, near(z, d, nz) * ny + y)
    for d in range(1, ny):
        greet(item, z * ny + lax.rem(y + d, ny))
    for d in range(1, na):
        greet(lax.rem(a + d, na) * 2 + c, row)
    greet(a * 2 + 1 - c, row)
    for d in range(-REACH, REACH + 1):
        if d != 0:
            greet(item, lax.rem(row + d + rows, rows))
    pl.semaphore_wait(barrier, nz + ny + na - 2 + 2 * REACH)

    def remote(src, dst, send, recv, i_, r_):
        return pltpu.make_async_remote_copy(
            src_ref=src, dst_ref=dst, send_sem=send, recv_sem=recv, device_id=(i_, r_), device_id_type=MESH
        )

    def arrived(part, recv):
        remote(part, part, s1.at[0, 0], recv, item, row).wait_recv()

    soon, later = (0, 1, 2, weights), (3, 4, 5)
    for group in (soon, later):
        for d in range(1, nz):
            for n in group:
                remote(
                    mine[n], full[n].at[slot(a, z, y)], s1.at[d, n], r1.at[z, n], item, near(z, d, nz) * ny + y
                ).start()
    locals_ = [pltpu.make_async_copy(mine[n], full[n].at[slot(a, z, y)], local_sem.at[n]) for n in range(count)]
    locals_.append(pltpu.make_async_copy(tokens, window.at[REACH], local_sem.at[count]))
    for copy in locals_:
        copy.start()

    def halo_at(k):
        beside = 1 - 2 * lax.rem(y, 2)
        two = (k * (3 - k)) // 2
        return (1 - two) * beside * (1 - 2 * (k // 3)) + two * 2 * (3 - 2 * k)

    def halo(d, start):
        k = d + REACH

        @pl.when((row + d >= 0) & (row + d < rows))
        def _():
            if start:
                remote(
                    tokens, window.at[REACH - d], halo_send.at[k], halo_recv.at[REACH - d], item, row + d
                ).start()
            else:
                part = window.at[k]
                arrived(part, halo_recv.at[k])

        @pl.when((row + d < 0) | (row + d >= rows))
        def _():
            copy = pltpu.make_async_copy(tokens, window.at[k], halo_recv.at[k])
            if start:
                copy.start()
            else:
                copy.wait()

    def second(step, group):
        zz = near(z, step, nz)
        for n in group:
            part = full[n].at[slot(a, zz, y)]
            if step:
                arrived(part, r1.at[zz, n])
            for d in range(1, ny):
                remote(
                    part if step else mine[n], part, s2.at[step, d, n], r2.at[zz, y, n], item, z * ny + lax.rem(y + d, ny)
                ).start()

    def third(step, group):
        zz = near(z, step, nz)
        for n in group:
            for d in range(1, ny):
                yy = lax.rem(y + d, ny)
                arrived(full[n].at[slot(a, zz, yy)], r2.at[zz, yy, n])
            if isinstance(step, int) and step == 0:
                locals_[n].wait()
            block = full[n].at[pl.ds(slot(a, zz, 0), ny)]
            for d in range(1, na):
                remote(
                    block, block, s3.at[step, d, n], r3.at[zz, a, n], lax.rem(a + d, na) * 2 + c, row
                ).start()

    def fourth(step, group):
        zz = near(z, step, nz)
        for e in range(na):
            aa = lax.rem(a + e, na)
            for n in group:
                block = full[n].at[pl.ds(slot(aa, zz, 0), ny)]
                if e:
                    arrived(block, r3.at[zz, aa, n])
                remote(block, block, s4.at[e, step, n], r4.at[aa, zz, n], a * 2 + 1 - c, row).start()

    def settle(group):
        for n in group:
            for e in range(na):
                for step in range(nz):
                    theirs = full[n].at[pl.ds((e * 2 + 1 - c) * rows + step * ny, ny)]
                    arrived(theirs, r4.at[e, step, n])

    loads = [
        pltpu.make_async_copy(full[n], matrix.at[n], load_sem.at[n]) for n in range(3)
    ]
    def store(block, n):
        rows_dev = tokens.shape[0]
        return pltpu.make_async_copy(
            made.at[block, n], wide.at[n, pl.ds(block * rows_dev, rows_dev)], out_sem.at[block, n]
        )

    def project(block):
        @pl.loop(0, 3)
        def _(n):
            factor = matrix[n].reshape(tokens.shape[1], tokens.shape[1])
            total = jnp.dot(window[block], factor, preferred_element_type=jnp.float32)
            made[block, n] = (total + bias[n]).astype(jnp.bfloat16)
            store(block, n).start()

    second(0, soon)
    second(0, later)
    for t in range(1, nz):
        second(t, soon)
        third(t - 1, soon)
    third(nz - 1, soon)
    third(0, later)
    halo(halo_at(0), True)
    second(1, later)
    halo(halo_at(1), True)
    halo(halo_at(2), True)
    for t in range(nz):
        fourth(t, soon)
    for t in range(2, nz):
        second(t, later)
    halo(halo_at(3), True)
    settle(soon)
    for load in loads:
        load.start()
    for n, size in enumerate(sizes[:-1]):
        rows_out[n : n + 1] = spread_row(tiles, n, size)
    last_out[...] = spread_row(tiles, len(sizes) - 1, sizes[-1])
    bias[0] = rows_out[0:1]
    bias[1] = jnp.zeros_like(bias[1])
    bias[2] = rows_out[1:2]
    locals_[count].wait()
    for load in loads:
        load.wait()

    rows_dev = tokens.shape[0]
    tile = acc.shape[3]
    spans = rows_dev // tile
    base = (row - REACH) * rows_dev
    pairs = tokens.shape[1] // PAIR
    top[...] = jnp.full_like(top, MASKED)
    total[...] = jnp.zeros_like(total)
    acc[...] = jnp.zeros_like(acc)
    for i in range(spans):
        bounds[i, 0], bounds[i, 1] = items_of(lengths, base + REACH * rows_dev + i * tile, tile)

    def visit(block, half, i):
        part = pl.ds(pl.multiple_of(half * tile, tile), tile)
        allowed = allowed_pairs(
            bounds[i, 0], bounds[i, 1], base + block * rows_dev + half * tile, (tile, tile)
        )
        done = attend_step(
            [sided[i, n] for n in range(2 * pairs)],
            lambda n: (top[i, n], total[i, n], acc[i, n]),
            made.at[block, 1, part], made.at[block, 2, part], allowed,
        )
        for n, (top_, total_, acc_) in enumerate(done):
            top[i, n] = top_
            total[i, n] = total_
            acc[i, n] = acc_

    @pl.loop(0, 2 * REACH + 1)
    def _(k):
        away = halo_at(jnp.maximum(k - 1, 0)) * jnp.minimum(k, 1)
        block = REACH + away

        @pl.when(k + 1 < nz)
        def _():
            third(k + 1, later)

        @pl.when(k > 0)
        def _():
            halo(away, False)

        @pl.when((k > 0) & (k <= nz))
        def _():
            fourth(k - 1, later)

        project(block)

        @pl.when(k == 0)
        def _():
            for i in range(spans):
                for n in range(2 * pairs):
                    query = made[REACH, 0, i * tile : (i + 1) * tile, n // 2 * PAIR : (n // 2 + 1) * PAIR]
                    sided[i, n] = one_side(query, n % 2, HEAD**-0.5)

        @pl.loop(0, spans * spans)
        def _(m):
            i, half = m // spans, lax.rem(m, spans)
            step = block * spans + half

            there = (row + away >= 0) & (row + away < rows)

            @pl.when(there & (step >= i) & (step <= 2 * REACH * spans + i))
            def _():
                visit(block, half, i)

    for t in range(2 * REACH + 2, nz):
        third(t, later)
    for t in range(2 * REACH, nz):
        fourth(t, later)
    for i in range(spans):
        mine_rows = slice(i * tile, (i + 1) * tile)

        def keep(p, result, sum0, sum1):
            c_ = slice(p * PAIR, (p + 1) * PAIR)
            low[mine_rows, c_] = result.astype(jnp.bfloat16)
            full_low[mine_rows, c_] = result
            logsum[2 * p, :, mine_rows] = sum0
            logsum[2 * p + 1, :, mine_rows] = sum1

        attend_done([(top[i, n], total[i, n], acc[i, n]) for n in range(2 * pairs)], keep)
    settle(later)

    for n in range(count):
        for step in range(nz):
            part = full[n].at[slot(a, z, y)]
            if step:
                remote(mine[n], part, s1.at[step, n], r1.at[z, n], item, row).wait_send()
            for d in range(1, ny):
                remote(part, part, s2.at[step, d, n], r2.at[z, y, n], item, row).wait_send()
            block = full[n].at[pl.ds(slot(a, z, 0), ny)]
            for d in range(1, na):
                remote(block, block, s3.at[step, d, n], r3.at[z, a, n], item, row).wait_send()
            for e in range(na):
                remote(block, block, s4.at[e, step, n], r4.at[0, 0, n], item, row).wait_send()
    for d in (1, -1, 2, -2):

        @pl.when((row + d >= 0) & (row + d < rows))
        def _():
            remote(
                tokens, window.at[REACH - d], halo_send.at[d + REACH], halo_recv.at[REACH - d], item, row
            ).wait_send()

    for block in range(2 * REACH + 1):
        for n in range(3):
            store(block, n).wait()


def gather_all(mesh_shape, lengths, tokens, shards, vectors, tile):
    na = mesh_shape["items"] // 2
    nz, ny = split_rows(mesh_shape["rows"])
    ndev = mesh_shape["items"] * mesh_shape["rows"]
    count = len(shards) + 1
    rows_dev, width = tokens.shape
    blocks = 2 * REACH + 1
    dma = pltpu.SemaphoreType.DMA
    packed = (-(-len(vectors) // 8) * 8, 128)
    sizes = tuple(v.shape[0] for v in vectors)
    wide = jax.ShapeDtypeStruct((3, blocks * rows_dev, width), tokens.dtype)
    hbm, vmem = pl.BlockSpec(memory_space=pl.ANY), pl.BlockSpec(memory_space=pltpu.VMEM)
    return pl.pallas_call(
        functools.partial(gather_kernel, na, nz, ny, sizes),
        out_shape=[jax.ShapeDtypeStruct((ndev,) + s.shape, s.dtype) for s in shards]
        + [jax.ShapeDtypeStruct((len(sizes) - 1, width), jnp.float32)]
        + [jax.ShapeDtypeStruct((1, ndev * sizes[-1]), jnp.float32), wide]
        + [jax.ShapeDtypeStruct(tokens.shape, tokens.dtype), jax.ShapeDtypeStruct(tokens.shape, jnp.float32)]
        + [jax.ShapeDtypeStruct((H, 1, rows_dev), jnp.float32)],
        in_specs=[pl.BlockSpec(memory_space=pltpu.SMEM)] + [vmem] * (count + len(vectors)),
        out_specs=[hbm] * len(shards) + [vmem, vmem, hbm, vmem, vmem, vmem],
        scratch_shapes=[
            pltpu.VMEM(packed, jnp.float32),
            pltpu.VMEM((ndev,) + packed, jnp.float32),
            pltpu.VMEM((blocks,) + tokens.shape, tokens.dtype),
            pltpu.VMEM((3, ndev) + shards[0].shape, tokens.dtype),
            pltpu.VMEM((3, 1, width), jnp.float32),
            pltpu.VMEM((blocks, 3) + tokens.shape, tokens.dtype),
            pltpu.VMEM((rows_dev // tile, H, tile, PAIR), tokens.dtype),
            pltpu.VMEM((rows_dev // tile, H, 1, tile), jnp.float32),
            pltpu.VMEM((rows_dev // tile, H, 1, tile), jnp.float32),
            pltpu.VMEM((rows_dev // tile, H, HEAD, tile), jnp.float32),
            pltpu.VMEM((rows_dev // tile, 2, 1, tile), jnp.int32),
            dma((blocks, 3)), dma((3,)),
            dma((blocks,)), dma((blocks,)), dma((count + 1,)),
            dma((nz, count)), dma((nz, count)),
            dma((nz, ny, count)), dma((nz, ny, count)),
            dma((nz, na, count)), dma((nz, na, count)),
            dma((na, nz, count)), dma((na, nz, count)),
        ],
        compiler_params=pltpu.CompilerParams(collective_id=1, has_side_effects=True, vmem_limit_bytes=60 << 20),
        name="gather_weights",
    )(lengths, tokens, *shards, *[v[None] for v in vectors])


def scatter_kernel(na, nz, ny, *refs):
    active, d_ffn, normed, d_hidden, attended, d_branch, tokens, d_query, d_keys, d_values, lines = refs[:11]
    sums, sum_lines = refs[11:13]
    (
        act, hid, left, right, turned, product, parts, parts_lines, low, low_lines,
        given_sem, s0, r0, s1, r1, s2, r2, s3, r3,
    ) = refs[13:]
    a, c, z, y = place(nz, ny)
    rows = nz * ny
    row = z * ny + y
    item = a * 2 + c
    devices = 2 * na * rows
    width = left.shape[2]
    height = width // devices
    blocks = hid.shape[1] // width
    many = 2 * blocks + 5
    tile = many - 1

    loads = [
        pltpu.make_async_copy(src, dst, given_sem.at[n])
        for n, (src, dst) in enumerate(
            (
                (normed, left.at[0]), (d_hidden, hid), (active, act), (d_ffn, right.at[0]), (attended, left.at[1]),
                (d_branch, right.at[1]), (tokens, left.at[2]), (d_query, right.at[2]), (d_keys, right.at[3]),
                (d_values, right.at[4]),
            )
        )
    ]
    for load in loads:
        load.start()
    for side in range(2):
        for aa in range(na):
            parts_lines[side, aa] = lines[aa, side]

    barrier = pltpu.get_barrier_semaphore()

    def greet(i_, r_):
        pl.semaphore_signal(barrier, inc=1, device_id=(i_, r_), device_id_type=MESH)

    def at_z(d):
        return lax.rem(z + d, nz) * ny + y

    def at_y(d):
        return z * ny + lax.rem(y + d, ny)

    def at_a(d):
        return lax.rem(a + d, na) * 2 + c

    for d in range(1, nz):
        greet(item, at_z(d))
    for d in range(1, ny):
        greet(item, at_y(d))
    for d in range(1, na):
        greet(at_a(d), row)
    greet(a * 2 + 1 - c, row)
    pl.semaphore_wait(barrier, nz + ny + na - 2)

    def remote(src, dst, send, recv, i_, r_):
        return pltpu.make_async_remote_copy(
            src_ref=src, dst_ref=dst, send_sem=send, recv_sem=recv, device_id=(i_, r_), device_id_type=MESH
        )

    def is_tile(k):
        return isinstance(k, int) and k == tile

    def part(k, side):
        return parts_lines.at[side] if is_tile(k) else parts.at[k, side]

    def mine(k):
        return part(k, c)

    def landing(k, which):
        return low_lines[which] if is_tile(k) else low[which].at[k]

    def core(k, aa, zz):
        return remote(
            part(k, 1 - c).at[aa, zz], landing(k, 0).at[aa, zz], s0.at[k, aa, zz], r0.at[k, aa, zz], a * 2 + 1 - c, row
        )

    def send_core(k):
        for e in range(na):
            for zz in range(nz):
                core(k, lax.rem(a + 1 + e, na), zz).start()

    def first0(k, d, zz):
        aa = lax.rem(a + d, na)
        return remote(
            mine(k).at[aa, zz], landing(k, 1).at[pl.ds((d - 1) * rows + zz * ny, ny)],
            s1.at[k, d, zz], r1.at[k, d, zz], at_a(d), row,
        )

    def first1(k, d, aa):
        return remote(
            mine(k).at[aa, :, lax.rem(y + d, ny)], landing(k, 1).at[pl.ds((d - 1) * na * nz + aa * nz, nz)],
            s1.at[k, d, aa], r1.at[k, d, aa], item, at_y(d),
        )

    def second0(k, d):
        return remote(
            mine(k).at[a, :, lax.rem(y + d, ny)], landing(k, 2).at[pl.ds((d - 1) * nz, nz)],
            s2.at[k, d], r2.at[k, d], item, at_y(d),
        )

    def second1(k, d):
        return remote(
            mine(k).at[lax.rem(a + d, na), :, y], landing(k, 2).at[pl.ds((d - 1) * nz, nz)],
            s2.at[k, d], r2.at[k, d], at_a(d), row,
        )

    def third(k, d):
        return remote(
            mine(k).at[a, lax.rem(z + d, nz), y], landing(k, 3).at[d - 1], s3.at[k, d], r3.at[k, d], item, at_z(d)
        )

    def summed(refs_):
        total = refs_[0][...].astype(jnp.float32)
        for ref in refs_[1:]:
            total = total + ref[...].astype(jnp.float32)
        return total

    def add_into(dst, others):
        dst[...] = summed([dst] + others).astype(dst.dtype)

    def stage1(k):
        for e in range(na):
            aa = lax.rem(a + 1 + e, na)
            for zz in range(nz):
                core(k, aa, zz).wait_recv()

                @pl.loop(0, ny)
                def _(yy):
                    add_into(mine(k).at[aa, zz, yy], [landing(k, 0).at[aa, zz, yy]])

                if e < na - 1:

                    @pl.when(c == 0)
                    def _():
                        first0(k, e + 1, zz).start()

        @pl.when(c == 1)
        def _():
            for d in range(1, ny):
                for aa in range(na):
                    first1(k, d, aa).start()

    def stage2(k):
        @pl.when(c == 0)
        def _():
            for zz in range(nz):
                for d in range(1, na):
                    first0(k, d, zz).wait_recv()

                @pl.loop(0, ny)
                def _(yy):
                    add_into(
                        mine(k).at[a, zz, yy], [landing(k, 1).at[(d - 1) * rows + zz * ny + yy] for d in range(1, na)]
                    )

            for d in range(1, ny):
                second0(k, d).start()

        @pl.when(c == 1)
        def _():
            for d in range(1, ny):
                for aa in range(na):
                    first1(k, d, aa).wait_recv()
            for aa in range(na):

                @pl.loop(0, nz)
                def _(zz):
                    add_into(
                        mine(k).at[aa, zz, y],
                        [landing(k, 1).at[(d - 1) * na * nz + aa * nz + zz] for d in range(1, ny)],
                    )

            for d in range(1, na):
                second1(k, d).start()

    def stage3(k):
        def rest(peers, second):
            for d in range(1, peers):
                second(k, d).wait_recv()

            @pl.loop(0, nz)
            def _(zz):
                add_into(mine(k).at[a, zz, y], [landing(k, 2).at[(d - 1) * nz + zz] for d in range(1, peers)])

        @pl.when(c == 0)
        def _():
            rest(ny, second0)

        @pl.when(c == 1)
        def _():
            rest(na, second1)

        for d in range(1, nz):
            third(k, d).start()

    def stage4(k):
        for d in range(1, nz):
            third(k, d).wait_recv()
        total = summed([mine(k).at[a, z, y]] + [landing(k, 3).at[d - 1] for d in range(1, nz)])
        if is_tile(k):
            sum_lines[...] = total
        else:
            sums[k] = total

    def spread(k):
        @pl.loop(0, devices)
        def _(n):
            i_, r_ = n // rows, lax.rem(n, rows)
            parts[k, lax.rem(i_, 2), i_ // 2, r_ // ny, lax.rem(r_, ny)] = product[
                pl.ds(pl.multiple_of(n * height, 8), height)
            ].astype(parts.dtype)

    def times(factor):
        product[...] = jnp.dot(turned[...], factor, preferred_element_type=jnp.float32)

    def make_hidden(first, last):
        @pl.loop(first, last)
        def _(k):
            times(hid[:, pl.ds(pl.multiple_of(k * width, width), width)])
            spread(k)
            send_core(k)

    def make_return():
        @pl.loop(0, 2 * na)
        def _(i_):
            turned[...] = act[:, pl.ds(pl.multiple_of(i_ * width, width), width)].T
            times(right[0])

            @pl.loop(0, rows)
            def _(r_):
                for k in range(blocks):
                    parts[blocks + k, lax.rem(i_, 2), i_ // 2, r_ // ny, lax.rem(r_, ny)] = product[
                        pl.ds(pl.multiple_of((r_ * blocks + k) * height, 8), height)
                    ].astype(parts.dtype)

        for k in range(blocks):
            send_core(blocks + k)

    def make_rest():
        @pl.loop(0, 4)
        def _(n):
            turned[...] = left[jnp.minimum(n + 1, 2)].T
            times(right[n + 1])
            spread(2 * blocks + n)
            send_core(2 * blocks + n)

    send_core(tile)
    loads[0].wait()
    turned[...] = left[0].T
    loads[1].wait()
    make_hidden(0, 2)
    def beat(t):
        for n, stage in enumerate((stage1, stage2, stage3, stage4)):
            if not isinstance(t, int) or 0 <= t - n < many:
                stage(t - n)

    beat(0)
    make_hidden(2, blocks)
    beat(1)
    loads[2].wait()
    loads[3].wait()
    make_return()
    beat(2)
    for load in loads[4:]:
        load.wait()
    make_rest()
    pl.loop(3, tile)(beat)
    for t in range(tile, many + 3):
        beat(t)

    def finish(k):
        for aa in range(na):
            for zz in range(nz):
                core(k, aa, zz).wait_send()
        for d in range(1, nz):
            third(k, d).wait_send()

        @pl.when(c == 0)
        def _():
            for d in range(1, na):
                for zz in range(nz):
                    first0(k, d, zz).wait_send()
            for d in range(1, ny):
                second0(k, d).wait_send()

        @pl.when(c == 1)
        def _():
            for d in range(1, ny):
                for aa in range(na):
                    first1(k, d, aa).wait_send()
            for d in range(1, na):
                second1(k, d).wait_send()

    pl.loop(0, tile)(finish)
    finish(tile)


def scatter_all(mesh_shape, factors, lines):
    na = mesh_shape["items"] // 2
    nz, ny = split_rows(mesh_shape["rows"])
    devices = 2 * na * nz * ny
    tokens, wide = factors[0].shape
    width = factors[1].shape[1]
    height = width // devices
    blocks = wide // width
    many = 2 * blocks + 5
    dma = pltpu.SemaphoreType.DMA
    nm = max(na, ny)
    low = jnp.bfloat16
    first = max((na - 1) * nz * ny, (ny - 1) * na * nz)
    second = (nm - 1) * nz
    lands = [(na, nz, ny), (first,), (second,), (nz - 1,)]
    one, tile = (height, width), lines.shape[1:]
    f32 = lambda *shape: jax.ShapeDtypeStruct(shape, jnp.float32)
    return pl.pallas_call(
        functools.partial(scatter_kernel, na, nz, ny),
        out_shape=[f32(many - 1, *one), f32(*tile)],
        in_specs=[pl.BlockSpec(memory_space=pl.ANY)] * 10 + [pl.BlockSpec(memory_space=pltpu.VMEM)],
        out_specs=[pl.BlockSpec(memory_space=pltpu.VMEM)] * 2,
        scratch_shapes=[
            pltpu.VMEM((tokens, wide), low),
            pltpu.VMEM((tokens, wide), low),
            pltpu.VMEM((3, tokens, width), low),
            pltpu.VMEM((5, tokens, width), low),
            pltpu.VMEM((width, tokens), low),
            pltpu.VMEM((width, width), jnp.float32),
            pltpu.VMEM((many - 1, 2, na, nz, ny) + one, low),
            pltpu.VMEM((2, na, nz, ny) + tile, jnp.float32),
            [pltpu.VMEM((many - 1,) + land + one, low) for land in lands],
            [pltpu.VMEM(land + tile, jnp.float32) for land in lands],
            dma((10,)),
        ]
        + [dma((many, na, nz))] * 2
        + [dma((many, nm, max(nz, na)))] * 2
        + [dma((many, nm))] * 2
        + [dma((many, nz))] * 2,
        compiler_params=pltpu.CompilerParams(collective_id=2, has_side_effects=True, vmem_limit_bytes=63 << 20),
        name="scatter_grads",
    )(*factors, lines.reshape((na, 2, nz, ny) + tile))


H = 12
HEAD = 64
PAIR = 2 * HEAD
MASKED = -1e30


def dot_last(x, y):
    return lax.dot_general(x, y, (((1,), (1,)), ((), ())), preferred_element_type=jnp.float32)


def dot_plain(x, y):
    return jnp.dot(x, y, preferred_element_type=jnp.float32)


def one_side(block, side, scale=1.0):
    lane = lax.broadcasted_iota(jnp.int32, (1, PAIR), 1)
    keep = (lane // HEAD == side).astype(jnp.float32) * scale
    return (block.astype(jnp.float32) * keep).astype(jnp.bfloat16)


FAR = 1 << 24


def item_at(lengths, place):
    first, last, end = jnp.zeros_like(place), jnp.full_like(place, FAR), 0
    for n in range(lengths.shape[1]):
        end = end + lengths[0, n]
        first = jnp.where(end <= place, end, first)
        last = jnp.where(end > place, jnp.minimum(last, end), last)
    return first, last, end


def span(lengths, start, tile, base, step, most):
    low = item_at(lengths, start)[0] - base
    high = item_at(lengths, start + tile - 1)[1] - base
    return jnp.maximum(low, 0) // step, jnp.minimum((high + step - 1) // step, most)


def items_of(lengths, start, count):
    place = start + lax.broadcasted_iota(jnp.int32, (1, count), 1)
    first, last, end = item_at(lengths, place)
    inside = (place >= 0) & (place < end)
    return jnp.where(inside, first, FAR), jnp.where(inside, last, -1)


def allowed_pairs(first, last, base, shape):
    place = lax.broadcasted_iota(jnp.int32, shape, 0)
    return (place >= first - base) & (place < last - base)


def skewed(count, *stages):
    held = [None] * count
    for t in range(count + len(stages) - 1):
        for k, stage in enumerate(stages):
            n = t - k
            if 0 <= n < count:
                held[n] = stage(n) if k == 0 else stage(n, held[n])
    return tuple(held)


def attend_step(heads, carry, keys, values, allowed):
    cols = [slice(p * PAIR, (p + 1) * PAIR) for p in range(len(heads) // 2)]
    turned = [values[:, c].T for c in cols]

    def score(n):
        return jnp.where(allowed, dot_last(keys[:, cols[n // 2]], heads[n]), MASKED)

    def soften(n, scores):
        top, total, acc = carry(n)
        peak = jnp.maximum(top, jnp.max(scores, axis=0, keepdims=True))
        lifted = jnp.exp(scores - peak)
        fade = jnp.exp(top - peak)
        return peak, total * fade + jnp.sum(lifted, axis=0, keepdims=True), acc * fade, lifted.astype(jnp.bfloat16)

    def gather(n, soft):
        peak, total, acc, lifted = soft
        side = slice(n % 2 * HEAD, (n % 2 + 1) * HEAD)
        return peak, total, acc + dot_plain(turned[n // 2][side], lifted)

    return skewed(len(heads), score, soften, gather)


def attend_done(done, store):
    for p in range(len(done) // 2):
        (top0, total0, acc0), (top1, total1, acc1) = done[2 * p : 2 * p + 2]
        result = jnp.concatenate([acc0 / total0, acc1 / total1], axis=0).T
        store(p, result, top0 + jnp.log(total0), top1 + jnp.log(total1))


def attend_kernel(tile, step, lengths, query, keys, values, low, full, logsum):
    wide, width = keys.shape
    tokens = wide // (2 * REACH + 1)
    base = (lax.axis_index("rows") - REACH) * tokens
    start = base + REACH * tokens + pl.program_id(0) * tile
    cols = [slice(p * PAIR, (p + 1) * PAIR) for p in range(width // PAIR)]
    heads = [one_side(query[:, c], s, HEAD**-0.5) for c in cols for s in range(2)]
    first, last = items_of(lengths, start, tile)

    def body(j, carry):
        block = pl.ds(pl.multiple_of(j * step, step), step)
        allowed = allowed_pairs(first, last, base + j * step, (step, tile))
        return attend_step(heads, lambda n: carry[n], keys.at[block], values.at[block], allowed)

    empty = tuple(
        (
            jnp.full((1, tile), MASKED, jnp.float32),
            jnp.zeros((1, tile), jnp.float32),
            jnp.zeros((HEAD, tile), jnp.float32),
        )
        for _ in heads
    )

    def store(p, result, sum0, sum1):
        low[:, cols[p]] = result.astype(jnp.bfloat16)
        full[:, cols[p]] = result
        logsum[2 * p] = sum0
        logsum[2 * p + 1] = sum1

    attend_done(lax.fori_loop(*span(lengths, start, tile, base, step, wide // step), body, empty), store)


def own_tile(n, tile, tiles, width):
    return pl.BlockSpec((None, tile, width), lambda i, b: (n, REACH * tiles + i, 0))


def window_of(n, wide, width):
    return pl.BlockSpec((None, wide, width), lambda i, b: (n, 0, 0))


def tile_of(tile, width):
    return pl.BlockSpec((tile, width), lambda i, b: (i, 0))


def lines(tile):
    return pl.BlockSpec((H, 1, tile), lambda i, b: (0, 0, i))


def cost(matmuls):
    return pl.CostEstimate(flops=matmuls * 2 * H * HEAD * 512 * 1536, bytes_accessed=12 << 20, transcendentals=0)


VMEM = pltpu.CompilerParams(vmem_limit_bytes=56 << 20)


def attend(lengths, projected, tile, step):
    _, wide, width = projected.shape
    tokens = wide // (2 * REACH + 1)
    tiles = tokens // tile
    return pl.pallas_call(
        functools.partial(attend_kernel, tile, step),
        grid_spec=pltpu.PrefetchScalarGridSpec(
            num_scalar_prefetch=1,
            grid=(tiles,),
            in_specs=[own_tile(0, tile, tiles, width), window_of(1, wide, width), window_of(2, wide, width)],
            out_specs=[tile_of(tile, width), tile_of(tile, width), lines(tile)],
        ),
        out_shape=[
            jax.ShapeDtypeStruct((tokens, width), jnp.bfloat16),
            jax.ShapeDtypeStruct((tokens, width), jnp.float32),
            jax.ShapeDtypeStruct((H, 1, tokens), jnp.float32),
        ],
        compiler_params=VMEM,
        cost_estimate=cost(2),
        name="attend",
    )(lengths, projected, projected, projected)


def query_grad_kernel(tile, step, lengths, query, grad, keys, values, logsum, centre, out):
    wide, width = keys.shape
    tokens = wide // (2 * REACH + 1)
    base = (lax.axis_index("rows") - REACH) * tokens
    start = base + REACH * tokens + pl.program_id(0) * tile
    cols = [slice(p * PAIR, (p + 1) * PAIR) for p in range(width // PAIR)]
    heads = [
        (c, s, one_side(query[:, c], s, HEAD**-0.5), one_side(grad[:, c], s), logsum[2 * p + s], centre[2 * p + s])
        for p, c in enumerate(cols)
        for s in range(2)
    ]
    first, last = items_of(lengths, start, tile)

    def body(j, carry):
        block = pl.ds(pl.multiple_of(j * step, step), step)
        allowed = allowed_pairs(first, last, base + j * step, (step, tile))
        turned = [keys[block, c].T for c in cols]

        def score(n):
            c, s, q, g, top, mid = heads[n]
            return dot_last(keys[block, c], q), dot_last(values[block, c], g)

        def soften(n, both):
            top, mid = heads[n][4:]
            weights = jnp.exp(jnp.where(allowed, both[0] - top, MASKED))
            return (weights * (both[1] - mid)).astype(jnp.bfloat16)

        def gather(n, d_scores):
            s = heads[n][1]
            return carry[n] + dot_plain(turned[n // 2][s * HEAD : (s + 1) * HEAD], d_scores)

        return skewed(len(heads), score, soften, gather)

    empty = tuple(jnp.zeros((HEAD, tile), jnp.float32) for _ in heads)
    done = lax.fori_loop(*span(lengths, start, tile, base, step, wide // step), body, empty)
    for p, c in enumerate(cols):
        both = jnp.concatenate(done[2 * p : 2 * p + 2], axis=0) * HEAD**-0.5
        out[:, c] = both.T.astype(jnp.bfloat16)


def query_grad(lengths, projected, grad, logsum, centre, tile, step):
    _, wide, width = projected.shape
    tokens = grad.shape[0]
    tiles = tokens // tile
    return pl.pallas_call(
        functools.partial(query_grad_kernel, tile, step),
        grid_spec=pltpu.PrefetchScalarGridSpec(
            num_scalar_prefetch=1,
            grid=(tiles,),
            in_specs=[
                own_tile(0, tile, tiles, width), tile_of(tile, width),
                window_of(1, wide, width), window_of(2, wide, width), lines(tile), lines(tile),
            ],
            out_specs=tile_of(tile, width),
        ),
        out_shape=jax.ShapeDtypeStruct((tokens, width), jnp.bfloat16),
        compiler_params=VMEM,
        cost_estimate=cost(3),
        name="query_grad",
    )(lengths, projected, grad, projected, projected, logsum, centre)


def key_grad_kernel(tile, step, lengths, keys, values, query, *refs):
    blocks = refs[: 2 * REACH + 1]
    d_keys, d_values, grad, arrived = refs[2 * REACH + 1 :]
    wide, width = query.shape
    tokens = wide // (2 * REACH + 1)
    base = (lax.axis_index("rows") - REACH) * tokens
    start = base + REACH * tokens + pl.program_id(0) * tile

    @pl.when(pl.program_id(0) == 0)
    def _():
        copies = [pltpu.make_async_copy(b, grad.at[k], arrived.at[k]) for k, b in enumerate(blocks)]
        for copy in copies:
            copy.start()
        for copy in copies:
            copy.wait()

    cols = [slice(p * PAIR, (p + 1) * PAIR) for p in range(width // PAIR)]
    heads = [(c, one_side(keys[:, c], s, HEAD**-0.5), one_side(values[:, c], s)) for c in cols for s in range(2)]
    many = len(heads)

    def body(j, carry):
        block = pl.ds(pl.multiple_of(j * step, step), step)
        of = j * step // tokens
        part = pl.ds(pl.multiple_of(j * step - of * tokens, step), step)
        first, last = items_of(lengths, base + j * step, step)
        allowed = allowed_pairs(first, last, start, (tile, step))
        stats = grad[of, part, width:].astype(jnp.float32).T
        stats = stats[: 2 * many] + stats[2 * many : 4 * many] + stats[4 * many : 6 * many]

        def score(n):
            c, k, v = heads[n]
            return dot_last(k, query[block, c]), dot_last(v, grad[of, part, c])

        def soften(n, both):
            weights = jnp.exp(jnp.where(allowed, both[0] - stats[n : n + 1], MASKED))
            d_scores = weights * (both[1] - stats[many + n : many + n + 1])
            return d_scores.astype(jnp.bfloat16), weights.astype(jnp.bfloat16)

        turned = [(query[block, c].T, grad[of, part, c].T) for c in cols]

        def gather(n, soft):
            side = slice(n % 2 * HEAD, (n % 2 + 1) * HEAD)
            q, g = turned[n // 2]
            return carry[n][0] + dot_last(q[side], soft[0]), carry[n][1] + dot_last(g[side], soft[1])

        return skewed(many, score, soften, gather)

    zero = jnp.zeros((HEAD, tile), jnp.float32)
    limits = span(lengths, start, tile, base, step, wide // step)
    done = lax.fori_loop(*limits, body, tuple((zero, zero) for _ in heads))
    for p, c in enumerate(cols):
        (k0, v0), (k1, v1) = done[2 * p : 2 * p + 2]
        d_keys[:, c] = (jnp.concatenate([k0, k1], axis=0) * HEAD**-0.5).T.astype(jnp.bfloat16)
        d_values[:, c] = jnp.concatenate([v0, v1], axis=0).T.astype(jnp.bfloat16)


def key_grad(lengths, projected, grads, tile, step):
    _, wide, width = projected.shape
    tokens = wide // (2 * REACH + 1)
    tiles = tokens // tile
    return pl.pallas_call(
        functools.partial(key_grad_kernel, tile, step),
        grid_spec=pltpu.PrefetchScalarGridSpec(
            num_scalar_prefetch=1,
            grid=(tiles,),
            in_specs=[own_tile(1, tile, tiles, width), own_tile(2, tile, tiles, width), window_of(0, wide, width)]
            + [pl.BlockSpec(memory_space=pl.ANY)] * (2 * REACH + 1),
            out_specs=[tile_of(tile, width)] * 2,
            scratch_shapes=[
                pltpu.VMEM((2 * REACH + 1,) + grads[0].shape, jnp.bfloat16), pltpu.SemaphoreType.DMA((2 * REACH + 1,))
            ],
        ),
        out_shape=[jax.ShapeDtypeStruct((tokens, width), jnp.bfloat16)] * 2,
        compiler_params=VMEM,
        cost_estimate=cost(4),
        name="key_grad",
    )(lengths, projected, projected, projected, *grads)


eps_norm = 1e-06
AXES = ("items", "rows")


NAMES = (
    "query_proj", "key_proj", "value_proj", "query_bias", "value_bias", "output_proj", "output_bias", "attn_gain",
    "attn_shift", "hidden_proj", "hidden_bias", "return_proj", "return_bias", "final_gain", "final_shift",
)


def dot_rows(matrix, factor):
    return lax.dot_general(matrix, factor, (((0,), (0,)), ((), ())), preferred_element_type=jnp.float32)


def layer_norm(hidden, norm_gain, norm_shift):
    row_mean = jnp.mean(hidden, axis=1, keepdims=True)
    centred = hidden - row_mean
    row_var = jnp.mean(centred * centred, axis=1, keepdims=True)
    return centred * lax.rsqrt(row_var + eps_norm) * norm_gain + norm_shift


def shifted(value, by):
    peers = lax.axis_size("rows")
    pairs = [(i, i + by) for i in range(peers) if 0 <= i + by < peers]
    return lax.ppermute(value, "rows", pairs)


def halo(value):
    return [value if d == 0 else shifted(value, -d) for d in range(-REACH, REACH + 1)]


def in_thirds(value, width):
    high = lax.reduce_precision(value, 8, 7)
    middle = lax.reduce_precision(value - high, 8, 7)
    pieces = jnp.concatenate([high, middle, value - high - middle], axis=1)
    return jnp.pad(pieces, ((0, 0), (0, width - pieces.shape[1]))).astype(jnp.bfloat16)


TILE, STEP = 256, 256


def per_device(mesh_shape, tokens, *given):
    names = NAMES
    part = dict(zip(names, given[:15]))
    item_lengths, out_grad = given[15:]
    matrices = ["query_proj", "key_proj", "value_proj", "output_proj", "hidden_proj", "return_proj"]
    vectors = [n for n in names if n not in matrices]
    outer = [n for n in vectors if n != "hidden_bias"]
    ndev = mesh_shape["items"] * mesh_shape["rows"]
    rows_dev, width = tokens.shape
    aligned = all(part[n].shape[0] % 8 == 0 for n in matrices) and all(part[n].shape[0] <= 128 for n in vectors)
    sizes = [part[n].shape[0] for n in vectors]
    used = sum(sizes)
    padded = -(-used // 1024) * 1024
    W = {}
    if aligned:
        got = gather_all(
            mesh_shape, item_lengths, tokens, [part[n] for n in matrices], [part[n] for n in outer + ["hidden_bias"]], TILE
        )
        wholes = [g.reshape((-1,) + g.shape[2:]) for g in got[: len(matrices)]]
        for k, n in enumerate(outer):
            W[n] = got[-6][k : k + 1]
        W["hidden_bias"] = got[-5]
        projected, attended, attended_full, logsum = got[-4:]
    else:
        wholes = [lax.all_gather(part[n], AXES, axis=0, tiled=True) for n in matrices]
        flat = lax.all_gather(jnp.concatenate([part[n] for n in vectors]), AXES, axis=0, tiled=False)
        at = 0
        for n, size in zip(vectors, sizes):
            W[n] = flat[:, at : at + size].reshape(1, -1).astype(jnp.float32)
            at += size
        window = jnp.concatenate(halo(tokens))
        query_wide = (dot_plain(window, wholes[0]) + W["query_bias"]).astype(jnp.bfloat16)
        keys_wide = dot_plain(window, wholes[1]).astype(jnp.bfloat16)
        values_wide = (dot_plain(window, wholes[2]) + W["value_bias"]).astype(jnp.bfloat16)
        projected = jnp.stack([query_wide, keys_wide, values_wide])
        attended, attended_full, logsum = attend(item_lengths, projected, TILE, STEP)
    W.update(zip(matrices, wholes))

    mixed = tokens.astype(jnp.float32) + (dot_plain(attended, W["output_proj"]) + W["output_bias"])
    normed, attn_back = jax.vjp(layer_norm, mixed, W["attn_gain"], W["attn_shift"])
    normed_low = normed.astype(jnp.bfloat16)
    hidden_pre = dot_plain(normed_low, W["hidden_proj"]) + W["hidden_bias"]
    cdf = 0.5 * (1.0 + lax.erf(hidden_pre * (0.5**0.5)))
    active = (hidden_pre * cdf).astype(jnp.bfloat16)
    slope = cdf + hidden_pre * jnp.exp(-0.5 * hidden_pre * hidden_pre) * 0.3989422804014327
    second = normed + (dot_plain(active, W["return_proj"]) + W["return_bias"])
    result, final_back = jax.vjp(layer_norm, second, W["final_gain"], W["final_shift"])

    grads = {}
    d_second, grads["final_gain"], grads["final_shift"] = final_back(out_grad.astype(jnp.float32))
    d_ffn = d_second.astype(jnp.bfloat16)
    grads["return_bias"] = jnp.sum(d_ffn.astype(jnp.float32), axis=0)
    d_hidden = (dot_last(d_ffn, W["return_proj"]) * slope).astype(jnp.bfloat16)
    grads["hidden_bias"] = jnp.sum(d_hidden.astype(jnp.float32), axis=0)
    d_normed = dot_last(d_hidden, W["hidden_proj"]) + d_second
    d_mixed, grads["attn_gain"], grads["attn_shift"] = attn_back(d_normed)
    d_branch = d_mixed.astype(jnp.bfloat16)
    grads["output_bias"] = jnp.sum(d_branch.astype(jnp.float32), axis=0)
    d_attended = dot_last(d_branch, W["output_proj"]).astype(jnp.bfloat16)

    lanes = jnp.arange(width, dtype=jnp.int32)[None, :] // HEAD == jnp.arange(16, dtype=jnp.int32)[:, None]
    product = d_attended.astype(jnp.float32) * attended_full
    lanes = lanes.astype(jnp.float32)
    highest = lax.Precision.HIGHEST
    centre = lax.dot_general(lanes, product, (((1,), (1,)), ((), ())), precision=highest)[:H, None]
    stats = jnp.concatenate([logsum[:, 0], centre[:, 0]]).T
    grad_blocks = halo(jnp.concatenate([d_attended, in_thirds(stats, PAIR)], axis=1))
    d_query = query_grad(item_lengths, projected, d_attended, logsum, centre, TILE, STEP)
    d_keys, d_values = key_grad(item_lengths, projected, grad_blocks, TILE, STEP)
    grads["query_bias"] = jnp.sum(d_query.astype(jnp.float32), axis=0)
    grads["value_bias"] = jnp.sum(d_values.astype(jnp.float32), axis=0)
    tokens_grad = (
        d_mixed
        + dot_last(d_query, W["query_proj"])
        + dot_last(d_keys, W["key_proj"])
        + dot_last(d_values, W["value_proj"])
    )

    rows_of = jnp.concatenate([grads[n].reshape(ndev, size) for n, size in zip(vectors, sizes)], axis=1)
    rows_of = jnp.pad(rows_of, ((0, 0), (0, padded - used))).reshape(ndev, 8, padded // 8)
    factors = (
        active, d_ffn, normed_low, d_hidden, attended, d_branch, tokens, d_query, d_keys, d_values
    )
    order = ("hidden_proj", "return_proj", "output_proj", "query_proj", "key_proj", "value_proj")
    if aligned:
        chunks, tile = scatter_all(mesh_shape, factors, rows_of)
        blocks = d_hidden.shape[1] // width
        sums = [
            jnp.concatenate([chunks[k] for k in range(blocks)], axis=1),
            chunks[blocks : 2 * blocks].reshape(-1, width),
        ] + [chunks[2 * blocks + k] for k in range(4)] + [tile]
    else:
        pairs = ((2, 3), (0, 1), (4, 5), (6, 7), (6, 8), (6, 9))
        low = [dot_rows(factors[i], factors[j]).astype(jnp.bfloat16) for i, j in pairs]
        low = [g.reshape((ndev, -1) + g.shape[1:]) for g in low] + [rows_of]
        sums = [lax.psum_scatter(g, AXES, scatter_dimension=0, tiled=True)[0] for g in low]
    total = {n: s.astype(jnp.float32) for n, s in zip(order, sums)}
    line = sums[-1].reshape(padded)
    at = 0
    for n, size in zip(vectors, sizes):
        total[n] = line[at : at + size]
        at += size
    return (result.astype(jnp.bfloat16), tokens_grad) + tuple(total[n] for n in names)


def solution(mesh):
    both = P(AXES)
    return jax.shard_map(
        functools.partial(per_device, dict(mesh.shape)),
        mesh=mesh,
        in_specs=(both,) * 16 + (P("items"), both),
        out_specs=(both,) * 17,
        check_vma=False,
    )
```

```python
import functools
import jax
import jax.numpy as jnp
from jax import lax
from jax.experimental import pallas as pl
from jax.experimental.pallas import tpu as pltpu

from jax.sharding import PartitionSpec as P

MESH = pl.DeviceIdType.MESH
REACH = 2


def split_rows(rows):
    inner = 1
    while (2 * inner) ** 2 <= rows:
        inner *= 2
    return rows // inner, inner


def place(nz, ny):
    item, row = lax.axis_index("items"), lax.axis_index("rows")
    return item // 2, item % 2, row // ny, row % ny


def near(z, step, nz):
    way = 1 - 2 * (z // ((nz + 1) // 2))
    return lax.rem(z + way * step + nz * 2, nz)


def spread_row(tiles, n, size):
    devices = tiles.shape[0]
    column = lax.broadcasted_iota(jnp.int32, (1, devices * size), 1).astype(jnp.float32)
    owner = jnp.floor((column + 0.5) / size)
    lane = lax.broadcasted_iota(jnp.int32, (tiles.shape[2], 1), 0).astype(jnp.float32)
    pick = (column - owner * size == lane).astype(jnp.float32).astype(jnp.bfloat16)
    spread = jnp.dot(tiles[:, n, :].astype(jnp.bfloat16), pick, preferred_element_type=jnp.float32)
    device = lax.broadcasted_iota(jnp.int32, (devices, 1), 0).astype(jnp.float32)
    return jnp.sum(jnp.where(owner == device, spread, 0.0), axis=0, keepdims=True)


def gather_kernel(na, nz, ny, sizes, *refs):
    weights = 6
    count = weights + 1
    lengths, tokens = refs[:2]
    refs = refs[1:]
    mine = list(refs[1 : 1 + weights])
    lines = refs[1 + weights : 1 + weights + len(sizes)]
    refs = refs[1 + weights + len(sizes) :]
    full = list(refs[:weights])
    rows_out, last_out, wide, low, full_low, logsum = refs[weights : weights + 6]
    (
        packed, tiles, window, matrix, bias, made, sided, top, total, acc, bounds, out_sem, load_sem, halo_send, halo_recv, local_sem,
        s1, r1, s2, r2, s3, r3, s4, r4,
    ) = refs[weights + 6 :]
    mine.append(packed)
    full.append(tiles)
    packed[...] = jnp.zeros_like(packed)
    for n, line in enumerate(lines):
        packed[n : n + 1, : line.shape[1]] = line[...].astype(jnp.float32)

    a, c, z, y = place(nz, ny)
    rows = nz * ny
    row = z * ny + y
    item = a * 2 + c

    def slot(a_, z_, y_):
        return (a_ * 2 + c) * rows + z_ * ny + y_

    barrier = pltpu.get_barrier_semaphore()

    def greet(i_, r_):
        pl.semaphore_signal(barrier, inc=1, device_id=(i_, r_), device_id_type=MESH)

    for d in range(1, nz):
        greet(item, near(z, d, nz) * ny + y)
    for d in range(1, ny):
        greet(item, z * ny + lax.rem(y + d, ny))
    for d in range(1, na):
        greet(lax.rem(a + d, na) * 2 + c, row)
    greet(a * 2 + 1 - c, row)
    for d in range(-REACH, REACH + 1):
        if d != 0:
            greet(item, lax.rem(row + d + rows, rows))
    pl.semaphore_wait(barrier, nz + ny + na - 2 + 2 * REACH)

    def remote(src, dst, send, recv, i_, r_):
        return pltpu.make_async_remote_copy(
            src_ref=src, dst_ref=dst, send_sem=send, recv_sem=recv, device_id=(i_, r_), device_id_type=MESH
        )

    def arrived(part, recv):
        remote(part, part, s1.at[0, 0], recv, item, row).wait_recv()

    soon, later = (0, 1, 2, weights), (3, 4, 5)
    for group in (soon, later):
        for d in range(1, nz):
            for n in group:
                remote(
                    mine[n], full[n].at[slot(a, z, y)], s1.at[d, n], r1.at[z, n], item, near(z, d, nz) * ny + y
                ).start()
    locals_ = [pltpu.make_async_copy(mine[n], full[n].at[slot(a, z, y)], local_sem.at[n]) for n in range(count)]
    locals_.append(pltpu.make_async_copy(tokens, window.at[REACH], local_sem.at[count]))
    for copy in locals_:
        copy.start()

    def halo_at(k):
        beside = 1 - 2 * lax.rem(y, 2)
        two = (k * (3 - k)) // 2
        return (1 - two) * beside * (1 - 2 * (k // 3)) + two * 2 * (3 - 2 * k)

    def halo(d, start):
        k = d + REACH

        @pl.when((row + d >= 0) & (row + d < rows))
        def _():
            if start:
                remote(
                    tokens, window.at[REACH - d], halo_send.at[k], halo_recv.at[REACH - d], item, row + d
                ).start()
            else:
                part = window.at[k]
                arrived(part, halo_recv.at[k])

        @pl.when((row + d < 0) | (row + d >= rows))
        def _():
            copy = pltpu.make_async_copy(tokens, window.at[k], halo_recv.at[k])
            if start:
                copy.start()
            else:
                copy.wait()

    def second(step, group):
        zz = near(z, step, nz)
        for n in group:
            part = full[n].at[slot(a, zz, y)]
            if step:
                arrived(part, r1.at[zz, n])
            for d in range(1, ny):
                remote(
                    part if step else mine[n], part, s2.at[step, d, n], r2.at[zz, y, n], item, z * ny + lax.rem(y + d, ny)
                ).start()

    def third(step, group):
        zz = near(z, step, nz)
        for n in group:
            for d in range(1, ny):
                yy = lax.rem(y + d, ny)
                arrived(full[n].at[slot(a, zz, yy)], r2.at[zz, yy, n])
            if isinstance(step, int) and step == 0:
                locals_[n].wait()
            block = full[n].at[pl.ds(slot(a, zz, 0), ny)]
            for d in range(1, na):
                remote(
                    block, block, s3.at[step, d, n], r3.at[zz, a, n], lax.rem(a + d, na) * 2 + c, row
                ).start()

    def fourth(step, group):
        zz = near(z, step, nz)
        for e in range(na):
            aa = lax.rem(a + e, na)
            for n in group:
                block = full[n].at[pl.ds(slot(aa, zz, 0), ny)]
                if e:
                    arrived(block, r3.at[zz, aa, n])
                remote(block, block, s4.at[e, step, n], r4.at[aa, zz, n], a * 2 + 1 - c, row).start()

    def settle(group):
        for n in group:
            for e in range(na):
                for step in range(nz):
                    theirs = full[n].at[pl.ds((e * 2 + 1 - c) * rows + step * ny, ny)]
                    arrived(theirs, r4.at[e, step, n])

    loads = [
        pltpu.make_async_copy(full[n], matrix.at[n], load_sem.at[n]) for n in range(3)
    ]
    def store(block, n):
        rows_dev = tokens.shape[0]
        return pltpu.make_async_copy(
            made.at[block, n], wide.at[n, pl.ds(block * rows_dev, rows_dev)], out_sem.at[block, n]
        )

    def project(block):
        @pl.loop(0, 3)
        def _(n):
            factor = matrix[n].reshape(tokens.shape[1], tokens.shape[1])
            total = jnp.dot(window[block], factor, preferred_element_type=jnp.float32)
            made[block, n] = (total + bias[n]).astype(jnp.bfloat16)
            store(block, n).start()

    second(0, soon)
    second(0, later)
    for t in range(1, nz):
        second(t, soon)
        third(t - 1, soon)
    third(nz - 1, soon)
    third(0, later)
    halo(halo_at(0), True)
    second(1, later)
    halo(halo_at(1), True)
    halo(halo_at(2), True)
    for t in range(nz):
        fourth(t, soon)
    for t in range(2, nz):
        second(t, later)
    halo(halo_at(3), True)
    settle(soon)
    for load in loads:
        load.start()
    for n, size in enumerate(sizes[:-1]):
        rows_out[n : n + 1] = spread_row(tiles, n, size)
    last_out[...] = spread_row(tiles, len(sizes) - 1, sizes[-1])
    bias[0] = rows_out[0:1]
    bias[1] = jnp.zeros_like(bias[1])
    bias[2] = rows_out[1:2]
    locals_[count].wait()
    for load in loads:
        load.wait()

    rows_dev = tokens.shape[0]
    tile = acc.shape[3]
    spans = rows_dev // tile
    base = (row - REACH) * rows_dev
    pairs = tokens.shape[1] // PAIR
    top[...] = jnp.full_like(top, MASKED)
    total[...] = jnp.zeros_like(total)
    acc[...] = jnp.zeros_like(acc)
    for i in range(spans):
        bounds[i, 0], bounds[i, 1] = items_of(lengths, base + REACH * rows_dev + i * tile, tile)

    def visit(block, half, i):
        part = pl.ds(pl.multiple_of(half * tile, tile), tile)
        allowed = allowed_pairs(
            bounds[i, 0], bounds[i, 1], base + block * rows_dev + half * tile, (tile, tile)
        )
        done = attend_step(
            [sided[i, n] for n in range(2 * pairs)],
            lambda n: (top[i, n], total[i, n], acc[i, n]),
            made.at[block, 1, part], made.at[block, 2, part], allowed,
        )
        for n, (top_, total_, acc_) in enumerate(done):
            top[i, n] = top_
            total[i, n] = total_
            acc[i, n] = acc_

    @pl.loop(0, 2 * REACH + 1)
    def _(k):
        away = halo_at(jnp.maximum(k - 1, 0)) * jnp.minimum(k, 1)
        block = REACH + away

        @pl.when(k + 1 < nz)
        def _():
            third(k + 1, later)

        @pl.when(k > 0)
        def _():
            halo(away, False)

        @pl.when((k > 0) & (k <= nz))
        def _():
            fourth(k - 1, later)

        project(block)

        @pl.when(k == 0)
        def _():
            for i in range(spans):
                for n in range(2 * pairs):
                    query = made[REACH, 0, i * tile : (i + 1) * tile, n // 2 * PAIR : (n // 2 + 1) * PAIR]
                    sided[i, n] = one_side(query, n % 2, HEAD**-0.5)

        @pl.loop(0, spans * spans)
        def _(m):
            i, half = m // spans, lax.rem(m, spans)
            step = block * spans + half

            there = (row + away >= 0) & (row + away < rows)

            @pl.when(there & (step >= i) & (step <= 2 * REACH * spans + i))
            def _():
                visit(block, half, i)

    for t in range(2 * REACH + 2, nz):
        third(t, later)
    for t in range(2 * REACH, nz):
        fourth(t, later)
    for i in range(spans):
        mine_rows = slice(i * tile, (i + 1) * tile)

        def keep(p, result, sum0, sum1):
            c_ = slice(p * PAIR, (p + 1) * PAIR)
            low[mine_rows, c_] = result.astype(jnp.bfloat16)
            full_low[mine_rows, c_] = result
            logsum[2 * p, :, mine_rows] = sum0
            logsum[2 * p + 1, :, mine_rows] = sum1

        attend_done([(top[i, n], total[i, n], acc[i, n]) for n in range(2 * pairs)], keep)
    settle(later)

    for n in range(count):
        for step in range(nz):
            part = full[n].at[slot(a, z, y)]
            if step:
                remote(mine[n], part, s1.at[step, n], r1.at[z, n], item, row).wait_send()
            for d in range(1, ny):
                remote(part, part, s2.at[step, d, n], r2.at[z, y, n], item, row).wait_send()
            block = full[n].at[pl.ds(slot(a, z, 0), ny)]
            for d in range(1, na):
                remote(block, block, s3.at[step, d, n], r3.at[z, a, n], item, row).wait_send()
            for e in range(na):
                remote(block, block, s4.at[e, step, n], r4.at[0, 0, n], item, row).wait_send()
    for d in (1, -1, 2, -2):

        @pl.when((row + d >= 0) & (row + d < rows))
        def _():
            remote(
                tokens, window.at[REACH - d], halo_send.at[d + REACH], halo_recv.at[REACH - d], item, row
            ).wait_send()

    for block in range(2 * REACH + 1):
        for n in range(3):
            store(block, n).wait()


def gather_all(mesh_shape, lengths, tokens, shards, vectors, tile):
    na = mesh_shape["items"] // 2
    nz, ny = split_rows(mesh_shape["rows"])
    ndev = mesh_shape["items"] * mesh_shape["rows"]
    count = len(shards) + 1
    rows_dev, width = tokens.shape
    blocks = 2 * REACH + 1
    dma = pltpu.SemaphoreType.DMA
    packed = (-(-len(vectors) // 8) * 8, 128)
    sizes = tuple(v.shape[0] for v in vectors)
    wide = jax.ShapeDtypeStruct((3, blocks * rows_dev, width), tokens.dtype)
    hbm, vmem = pl.BlockSpec(memory_space=pl.ANY), pl.BlockSpec(memory_space=pltpu.VMEM)
    return pl.pallas_call(
        functools.partial(gather_kernel, na, nz, ny, sizes),
        out_shape=[jax.ShapeDtypeStruct((ndev,) + s.shape, s.dtype) for s in shards]
        + [jax.ShapeDtypeStruct((len(sizes) - 1, width), jnp.float32)]
        + [jax.ShapeDtypeStruct((1, ndev * sizes[-1]), jnp.float32), wide]
        + [jax.ShapeDtypeStruct(tokens.shape, tokens.dtype), jax.ShapeDtypeStruct(tokens.shape, jnp.float32)]
        + [jax.ShapeDtypeStruct((H, 1, rows_dev), jnp.float32)],
        in_specs=[pl.BlockSpec(memory_space=pltpu.SMEM)] + [vmem] * (count + len(vectors)),
        out_specs=[hbm] * len(shards) + [vmem, vmem, hbm, vmem, vmem, vmem],
        scratch_shapes=[
            pltpu.VMEM(packed, jnp.float32),
            pltpu.VMEM((ndev,) + packed, jnp.float32),
            pltpu.VMEM((blocks,) + tokens.shape, tokens.dtype),
            pltpu.VMEM((3, ndev) + shards[0].shape, tokens.dtype),
            pltpu.VMEM((3, 1, width), jnp.float32),
            pltpu.VMEM((blocks, 3) + tokens.shape, tokens.dtype),
            pltpu.VMEM((rows_dev // tile, H, tile, PAIR), tokens.dtype),
            pltpu.VMEM((rows_dev // tile, H, 1, tile), jnp.float32),
            pltpu.VMEM((rows_dev // tile, H, 1, tile), jnp.float32),
            pltpu.VMEM((rows_dev // tile, H, HEAD, tile), jnp.float32),
            pltpu.VMEM((rows_dev // tile, 2, 1, tile), jnp.int32),
            dma((blocks, 3)), dma((3,)),
            dma((blocks,)), dma((blocks,)), dma((count + 1,)),
            dma((nz, count)), dma((nz, count)),
            dma((nz, ny, count)), dma((nz, ny, count)),
            dma((nz, na, count)), dma((nz, na, count)),
            dma((na, nz, count)), dma((na, nz, count)),
        ],
        compiler_params=pltpu.CompilerParams(collective_id=1, has_side_effects=True, vmem_limit_bytes=60 << 20),
        name="gather_weights",
    )(lengths, tokens, *shards, *[v[None] for v in vectors])


def scatter_kernel(na, nz, ny, *refs):
    (
        active, d_ffn, normed, d_hidden, attended, d_branch, tokens, d_query, d_keys, d_values, d_mixed,
        query_proj, key_proj, value_proj, lines,
    ) = refs[:15]
    sums, sum_lines, tokens_grad = refs[15:18]
    (
        act, hid, left, right, factors, turned, product, parts, parts_lines, low, low_lines,
        given_sem, s0, r0, s1, r1, s2, r2, s3, r3,
    ) = refs[18:]
    a, c, z, y = place(nz, ny)
    rows = nz * ny
    row = z * ny + y
    item = a * 2 + c
    devices = 2 * na * rows
    width = left.shape[2]
    height = width // devices
    blocks = hid.shape[1] // width
    many = 2 * blocks + 5
    tile = many - 1

    loads = [
        pltpu.make_async_copy(src, dst, given_sem.at[n])
        for n, (src, dst) in enumerate(
            (
                (normed, left.at[0]), (d_hidden, hid), (active, act), (d_ffn, right.at[0]), (attended, left.at[1]),
                (d_branch, right.at[1]), (tokens, left.at[2]), (d_query, right.at[2]), (d_keys, right.at[3]),
                (d_values, right.at[4]), (d_mixed, tokens_grad), (query_proj, factors.at[0]), (key_proj, factors.at[1]),
                (value_proj, factors.at[2]),
            )
        )
    ]
    for load in loads:
        load.start()
    for side in range(2):
        for aa in range(na):
            parts_lines[side, aa] = lines[aa, side]

    barrier = pltpu.get_barrier_semaphore()

    def greet(i_, r_):
        pl.semaphore_signal(barrier, inc=1, device_id=(i_, r_), device_id_type=MESH)

    def at_z(d):
        return lax.rem(z + d, nz) * ny + y

    def at_y(d):
        return z * ny + lax.rem(y + d, ny)

    def at_a(d):
        return lax.rem(a + d, na) * 2 + c

    for d in range(1, nz):
        greet(item, at_z(d))
    for d in range(1, ny):
        greet(item, at_y(d))
    for d in range(1, na):
        greet(at_a(d), row)
    greet(a * 2 + 1 - c, row)
    pl.semaphore_wait(barrier, nz + ny + na - 2)

    def remote(src, dst, send, recv, i_, r_):
        return pltpu.make_async_remote_copy(
            src_ref=src, dst_ref=dst, send_sem=send, recv_sem=recv, device_id=(i_, r_), device_id_type=MESH
        )

    def is_tile(k):
        return isinstance(k, int) and k == tile

    def part(k, side):
        return parts_lines.at[side] if is_tile(k) else parts.at[k, side]

    def mine(k):
        return part(k, c)

    def landing(k, which):
        return low_lines[which] if is_tile(k) else low[which].at[k]

    def core(k, aa, zz):
        return remote(
            part(k, 1 - c).at[aa, zz], landing(k, 0).at[aa, zz], s0.at[k, aa, zz], r0.at[k, aa, zz], a * 2 + 1 - c, row
        )

    def send_core(k):
        for e in range(na):
            for zz in range(nz):
                core(k, lax.rem(a + 1 + e, na), zz).start()

    def first0(k, d, zz):
        aa = lax.rem(a + d, na)
        return remote(
            mine(k).at[aa, zz], landing(k, 1).at[pl.ds((d - 1) * rows + zz * ny, ny)],
            s1.at[k, d, zz], r1.at[k, d, zz], at_a(d), row,
        )

    def first1(k, d, aa):
        return remote(
            mine(k).at[aa, :, lax.rem(y + d, ny)], landing(k, 1).at[pl.ds((d - 1) * na * nz + aa * nz, nz)],
            s1.at[k, d, aa], r1.at[k, d, aa], item, at_y(d),
        )

    def second0(k, d):
        return remote(
            mine(k).at[a, :, lax.rem(y + d, ny)], landing(k, 2).at[pl.ds((d - 1) * nz, nz)],
            s2.at[k, d], r2.at[k, d], item, at_y(d),
        )

    def second1(k, d):
        return remote(
            mine(k).at[lax.rem(a + d, na), :, y], landing(k, 2).at[pl.ds((d - 1) * nz, nz)],
            s2.at[k, d], r2.at[k, d], at_a(d), row,
        )

    def third(k, d):
        return remote(
            mine(k).at[a, lax.rem(z + d, nz), y], landing(k, 3).at[d - 1], s3.at[k, d], r3.at[k, d], item, at_z(d)
        )

    def summed(refs_):
        total = refs_[0][...].astype(jnp.float32)
        for ref in refs_[1:]:
            total = total + ref[...].astype(jnp.float32)
        return total

    def add_into(dst, others):
        dst[...] = summed([dst] + others).astype(dst.dtype)

    def stage1(k):
        for e in range(na):
            aa = lax.rem(a + 1 + e, na)
            for zz in range(nz):
                core(k, aa, zz).wait_recv()

                add_into(mine(k).at[aa, zz], [landing(k, 0).at[aa, zz]])

                if e < na - 1:

                    @pl.when(c == 0)
                    def _():
                        first0(k, e + 1, zz).start()

        @pl.when(c == 1)
        def _():
            for d in range(1, ny):
                for aa in range(na):
                    first1(k, d, aa).start()

    def stage2(k):
        @pl.when(c == 0)
        def _():
            for zz in range(nz):
                for d in range(1, na):
                    first0(k, d, zz).wait_recv()

                add_into(
                    mine(k).at[a, zz], [landing(k, 1).at[pl.ds((d - 1) * rows + zz * ny, ny)] for d in range(1, na)]
                )

            for d in range(1, ny):
                second0(k, d).start()

        @pl.when(c == 1)
        def _():
            for d in range(1, ny):
                for aa in range(na):
                    first1(k, d, aa).wait_recv()
            for aa in range(na):

                add_into(
                    mine(k).at[aa, :, y],
                    [landing(k, 1).at[pl.ds((d - 1) * na * nz + aa * nz, nz)] for d in range(1, ny)],
                )

            for d in range(1, na):
                second1(k, d).start()

    def stage3(k):
        def rest(peers, second):
            for d in range(1, peers):
                second(k, d).wait_recv()

            add_into(mine(k).at[a, :, y], [landing(k, 2).at[pl.ds((d - 1) * nz, nz)] for d in range(1, peers)])

        @pl.when(c == 0)
        def _():
            rest(ny, second0)

        @pl.when(c == 1)
        def _():
            rest(na, second1)

        for d in range(1, nz):
            third(k, d).start()

    def stage4(k):
        for d in range(1, nz):
            third(k, d).wait_recv()
        total = summed([mine(k).at[a, z, y]] + [landing(k, 3).at[d - 1] for d in range(1, nz)])
        if is_tile(k):
            sum_lines[...] = total
        else:
            sums[k] = total

    def spread(k):
        @pl.loop(0, devices)
        def _(n):
            i_, r_ = n // rows, lax.rem(n, rows)
            parts[k, lax.rem(i_, 2), i_ // 2, r_ // ny, lax.rem(r_, ny)] = product[
                pl.ds(pl.multiple_of(n * height, 8), height)
            ].astype(parts.dtype)

    def times(factor):
        product[...] = jnp.dot(turned[...], factor, preferred_element_type=jnp.float32)

    def make_hidden(first, last):
        @pl.loop(first, last)
        def _(k):
            times(hid[:, pl.ds(pl.multiple_of(k * width, width), width)])
            spread(k)
            send_core(k)

    def make_return():
        @pl.loop(0, 2 * na)
        def _(i_):
            turned[...] = act[:, pl.ds(pl.multiple_of(i_ * width, width), width)].T
            times(right[0])

            @pl.loop(0, rows)
            def _(r_):
                for k in range(blocks):
                    parts[blocks + k, lax.rem(i_, 2), i_ // 2, r_ // ny, lax.rem(r_, ny)] = product[
                        pl.ds(pl.multiple_of((r_ * blocks + k) * height, 8), height)
                    ].astype(parts.dtype)

        for k in range(blocks):
            send_core(blocks + k)

    def make_rest():
        @pl.loop(0, 4)
        def _(n):
            turned[...] = left[jnp.minimum(n + 1, 2)].T
            times(right[n + 1])
            spread(2 * blocks + n)
            send_core(2 * blocks + n)

    send_core(tile)
    loads[0].wait()
    turned[...] = left[0].T
    loads[1].wait()
    make_hidden(0, 2)
    def beat(t):
        for n, stage in enumerate((stage1, stage2, stage3, stage4)):
            if not isinstance(t, int) or 0 <= t - n < many:
                stage(t - n)

    beat(0)
    make_hidden(2, blocks)
    beat(1)
    loads[2].wait()
    loads[3].wait()
    make_return()
    beat(2)

    @pl.loop(3, tile)
    def _(t):
        @pl.when(t == 4)
        def _():
            for load in loads[4:10]:
                load.wait()
            make_rest()

        beat(t)

        @pl.when(t == 6)
        def _():
            for load in loads[10:]:
                load.wait()

            @pl.loop(0, 3)
            def _(n):
                factor = factors[n].reshape(width, width)
                tokens_grad[...] += lax.dot_general(
                    right[n + 2], factor, (((1,), (1,)), ((), ())), preferred_element_type=jnp.float32
                )

    for t in range(tile, many + 3):
        beat(t)

    def finish(k):
        for aa in range(na):
            for zz in range(nz):
                core(k, aa, zz).wait_send()
        for d in range(1, nz):
            third(k, d).wait_send()

        @pl.when(c == 0)
        def _():
            for d in range(1, na):
                for zz in range(nz):
                    first0(k, d, zz).wait_send()
            for d in range(1, ny):
                second0(k, d).wait_send()

        @pl.when(c == 1)
        def _():
            for d in range(1, ny):
                for aa in range(na):
                    first1(k, d, aa).wait_send()
            for d in range(1, na):
                second1(k, d).wait_send()

    pl.loop(0, tile)(finish)
    finish(tile)


def scatter_all(mesh_shape, factors, d_mixed, projections, lines):
    na = mesh_shape["items"] // 2
    nz, ny = split_rows(mesh_shape["rows"])
    devices = 2 * na * nz * ny
    tokens, wide = factors[0].shape
    width = factors[1].shape[1]
    height = width // devices
    blocks = wide // width
    many = 2 * blocks + 5
    dma = pltpu.SemaphoreType.DMA
    nm = max(na, ny)
    low = jnp.bfloat16
    first = max((na - 1) * nz * ny, (ny - 1) * na * nz)
    second = (nm - 1) * nz
    lands = [(na, nz, ny), (first,), (second,), (nz - 1,)]
    one, tile = (height, width), lines.shape[1:]
    f32 = lambda *shape: jax.ShapeDtypeStruct(shape, jnp.float32)
    return pl.pallas_call(
        functools.partial(scatter_kernel, na, nz, ny),
        out_shape=[f32(many - 1, *one), f32(*tile), f32(tokens, width)],
        in_specs=[pl.BlockSpec(memory_space=pl.ANY)] * 14 + [pl.BlockSpec(memory_space=pltpu.VMEM)],
        out_specs=[pl.BlockSpec(memory_space=pltpu.VMEM)] * 3,
        scratch_shapes=[
            pltpu.VMEM((tokens, wide), low),
            pltpu.VMEM((tokens, wide), low),
            pltpu.VMEM((3, tokens, width), low),
            pltpu.VMEM((5, tokens, width), low),
            pltpu.VMEM((3, devices, height, width), low),
            pltpu.VMEM((width, tokens), low),
            pltpu.VMEM((width, width), jnp.float32),
            pltpu.VMEM((many - 1, 2, na, nz, ny) + one, low),
            pltpu.VMEM((2, na, nz, ny) + tile, jnp.float32),
            [pltpu.VMEM((many - 1,) + land + one, low) for land in lands],
            [pltpu.VMEM(land + tile, jnp.float32) for land in lands],
            dma((14,)),
        ]
        + [dma((many, na, nz))] * 2
        + [dma((many, nm, max(nz, na)))] * 2
        + [dma((many, nm))] * 2
        + [dma((many, nz))] * 2,
        compiler_params=pltpu.CompilerParams(collective_id=2, has_side_effects=True, vmem_limit_bytes=63 << 20),
        name="scatter_grads",
    )(*factors, d_mixed, *projections, lines.reshape((na, 2, nz, ny) + tile))


H = 12
HEAD = 64
PAIR = 2 * HEAD
MASKED = -1e30


def dot_last(x, y):
    return lax.dot_general(x, y, (((1,), (1,)), ((), ())), preferred_element_type=jnp.float32)


def dot_plain(x, y):
    return jnp.dot(x, y, preferred_element_type=jnp.float32)


def one_side(block, side, scale=1.0):
    lane = lax.broadcasted_iota(jnp.int32, (1, PAIR), 1)
    keep = (lane // HEAD == side).astype(jnp.float32) * scale
    return (block.astype(jnp.float32) * keep).astype(jnp.bfloat16)


FAR = 1 << 24


def item_at(lengths, place):
    first, last, end = jnp.zeros_like(place), jnp.full_like(place, FAR), 0
    for n in range(lengths.shape[1]):
        end = end + lengths[0, n]
        first = jnp.where(end <= place, end, first)
        last = jnp.where(end > place, jnp.minimum(last, end), last)
    return first, last, end


def span(lengths, start, tile, base, step, most):
    low = item_at(lengths, start)[0] - base
    high = item_at(lengths, start + tile - 1)[1] - base
    return jnp.maximum(low, 0) // step, jnp.minimum((high + step - 1) // step, most)


def items_of(lengths, start, count):
    place = start + lax.broadcasted_iota(jnp.int32, (1, count), 1)
    first, last, end = item_at(lengths, place)
    inside = (place >= 0) & (place < end)
    return jnp.where(inside, first, FAR), jnp.where(inside, last, -1)


def allowed_pairs(first, last, base, shape):
    place = lax.broadcasted_iota(jnp.int32, shape, 0)
    return (place >= first - base) & (place < last - base)


def skewed(count, *stages):
    held = [None] * count
    for t in range(count + len(stages) - 1):
        for k, stage in enumerate(stages):
            n = t - k
            if 0 <= n < count:
                held[n] = stage(n) if k == 0 else stage(n, held[n])
    return tuple(held)


def attend_step(heads, carry, keys, values, allowed):
    cols = [slice(p * PAIR, (p + 1) * PAIR) for p in range(len(heads) // 2)]
    turned = [values[:, c].T for c in cols]

    def score(n):
        return jnp.where(allowed, dot_last(keys[:, cols[n // 2]], heads[n]), MASKED)

    def soften(n, scores):
        top, total, acc = carry(n)
        peak = jnp.maximum(top, jnp.max(scores, axis=0, keepdims=True))
        lifted = jnp.exp(scores - peak)
        fade = jnp.exp(top - peak)
        return peak, total * fade + jnp.sum(lifted, axis=0, keepdims=True), acc * fade, lifted.astype(jnp.bfloat16)

    def gather(n, soft):
        peak, total, acc, lifted = soft
        side = slice(n % 2 * HEAD, (n % 2 + 1) * HEAD)
        return peak, total, acc + dot_plain(turned[n // 2][side], lifted)

    return skewed(len(heads), score, soften, gather)


def attend_done(done, store):
    for p in range(len(done) // 2):
        (top0, total0, acc0), (top1, total1, acc1) = done[2 * p : 2 * p + 2]
        result = jnp.concatenate([acc0 / total0, acc1 / total1], axis=0).T
        store(p, result, top0 + jnp.log(total0), top1 + jnp.log(total1))


def attend_kernel(tile, step, lengths, query, keys, values, low, full, logsum):
    wide, width = keys.shape
    tokens = wide // (2 * REACH + 1)
    base = (lax.axis_index("rows") - REACH) * tokens
    start = base + REACH * tokens + pl.program_id(0) * tile
    cols = [slice(p * PAIR, (p + 1) * PAIR) for p in range(width // PAIR)]
    heads = [one_side(query[:, c], s, HEAD**-0.5) for c in cols for s in range(2)]
    first, last = items_of(lengths, start, tile)

    def body(j, carry):
        block = pl.ds(pl.multiple_of(j * step, step), step)
        allowed = allowed_pairs(first, last, base + j * step, (step, tile))
        return attend_step(heads, lambda n: carry[n], keys.at[block], values.at[block], allowed)

    empty = tuple(
        (
            jnp.full((1, tile), MASKED, jnp.float32),
            jnp.zeros((1, tile), jnp.float32),
            jnp.zeros((HEAD, tile), jnp.float32),
        )
        for _ in heads
    )

    def store(p, result, sum0, sum1):
        low[:, cols[p]] = result.astype(jnp.bfloat16)
        full[:, cols[p]] = result
        logsum[2 * p] = sum0
        logsum[2 * p + 1] = sum1

    attend_done(lax.fori_loop(*span(lengths, start, tile, base, step, wide // step), body, empty), store)


def own_tile(n, tile, tiles, width):
    return pl.BlockSpec((None, tile, width), lambda i, b: (n, REACH * tiles + i, 0))


def window_of(n, wide, width):
    return pl.BlockSpec((None, wide, width), lambda i, b: (n, 0, 0))


def tile_of(tile, width):
    return pl.BlockSpec((tile, width), lambda i, b: (i, 0))


def lines(tile):
    return pl.BlockSpec((H, 1, tile), lambda i, b: (0, 0, i))


def cost(matmuls):
    return pl.CostEstimate(flops=matmuls * 2 * H * HEAD * 512 * 1536, bytes_accessed=12 << 20, transcendentals=0)


VMEM = pltpu.CompilerParams(vmem_limit_bytes=56 << 20)


def attend(lengths, projected, tile, step):
    _, wide, width = projected.shape
    tokens = wide // (2 * REACH + 1)
    tiles = tokens // tile
    return pl.pallas_call(
        functools.partial(attend_kernel, tile, step),
        grid_spec=pltpu.PrefetchScalarGridSpec(
            num_scalar_prefetch=1,
            grid=(tiles,),
            in_specs=[own_tile(0, tile, tiles, width), window_of(1, wide, width), window_of(2, wide, width)],
            out_specs=[tile_of(tile, width), tile_of(tile, width), lines(tile)],
        ),
        out_shape=[
            jax.ShapeDtypeStruct((tokens, width), jnp.bfloat16),
            jax.ShapeDtypeStruct((tokens, width), jnp.float32),
            jax.ShapeDtypeStruct((H, 1, tokens), jnp.float32),
        ],
        compiler_params=VMEM,
        cost_estimate=cost(2),
        name="attend",
    )(lengths, projected, projected, projected)


def query_grad_kernel(tile, step, lengths, query, grad, keys, values, logsum, centre, out):
    wide, width = keys.shape
    tokens = wide // (2 * REACH + 1)
    base = (lax.axis_index("rows") - REACH) * tokens
    start = base + REACH * tokens + pl.program_id(0) * tile
    cols = [slice(p * PAIR, (p + 1) * PAIR) for p in range(width // PAIR)]
    heads = [
        (c, s, one_side(query[:, c], s, HEAD**-0.5), one_side(grad[:, c], s), logsum[2 * p + s], centre[2 * p + s])
        for p, c in enumerate(cols)
        for s in range(2)
    ]
    first, last = items_of(lengths, start, tile)

    def body(j, carry):
        block = pl.ds(pl.multiple_of(j * step, step), step)
        allowed = allowed_pairs(first, last, base + j * step, (step, tile))
        turned = [keys[block, c].T for c in cols]

        def score(n):
            c, s, q, g, top, mid = heads[n]
            return dot_last(keys[block, c], q), dot_last(values[block, c], g)

        def soften(n, both):
            top, mid = heads[n][4:]
            weights = jnp.exp(jnp.where(allowed, both[0] - top, MASKED))
            return (weights * (both[1] - mid)).astype(jnp.bfloat16)

        def gather(n, d_scores):
            s = heads[n][1]
            return carry[n] + dot_plain(turned[n // 2][s * HEAD : (s + 1) * HEAD], d_scores)

        return skewed(len(heads), score, soften, gather)

    empty = tuple(jnp.zeros((HEAD, tile), jnp.float32) for _ in heads)
    done = lax.fori_loop(*span(lengths, start, tile, base, step, wide // step), body, empty)
    for p, c in enumerate(cols):
        both = jnp.concatenate(done[2 * p : 2 * p + 2], axis=0) * HEAD**-0.5
        out[:, c] = both.T.astype(jnp.bfloat16)


def query_grad(lengths, projected, grad, logsum, centre, tile, step):
    _, wide, width = projected.shape
    tokens = grad.shape[0]
    tiles = tokens // tile
    return pl.pallas_call(
        functools.partial(query_grad_kernel, tile, step),
        grid_spec=pltpu.PrefetchScalarGridSpec(
            num_scalar_prefetch=1,
            grid=(tiles,),
            in_specs=[
                own_tile(0, tile, tiles, width), tile_of(tile, width),
                window_of(1, wide, width), window_of(2, wide, width), lines(tile), lines(tile),
            ],
            out_specs=tile_of(tile, width),
        ),
        out_shape=jax.ShapeDtypeStruct((tokens, width), jnp.bfloat16),
        compiler_params=VMEM,
        cost_estimate=cost(3),
        name="query_grad",
    )(lengths, projected, grad, projected, projected, logsum, centre)


def key_grad_kernel(tile, step, lengths, keys, values, query, *refs):
    blocks = refs[: 2 * REACH + 1]
    d_keys, d_values, grad, arrived = refs[2 * REACH + 1 :]
    wide, width = query.shape
    tokens = wide // (2 * REACH + 1)
    base = (lax.axis_index("rows") - REACH) * tokens
    start = base + REACH * tokens + pl.program_id(0) * tile

    @pl.when(pl.program_id(0) == 0)
    def _():
        copies = [pltpu.make_async_copy(b, grad.at[k], arrived.at[k]) for k, b in enumerate(blocks)]
        for copy in copies:
            copy.start()
        for copy in copies:
            copy.wait()

    cols = [slice(p * PAIR, (p + 1) * PAIR) for p in range(width // PAIR)]
    heads = [(c, one_side(keys[:, c], s, HEAD**-0.5), one_side(values[:, c], s)) for c in cols for s in range(2)]
    many = len(heads)

    def body(j, carry):
        block = pl.ds(pl.multiple_of(j * step, step), step)
        of = j * step // tokens
        part = pl.ds(pl.multiple_of(j * step - of * tokens, step), step)
        first, last = items_of(lengths, base + j * step, step)
        allowed = allowed_pairs(first, last, start, (tile, step))
        stats = grad[of, part, width:].astype(jnp.float32).T
        stats = stats[: 2 * many] + stats[2 * many : 4 * many] + stats[4 * many : 6 * many]

        def score(n):
            c, k, v = heads[n]
            return dot_last(k, query[block, c]), dot_last(v, grad[of, part, c])

        def soften(n, both):
            weights = jnp.exp(jnp.where(allowed, both[0] - stats[n : n + 1], MASKED))
            d_scores = weights * (both[1] - stats[many + n : many + n + 1])
            return d_scores.astype(jnp.bfloat16), weights.astype(jnp.bfloat16)

        turned = [(query[block, c].T, grad[of, part, c].T) for c in cols]

        def gather(n, soft):
            side = slice(n % 2 * HEAD, (n % 2 + 1) * HEAD)
            q, g = turned[n // 2]
            return carry[n][0] + dot_last(q[side], soft[0]), carry[n][1] + dot_last(g[side], soft[1])

        return skewed(many, score, soften, gather)

    zero = jnp.zeros((HEAD, tile), jnp.float32)
    limits = span(lengths, start, tile, base, step, wide // step)
    done = lax.fori_loop(*limits, body, tuple((zero, zero) for _ in heads))
    for p, c in enumerate(cols):
        (k0, v0), (k1, v1) = done[2 * p : 2 * p + 2]
        d_keys[:, c] = (jnp.concatenate([k0, k1], axis=0) * HEAD**-0.5).T.astype(jnp.bfloat16)
        d_values[:, c] = jnp.concatenate([v0, v1], axis=0).T.astype(jnp.bfloat16)


def key_grad(lengths, projected, grads, tile, step):
    _, wide, width = projected.shape
    tokens = wide // (2 * REACH + 1)
    tiles = tokens // tile
    return pl.pallas_call(
        functools.partial(key_grad_kernel, tile, step),
        grid_spec=pltpu.PrefetchScalarGridSpec(
            num_scalar_prefetch=1,
            grid=(tiles,),
            in_specs=[own_tile(1, tile, tiles, width), own_tile(2, tile, tiles, width), window_of(0, wide, width)]
            + [pl.BlockSpec(memory_space=pl.ANY)] * (2 * REACH + 1),
            out_specs=[tile_of(tile, width)] * 2,
            scratch_shapes=[
                pltpu.VMEM((2 * REACH + 1,) + grads[0].shape, jnp.bfloat16), pltpu.SemaphoreType.DMA((2 * REACH + 1,))
            ],
        ),
        out_shape=[jax.ShapeDtypeStruct((tokens, width), jnp.bfloat16)] * 2,
        compiler_params=VMEM,
        cost_estimate=cost(4),
        name="key_grad",
    )(lengths, projected, projected, projected, *grads)


eps_norm = 1e-06
AXES = ("items", "rows")


NAMES = (
    "query_proj", "key_proj", "value_proj", "query_bias", "value_bias", "output_proj", "output_bias", "attn_gain",
    "attn_shift", "hidden_proj", "hidden_bias", "return_proj", "return_bias", "final_gain", "final_shift",
)


def dot_rows(matrix, factor):
    return lax.dot_general(matrix, factor, (((0,), (0,)), ((), ())), preferred_element_type=jnp.float32)


def layer_norm(hidden, norm_gain, norm_shift):
    row_mean = jnp.mean(hidden, axis=1, keepdims=True)
    centred = hidden - row_mean
    row_var = jnp.mean(centred * centred, axis=1, keepdims=True)
    return centred * lax.rsqrt(row_var + eps_norm) * norm_gain + norm_shift


def shifted(value, by):
    peers = lax.axis_size("rows")
    pairs = [(i, i + by) for i in range(peers) if 0 <= i + by < peers]
    return lax.ppermute(value, "rows", pairs)


def halo(value):
    return [value if d == 0 else shifted(value, -d) for d in range(-REACH, REACH + 1)]


def in_thirds(value, width):
    high = lax.reduce_precision(value, 8, 7)
    middle = lax.reduce_precision(value - high, 8, 7)
    pieces = jnp.concatenate([high, middle, value - high - middle], axis=1)
    return jnp.pad(pieces, ((0, 0), (0, width - pieces.shape[1]))).astype(jnp.bfloat16)


TILE, STEP = 256, 256


def per_device(mesh_shape, tokens, *given):
    names = NAMES
    part = dict(zip(names, given[:15]))
    item_lengths, out_grad = given[15:]
    matrices = ["query_proj", "key_proj", "value_proj", "output_proj", "hidden_proj", "return_proj"]
    vectors = [n for n in names if n not in matrices]
    outer = [n for n in vectors if n != "hidden_bias"]
    ndev = mesh_shape["items"] * mesh_shape["rows"]
    rows_dev, width = tokens.shape
    aligned = all(part[n].shape[0] % 8 == 0 for n in matrices) and all(part[n].shape[0] <= 128 for n in vectors)
    sizes = [part[n].shape[0] for n in vectors]
    used = sum(sizes)
    padded = -(-used // 1024) * 1024
    W = {}
    if aligned:
        got = gather_all(
            mesh_shape, item_lengths, tokens, [part[n] for n in matrices], [part[n] for n in outer + ["hidden_bias"]], TILE
        )
        wholes = [g.reshape((-1,) + g.shape[2:]) for g in got[: len(matrices)]]
        for k, n in enumerate(outer):
            W[n] = got[-6][k : k + 1]
        W["hidden_bias"] = got[-5]
        projected, attended, attended_full, logsum = got[-4:]
    else:
        wholes = [lax.all_gather(part[n], AXES, axis=0, tiled=True) for n in matrices]
        flat = lax.all_gather(jnp.concatenate([part[n] for n in vectors]), AXES, axis=0, tiled=False)
        at = 0
        for n, size in zip(vectors, sizes):
            W[n] = flat[:, at : at + size].reshape(1, -1).astype(jnp.float32)
            at += size
        window = jnp.concatenate(halo(tokens))
        query_wide = (dot_plain(window, wholes[0]) + W["query_bias"]).astype(jnp.bfloat16)
        keys_wide = dot_plain(window, wholes[1]).astype(jnp.bfloat16)
        values_wide = (dot_plain(window, wholes[2]) + W["value_bias"]).astype(jnp.bfloat16)
        projected = jnp.stack([query_wide, keys_wide, values_wide])
        attended, attended_full, logsum = attend(item_lengths, projected, TILE, STEP)
    W.update(zip(matrices, wholes))

    mixed = tokens.astype(jnp.float32) + (dot_plain(attended, W["output_proj"]) + W["output_bias"])
    normed, attn_back = jax.vjp(layer_norm, mixed, W["attn_gain"], W["attn_shift"])
    normed_low = normed.astype(jnp.bfloat16)
    hidden_pre = dot_plain(normed_low, W["hidden_proj"]) + W["hidden_bias"]
    cdf = 0.5 * (1.0 + lax.erf(hidden_pre * (0.5**0.5)))
    active = (hidden_pre * cdf).astype(jnp.bfloat16)
    slope = cdf + hidden_pre * jnp.exp(-0.5 * hidden_pre * hidden_pre) * 0.3989422804014327
    second = normed + (dot_plain(active, W["return_proj"]) + W["return_bias"])
    result, final_back = jax.vjp(layer_norm, second, W["final_gain"], W["final_shift"])

    grads = {}
    d_second, grads["final_gain"], grads["final_shift"] = final_back(out_grad.astype(jnp.float32))
    d_ffn = d_second.astype(jnp.bfloat16)
    grads["return_bias"] = jnp.sum(d_ffn.astype(jnp.float32), axis=0)
    d_hidden = (dot_last(d_ffn, W["return_proj"]) * slope).astype(jnp.bfloat16)
    grads["hidden_bias"] = jnp.sum(d_hidden.astype(jnp.float32), axis=0)
    d_normed = dot_last(d_hidden, W["hidden_proj"]) + d_second
    d_mixed, grads["attn_gain"], grads["attn_shift"] = attn_back(d_normed)
    d_branch = d_mixed.astype(jnp.bfloat16)
    grads["output_bias"] = jnp.sum(d_branch.astype(jnp.float32), axis=0)
    d_attended = dot_last(d_branch, W["output_proj"]).astype(jnp.bfloat16)

    lanes = jnp.arange(width, dtype=jnp.int32)[None, :] // HEAD == jnp.arange(16, dtype=jnp.int32)[:, None]
    product = d_attended.astype(jnp.float32) * attended_full
    lanes = lanes.astype(jnp.float32)
    highest = lax.Precision.HIGHEST
    centre = lax.dot_general(lanes, product, (((1,), (1,)), ((), ())), precision=highest)[:H, None]
    stats = jnp.concatenate([logsum[:, 0], centre[:, 0]]).T
    grad_blocks = halo(jnp.concatenate([d_attended, in_thirds(stats, PAIR)], axis=1))
    d_query = query_grad(item_lengths, projected, d_attended, logsum, centre, TILE, STEP)
    d_keys, d_values = key_grad(item_lengths, projected, grad_blocks, TILE, STEP)
    grads["query_bias"] = jnp.sum(d_query.astype(jnp.float32), axis=0)
    grads["value_bias"] = jnp.sum(d_values.astype(jnp.float32), axis=0)

    rows_of = jnp.concatenate([grads[n].reshape(ndev, size) for n, size in zip(vectors, sizes)], axis=1)
    rows_of = jnp.pad(rows_of, ((0, 0), (0, padded - used))).reshape(ndev, 8, padded // 8)
    factors = (
        active, d_ffn, normed_low, d_hidden, attended, d_branch, tokens, d_query, d_keys, d_values
    )
    order = ("hidden_proj", "return_proj", "output_proj", "query_proj", "key_proj", "value_proj")
    if aligned:
        projections = [W[n].reshape(ndev, -1, width) for n in matrices[:3]]
        chunks, tile, tokens_grad = scatter_all(mesh_shape, factors, d_mixed, projections, rows_of)
        blocks = d_hidden.shape[1] // width
        sums = [
            jnp.concatenate([chunks[k] for k in range(blocks)], axis=1),
            chunks[blocks : 2 * blocks].reshape(-1, width),
        ] + [chunks[2 * blocks + k] for k in range(4)] + [tile]
    else:
        tokens_grad = (
            d_mixed
            + dot_last(d_query, W["query_proj"])
            + dot_last(d_keys, W["key_proj"])
            + dot_last(d_values, W["value_proj"])
        )
        pairs = ((2, 3), (0, 1), (4, 5), (6, 7), (6, 8), (6, 9))
        low = [dot_rows(factors[i], factors[j]).astype(jnp.bfloat16) for i, j in pairs]
        low = [g.reshape((ndev, -1) + g.shape[1:]) for g in low] + [rows_of]
        sums = [lax.psum_scatter(g, AXES, scatter_dimension=0, tiled=True)[0] for g in low]
    total = {n: s.astype(jnp.float32) for n, s in zip(order, sums)}
    line = sums[-1].reshape(padded)
    at = 0
    for n, size in zip(vectors, sizes):
        total[n] = line[at : at + size]
        at += size
    return (result.astype(jnp.bfloat16), tokens_grad) + tuple(total[n] for n in names)


def solution(mesh):
    both = P(AXES)
    return jax.shard_map(
        functools.partial(per_device, dict(mesh.shape)),
        mesh=mesh,
        in_specs=(both,) * 16 + (P("items"), both),
        out_specs=(both,) * 17,
        check_vma=False,
    )
```
